32 devices in a mesh: dp: 4 (over y, x), row: 4 (over z), col: 2 (over core).
Axes of the slice: x: 2, y: 2, z: 4, core: 2. Of those that a mesh axis runs over, the one named last changes fastest.
Arguments:
- images: bfloat16 [32, 577, 1024], P(('dp', 'row'), None, 'col'), may hold values from -6 to 6
- cotangent: bfloat16 [32, 577, 1024], P(('dp', 'row'), None, 'col'), may hold values from -6 to 6
- micro_batch: int32 [32], P(('dp', 'row')), may hold values from 0 to 1, as said below
- heads_weight: bfloat16 [1024, 3, 1024], P('row', None, 'col'), may hold values from -0.1875 to 0.1875
- heads_bias: bfloat16 [2, 1024], P(None, 'col'), may hold values from -3 to 3
- merge_weight: bfloat16 [1024, 1024], P('col', 'row'), may hold values from -2 to 2
- merge_bias: bfloat16 [1024], P('col'), may hold values from -3 to 3
- expand_weight: bfloat16 [1024, 4096], P('row', 'col'), may hold values from -0.1875 to 0.1875
- expand_bias: bfloat16 [4096], P('col'), may hold values from -3 to 3
- shrink_weight: bfloat16 [4096, 1024], P('col', 'row'), may hold values from -0.09375 to 0.09375
- shrink_bias: bfloat16 [1024], P('col'), may hold values from -3 to 3
- norm_gains: bfloat16 [2, 1024], P(None, 'col'), may hold values from 0.5 to 1.5
- norm_shifts: bfloat16 [2, 1024], P(None, 'col'), may hold values from -2 to 2
Outputs:
- block_out: bfloat16 [32, 577, 1024], P(('dp', 'row'), None, 'col')
- input_grad: float32 [32, 577, 1024], P(('dp', 'row'), None, 'col')
- heads_weight_grad: float32 [1024, 3, 1024], P('row', None, 'col')
- heads_bias_grad: float32 [2, 1024], P(None, 'col')
- merge_weight_grad: float32 [1024, 1024], P('col', 'row')
- merge_bias_grad: float32 [1024], P('col')
- expand_weight_grad: float32 [1024, 4096], P('row', 'col')
- expand_bias_grad: float32 [4096], P('col')
- shrink_weight_grad: float32 [4096, 1024], P('col', 'row')
- shrink_bias_grad: float32 [1024], P('col')
- norm_gains_grad: float32 [2, 1024], P(None, 'col')
- norm_shifts_grad: float32 [2, 1024], P(None, 'col')
The draws below stay inside these ranges and needn't reach their ends.
Inputs may be any that keep to these rules, and one draw needn't show every extreme that they name: `micro_batch`: every micro-batch number 0 to 1 belongs to at least one image.
All inputs are finite; a program needn't handle non-finite values.
Results may differ from the reference program's by a relative error of at most 0.018.
Values may be sent and summed in bfloat16 or wider, within the bound.
No kernel may reach another device: no remote copies, remote signals or barrier semaphores. Data moves between devices by JAX's collectives and lax.ppermute only.
A program may use at most 192 MiB of HBM per device.

```python
import jax
import jax.numpy as jnp
from jax import lax

D = 1024
HEADS = 16
HEAD_DIM = 64
FF = 4096
SEQ = 577
MICRO = 2
SLOTS = 32
N_COL = 2


def draw_micro_batch(key, part):
    picks = jax.random.randint(key, (SLOTS,), 0, MICRO + 1)
    picks = jnp.minimum(picks, MICRO - 1)
    picks = picks.at[:MICRO].set(jnp.arange(MICRO, dtype=jnp.int32))
    return picks.astype(jnp.int32)


def block_scale(rng, shape, cuts, least, high):
    def one(axis_at, shards_of):
        draws = jax.random.uniform(jax.random.fold_in(jax.random.fold_in(rng, 6), axis_at), (shards_of,), jnp.float32, least / len(cuts), high / len(cuts))
        return jnp.repeat(jnp.exp(draws), shape[axis_at] // shards_of).reshape((-1,) + (1,) * (len(shape) - axis_at - 1))

    level = one(*cuts[0])
    for cut in cuts[1:]:
        level = level * one(*cut)
    return level


def centred(stream_key, dims, scale, bound, pieces=(), kind=jnp.bfloat16):
    result = scale * jax.random.normal(stream_key, dims, jnp.float32)
    if pieces:
        result = result * block_scale(stream_key, dims, pieces, -0.22, 0.18)
    return jnp.clip(result, -bound, bound).astype(kind)


def setup_inputs(seed: int = 0) -> dict:
    key_of = jax.random.split(jax.random.key(seed), 14)
    images = centred(key_of[0], (SLOTS, SEQ, D), 1.0, 6.0, ((0, 16), (2, 2)))
    cotangent = centred(key_of[1], (SLOTS, SEQ, D), 1.0, 6.0, ((0, 16), (2, 2)))
    micro_batch = draw_micro_batch(jax.random.fold_in(key_of[13], 71), 0)
    heads_weight = centred(key_of[3], (D, 3, D), D ** -0.5, 0.1875, ((0, 4), (2, 2)))
    heads_bias = centred(key_of[4], (2, D), 0.5, 3.0, ((1, 2),))
    merge_weight = centred(key_of[5], (D, D), (max(D // 128, 1)) ** -0.5, 2.0, ((0, 2), (1, 4)))
    merge_bias = centred(key_of[6], (D,), 0.5, 3.0, ((0, 2),))
    expand_weight = centred(key_of[7], (D, FF), D ** -0.5, 0.1875, ((0, 4), (1, 2)))
    expand_bias = centred(key_of[8], (FF,), 0.5, 3.0, ((0, 2),))
    shrink_weight = centred(key_of[9], (FF, D), FF ** -0.5, 0.09375, ((0, 2), (1, 4)))
    shrink_bias = centred(key_of[10], (D,), 0.5, 3.0, ((0, 2),))
    norm_gains = jnp.clip(1.0 + 0.1 * jax.random.normal(key_of[11], (2, D), jnp.float32), 0.5, 1.5).astype(jnp.bfloat16)
    norm_shifts = centred(key_of[12], (2, D), 0.3, 2.0, ((1, 2),))
    return {"images": images, "cotangent": cotangent, "micro_batch": micro_batch, "heads_weight": heads_weight, "heads_bias": heads_bias, "merge_weight": merge_weight, "merge_bias": merge_bias, "expand_weight": expand_weight, "expand_bias": expand_bias, "shrink_weight": shrink_weight, "shrink_bias": shrink_bias, "norm_gains": norm_gains, "norm_shifts": norm_shifts}


@jax.custom_vjp
def low(v):
    return lax.optimization_barrier(v.astype(jnp.bfloat16)).astype(jnp.float32)

@jax.custom_vjp
def low_back(v):
    return v

def low_keep(v):
    return (low(v), None)

def low_pass(kept, grad):
    return (grad,)

def back_keep(v):
    return (v, None)

def back_low(kept, grad):
    return (low(grad),)
low.defvjp(low_keep, low_pass)
low_back.defvjp(back_keep, back_low)
precise = lax.Precision.HIGHEST

def layer_norm(values, gain, shift):
    average = lax.optimization_barrier(jnp.mean(values, axis=-1, keepdims=True))
    variance = lax.optimization_barrier(jnp.mean((values - average) ** 2, axis=-1, keepdims=True))
    return (values - average) * lax.rsqrt(variance + 1e-05) * gain + shift

def copies_of(values):
    return low_back(jnp.broadcast_to(values[None], (N_COL,) + values.shape))

def image_block(one_image, params):
    heads_weight, heads_bias, merge_weight, merge_bias, expand_weight, expand_bias, shrink_weight, shrink_bias, norm_gains, norm_shifts = params
    length = one_image.shape[0]
    block_width = D // N_COL
    block_units = FF // N_COL
    normed = low(layer_norm(one_image, norm_gains[0], norm_shifts[0]))
    heads_blocks = heads_weight.reshape(D, 3, N_COL, block_width)
    mixed_heads = jnp.einsum('ctd,dkcf->tkcf', copies_of(normed), heads_blocks, precision=precise).reshape(length, 3, D)
    query_low = low(low_back((mixed_heads[:, 0] + heads_bias[0]) * HEAD_DIM ** (-0.5))).reshape(length, HEADS, HEAD_DIM)
    key_low = low(low_back(mixed_heads[:, 1])).reshape(length, HEADS, HEAD_DIM)
    value_low = low(low_back(mixed_heads[:, 2] + heads_bias[1])).reshape(length, HEADS, HEAD_DIM)
    scores = low_back(jnp.einsum('qhe,khe->hqk', query_low, key_low, precision=precise))
    probabilities = low(jax.nn.softmax(scores, axis=-1))
    attended = jnp.einsum('hqk,khe->qhe', probabilities, value_low, precision=precise).reshape(length, D)
    attended = low(low_back(attended))
    merge_parts = low(jnp.einsum('tcf,cfd->tcd', attended.reshape(length, N_COL, block_width), merge_weight.reshape(N_COL, block_width, D), precision=precise))
    branch = low_back(lax.optimization_barrier(jnp.sum(merge_parts, axis=1)) + merge_bias)
    middle = one_image + branch
    normed_two = low(layer_norm(middle, norm_gains[1], norm_shifts[1]))
    expand_blocks = expand_weight.reshape(D, N_COL, block_units)
    hidden = jnp.einsum('ctd,dcf->tcf', copies_of(normed_two), expand_blocks, precision=precise).reshape(length, FF)
    hidden = low_back(hidden + expand_bias)
    activated = low(hidden * jax.nn.sigmoid(1.702 * hidden))
    shrink_parts = low(jnp.einsum('tcf,cfd->tcd', activated.reshape(length, N_COL, block_units), shrink_weight.reshape(N_COL, block_units, D), precision=precise))
    branch_two = low_back(lax.optimization_barrier(jnp.sum(shrink_parts, axis=1)) + shrink_bias)
    return middle + branch_two

def forward(inputs, params):
    checked = jax.checkpoint(image_block)

    def apply_one(one_image):
        return checked(one_image, params)
    return lax.map(apply_one, inputs)

def reference(images, cotangent, micro_batch, heads_weight, heads_bias, merge_weight, merge_bias, expand_weight, expand_bias, shrink_weight, shrink_bias, norm_gains, norm_shifts):
    params = tuple((item.astype(jnp.float32) for item in (heads_weight, heads_bias, merge_weight, merge_bias, expand_weight, expand_bias, shrink_weight, shrink_bias, norm_gains, norm_shifts)))
    inputs = images.astype(jnp.float32)
    member = (micro_batch[:, None] == jnp.arange(MICRO, dtype=jnp.int32)[None, :]).astype(jnp.float32)
    totals = lax.optimization_barrier(jnp.sum(member, axis=0))
    batch_weight = SLOTS / (MICRO * totals)
    slot_weight = lax.optimization_barrier(jnp.sum(member * batch_weight[None, :], axis=1))
    output, pullback = jax.vjp(forward, inputs, params)
    cot_scaled = cotangent.astype(jnp.float32) * slot_weight[:, None, None]
    input_grad, grads = pullback(cot_scaled)
    return (output.astype(jnp.bfloat16), input_grad, grads[0], grads[1], grads[2], grads[3], grads[4], grads[5], grads[6], grads[7], grads[8], grads[9])
```

```python
import functools

import jax
import jax.numpy as jnp
from jax import lax
from jax.experimental import pallas as pl
from jax.experimental.pallas import tpu as pltpu
from jax.sharding import PartitionSpec as P

HEAD_DIM = 64
MICRO = 2
BF16 = jnp.bfloat16
F32 = jnp.float32
VMEM_LIMIT = 56 << 20


def peer(value, axis, p):
    n = lax.axis_size(axis)
    return lax.ppermute(value, axis, [(i, i ^ p) for i in range(n)])


def xor_order(value, dim, axis):
    n = lax.axis_size(axis)
    index = lax.axis_index(axis)
    size = value.shape[dim]
    bit = 1
    while bit < n:
        run = size * bit // n
        pieces = [lax.slice_in_dim(value, at, at + run, axis=dim) for at in range(0, size, run)]
        swapped = lax.concatenate([pieces[k ^ 1] for k in range(len(pieces))], dim)
        value = jnp.where((index & bit) != 0, swapped, value)
        bit *= 2
    return value


def cut(value, dim, n, k):
    run = value.shape[dim] // n
    return lax.slice_in_dim(value, k * run, (k + 1) * run, axis=dim)


def col_full(own, feature_dim):
    n_col = lax.axis_size("col")
    if n_col != 2:
        return xor_order(lax.all_gather(own, "col", axis=feature_dim, tiled=True), feature_dim, "row")
    other = peer(own, "col", 1)
    first = lax.axis_index("col") == 0
    full = lax.concatenate(
        [jnp.where(first, own, other), jnp.where(first, other, own)], feature_dim
    )
    return xor_order(full, feature_dim, "row")


def col_own(full, feature_dim):
    n_col = lax.axis_size("col")
    width = full.shape[feature_dim] // n_col
    plain = xor_order(full, feature_dim, "row")
    if n_col == 2:
        low = lax.slice_in_dim(plain, 0, width, axis=feature_dim)
        high = lax.slice_in_dim(plain, width, 2 * width, axis=feature_dim)
        return jnp.where(lax.axis_index("col") == 0, low, high)
    return lax.dynamic_slice_in_dim(plain, lax.axis_index("col") * width, width, feature_dim)


def col_sum(part):
    low = part.astype(BF16)
    if lax.axis_size("col") == 2:
        return low.astype(F32) + peer(low, "col", 1).astype(F32)
    return lax.psum(low, "col").astype(F32)


def col_sum_own(part):
    low = part.astype(BF16)
    if lax.axis_size("col") == 2:
        plain = xor_order(low, low.ndim - 1, "row")
        width = plain.shape[-1] // 2
        first = lax.axis_index("col") == 0
        head, tail = plain[..., :width], plain[..., width:]
        kept = jnp.where(first, head, tail)
        other = peer(jnp.where(first, tail, head), "col", 1)
        return kept.astype(F32) + other.astype(F32)
    return col_own(lax.psum(low, "col").astype(F32), low.ndim - 1)


def gather_weight(own, inner_dim, model_dim):
    n_dp, n_row = lax.axis_size("dp"), lax.axis_size("row")
    own = xor_order(own, inner_dim, "dp")
    quarter = cut(own, inner_dim, n_dp, 0)
    over_row = lax.concatenate([peer(quarter, "row", j) for j in range(1, n_row)], model_dim)
    rest = [over_row] + [peer(over_row, "dp", p) for p in range(1, n_dp)]
    return lax.concatenate([own, lax.concatenate(rest, inner_dim)], model_dim)


def reduce_weight(grad, inner_dim, model_dim):
    n_dp, n_row = lax.axis_size("dp"), lax.axis_size("row")
    total = cut(grad, inner_dim, n_dp, 0).astype(F32)
    for p in range(1, n_dp):
        total = total + peer(cut(grad, inner_dim, n_dp, p), "dp", p).astype(F32)
    part = total.astype(BF16)
    total = cut(part, model_dim, n_row, 0).astype(F32)
    for j in range(1, n_row):
        total = total + peer(cut(part, model_dim, n_row, j), "row", j).astype(F32)
    part = total.astype(BF16)
    whole = lax.concatenate([part] + [peer(part, "dp", p) for p in range(1, n_dp)], inner_dim)
    return xor_order(whole, inner_dim, "dp").astype(F32)


def sum_all(value):
    for axis in ("dp", "row"):
        bit = 1
        while bit < lax.axis_size(axis):
            value = value + peer(value, axis, bit)
            bit *= 2
    return value


def head_mask(rows, width, h, count):
    lane = lax.broadcasted_iota(jnp.int32, (rows, width), 1)
    return (lane >= h * HEAD_DIM) & (lane < (h + 1) * HEAD_DIM)


def nt(a, b):
    return lax.dot_general(a, b, (((1,), (1,)), ((), ())), preferred_element_type=F32)


def nn(a, b):
    return lax.dot_general(a, b, (((1,), (0,)), ((), ())), preferred_element_type=F32)


def attend_kernel(length, q_ref, k_ref, v_ref, o_ref):
    rows, width = q_ref.shape
    count = width // HEAD_DIM
    k = k_ref[...]
    v = v_ref[...]
    chunk = 256
    for start in range(0, rows, chunk):
        size = min(chunk, rows - start)
        q = q_ref[pl.ds(start, size), :]
        result = None
        for h in range(count):
            mask = head_mask(size, width, h, count)
            scores = nt(jnp.where(mask, q, jnp.zeros_like(q)), k)
            key = lax.broadcasted_iota(jnp.int32, scores.shape, 1)
            scores = jnp.where(key < length, scores, -1e30)
            top = jnp.max(scores, axis=1, keepdims=True)
            grown = jnp.exp(scores - top)
            total = jnp.sum(grown, axis=1, keepdims=True)
            out = nn(grown.astype(BF16), v) / total
            result = out if result is None else jnp.where(mask, out, result)
        o_ref[pl.ds(start, size), :] = result.astype(BF16)


def attend(q, k, v, length):
    count, rows, width = q.shape
    block = min(width, 2 * HEAD_DIM)
    spec = pl.BlockSpec((None, rows, block), lambda i, b: (i, 0, b))
    flops = 4 * count * rows * rows * width
    return pl.pallas_call(
        functools.partial(attend_kernel, length),
        grid=(count, width // block),
        in_specs=[spec] * 3,
        out_specs=spec,
        out_shape=jax.ShapeDtypeStruct(q.shape, BF16),
        compiler_params=pltpu.CompilerParams(vmem_limit_bytes=VMEM_LIMIT),
        cost_estimate=pl.CostEstimate(
            flops=flops, bytes_accessed=8 * q.size, transcendentals=count * rows * rows * width // 64
        ),
        name="attend",
    )(q, k, v)


def attend_back_kernel(length, q_ref, k_ref, v_ref, up_ref, dq_ref, dk_ref, dv_ref, probs, grads, q_all, up_all):
    rows, width = q_ref.shape
    count = width // HEAD_DIM
    lanes = probs.shape[1] // count
    k = k_ref[...]
    v = v_ref[...]
    chunk = 256
    for h in range(count):
        base = h * lanes
        if rows < lanes:
            probs[:, pl.ds(base + rows, lanes - rows)] = jnp.zeros((rows, lanes - rows), BF16)
            grads[:, pl.ds(base + rows, lanes - rows)] = jnp.zeros((rows, lanes - rows), BF16)
            q_all[pl.ds(base + rows, lanes - rows), :] = jnp.zeros((lanes - rows, width), BF16)
            up_all[pl.ds(base + rows, lanes - rows), :] = jnp.zeros((lanes - rows, width), BF16)
        for start in range(0, rows, chunk):
            size = min(chunk, rows - start)
            mask = head_mask(size, width, h, count)
            q = q_ref[pl.ds(start, size), :]
            up = up_ref[pl.ds(start, size), :]
            q = jnp.where(mask, q, jnp.zeros_like(q))
            up = jnp.where(mask, up, jnp.zeros_like(up))
            q_all[pl.ds(base + start, size), :] = q
            up_all[pl.ds(base + start, size), :] = up
            scores = nt(k, q)
            key = lax.broadcasted_iota(jnp.int32, scores.shape, 0)
            scores = jnp.where(key < length, scores, -1e30)
            top = jnp.max(scores, axis=0, keepdims=True)
            grown = jnp.exp(scores - top)
            share = grown * (1.0 / jnp.sum(grown, axis=0, keepdims=True))
            prob_grad = nt(v, up)
            delta = jnp.sum(share * prob_grad, axis=0, keepdims=True)
            probs[:, pl.ds(base + start, size)] = share.astype(BF16)
            grads[:, pl.ds(base + start, size)] = (share * (prob_grad - delta)).astype(BF16)
    dv_ref[...] = nn(probs[...], up_all[...]).astype(BF16)
    dk_ref[...] = nn(grads[...], q_all[...]).astype(BF16)
    turned = k.astype(F32).T.astype(BF16)
    pieces = []
    for h in range(count):
        pieces.append(nn(turned[h * HEAD_DIM : (h + 1) * HEAD_DIM, :], grads[:, pl.ds(h * lanes, rows)]))
    dq = jnp.concatenate(pieces, axis=0).T if count > 1 else pieces[0].T
    dq_ref[...] = (dq.astype(BF16).astype(F32) * HEAD_DIM**-0.5).astype(BF16)


def attend_back(q, k, v, up, length):
    count, rows, width = q.shape
    block = min(width, 2 * HEAD_DIM)
    lanes = -(-rows // 128) * 128
    heads = block // HEAD_DIM
    spec = pl.BlockSpec((None, rows, block), lambda i, b: (i, 0, b))
    shape = jax.ShapeDtypeStruct(q.shape, BF16)
    return pl.pallas_call(
        functools.partial(attend_back_kernel, length),
        grid=(count, width // block),
        in_specs=[spec] * 4,
        out_specs=[spec] * 3,
        out_shape=[shape] * 3,
        scratch_shapes=[
            pltpu.VMEM((rows, heads * lanes), BF16),
            pltpu.VMEM((rows, heads * lanes), BF16),
            pltpu.VMEM((heads * lanes, block), BF16),
            pltpu.VMEM((heads * lanes, block), BF16),
        ],
        compiler_params=pltpu.CompilerParams(vmem_limit_bytes=VMEM_LIMIT),
        cost_estimate=pl.CostEstimate(
            flops=10 * count * rows * rows * width,
            bytes_accessed=14 * q.size,
            transcendentals=count * rows * rows * width // 64,
        ),
        name="attend_back",
    )(q, k, v, up)


def norm_forward(values, gain, shift):
    mean = jnp.mean(values, axis=-1, keepdims=True)
    centered = values - mean
    inverse = lax.rsqrt(jnp.mean(centered * centered, axis=-1, keepdims=True) + 1e-05)
    xhat = centered * inverse
    return (xhat * gain + shift).astype(BF16), mean, inverse


def norm_back(upstream, values, mean, inverse, gain):
    xhat = (values - mean) * inverse
    scaled = upstream * gain
    first = jnp.mean(scaled, axis=-1, keepdims=True)
    second = jnp.mean(scaled * xhat, axis=-1, keepdims=True)
    grad = inverse * (scaled - first - xhat * second)
    return grad, jnp.sum(upstream * xhat, axis=(0, 1)), jnp.sum(upstream, axis=(0, 1))


def shards(
    images,
    cotangent,
    micro_batch,
    heads_weight,
    heads_bias,
    merge_weight,
    merge_bias,
    expand_weight,
    expand_bias,
    shrink_weight,
    shrink_bias,
    norm_gains,
    norm_shifts,
):
    count, length, width = images.shape
    rows = -(-length // 16) * 16
    pad = ((0, 0), (0, rows - length), (0, 0))

    heads_full = gather_weight(jnp.transpose(heads_weight, (1, 0, 2)), 2, 1)
    x_own = jnp.pad(images, pad)
    x_low = col_full(x_own, 2)
    params = jnp.concatenate(
        [norm_gains, norm_shifts, merge_bias[None], shrink_bias[None]], axis=0
    )
    params = col_full(params, 1).astype(F32)
    gain_one, gain_two, shift_one, shift_two, merge_bias_full, shrink_bias_full = (
        params[k] for k in range(6)
    )
    merge_full = gather_weight(merge_weight, 0, 1)
    cot_low = col_full(jnp.pad(cotangent, pad), 2)
    expand_full = gather_weight(expand_weight, 1, 0)
    shrink_full = gather_weight(shrink_weight, 0, 1)
    heads_bias_own = xor_order(heads_bias, 1, "dp").astype(F32)
    expand_bias_own = xor_order(expand_bias, 0, "dp").astype(F32)

    member = (micro_batch[:, None] == jnp.arange(MICRO, dtype=jnp.int32)[None, :]).astype(jnp.int32)
    totals = lax.psum(jnp.sum(member, axis=0), ("dp", "row"))
    all_slots = count * lax.axis_size("dp") * lax.axis_size("row")
    batch_weight = all_slots / (MICRO * totals.astype(F32))
    slot_weight = jnp.sum(member.astype(F32) * batch_weight[None, :], axis=1)

    x = x_low.astype(F32)
    normed, mean_one, inverse_one = norm_forward(x, gain_one, shift_one)
    mixed = jnp.einsum("itd,kdf->kitf", normed, heads_full, preferred_element_type=F32)
    query = ((mixed[0] + heads_bias_own[0]) * HEAD_DIM**-0.5).astype(BF16)
    key = mixed[1].astype(BF16)
    value = (mixed[2] + heads_bias_own[1]).astype(BF16)
    attended = attend(query, key, value, length)
    merge_part = jnp.einsum("itf,fd->itd", attended, merge_full, preferred_element_type=F32)
    middle = x + (col_sum(merge_part) + merge_bias_full)
    normed_two, mean_two, inverse_two = norm_forward(middle, gain_two, shift_two)
    hidden = (
        jnp.einsum("itd,dh->ith", normed_two, expand_full, preferred_element_type=F32)
        + expand_bias_own
    )
    gate = jax.nn.sigmoid(1.702 * hidden)
    activated = (hidden * gate).astype(BF16)
    slope = (gate + 1.702 * hidden * gate * (1.0 - gate)).astype(BF16)
    seed = cot_low.astype(F32) * slot_weight[:, None, None]
    seed_low = seed.astype(BF16)

    shrink_grad = jnp.einsum("ith,itd->hd", activated, seed_low, preferred_element_type=F32)
    shrink_sum = reduce_weight(shrink_grad.astype(BF16), 0, 1)
    act_grad = jnp.einsum("itd,hd->ith", seed_low, shrink_full, preferred_element_type=F32)
    hidden_grad = (act_grad * slope.astype(F32)).astype(BF16)
    norm_part = jnp.einsum("ith,dh->itd", hidden_grad, expand_full, preferred_element_type=F32)
    normed_two_grad = col_sum(norm_part)
    expand_grad = jnp.einsum("itd,ith->dh", normed_two, hidden_grad, preferred_element_type=F32)
    expand_sum = reduce_weight(expand_grad.astype(BF16), 1, 0)
    result, gain_sum_two, shift_sum_two = norm_back(
        normed_two_grad, middle, mean_two, inverse_two, gain_two
    )
    middle_grad = seed + result
    branch_grad = middle_grad.astype(BF16)

    shrink_part = jnp.einsum("ith,hd->itd", activated, shrink_full, preferred_element_type=F32)
    output = (
        col_own(middle, 2) + (col_sum_own(shrink_part) + shrink_bias.astype(F32))
    ).astype(BF16)[:, :length]

    attended_grad = jnp.einsum(
        "itd,fd->itf", branch_grad, merge_full, preferred_element_type=F32
    ).astype(BF16)
    merge_grad = jnp.einsum("itf,itd->fd", attended, branch_grad, preferred_element_type=F32)
    merge_sum = reduce_weight(merge_grad.astype(BF16), 0, 1)
    grads = attend_back(query, key, value, attended_grad, length)
    mixed_grad = jnp.stack(grads)
    heads_grad = jnp.einsum("itd,kitf->kdf", normed, mixed_grad, preferred_element_type=F32)
    heads_sum = reduce_weight(heads_grad.astype(BF16), 2, 1)
    first_part = jnp.einsum("kitf,kdf->itd", mixed_grad, heads_full, preferred_element_type=F32)
    normed_grad = col_sum(first_part)
    result, gain_sum_one, shift_sum_one = norm_back(normed_grad, x, mean_one, inverse_one, gain_one)
    input_grad = col_own(middle_grad + result, 2)[:, :length]

    model_sums = jnp.stack(
        [
            gain_sum_one,
            gain_sum_two,
            shift_sum_one,
            shift_sum_two,
            jnp.sum(branch_grad.astype(F32), axis=(0, 1)),
            jnp.sum(seed_low.astype(F32), axis=(0, 1)),
        ]
    )
    model_sums = col_own(model_sums, 1)
    heads_bias_grad = xor_order(
        jnp.stack(
            [jnp.sum(grads[0].astype(F32), axis=(0, 1)), jnp.sum(grads[2].astype(F32), axis=(0, 1))]
        ),
        1,
        "dp",
    )
    expand_bias_grad = xor_order(jnp.sum(hidden_grad.astype(F32), axis=(0, 1)), 0, "dp")
    packed = sum_all(
        jnp.concatenate([model_sums.ravel(), heads_bias_grad.ravel(), expand_bias_grad])
    )
    model_sums = packed[: 6 * width].reshape(6, width)
    heads_bias_grad = packed[6 * width : 8 * width].reshape(2, width)
    expand_bias_grad = packed[8 * width :]
    return (
        output,
        input_grad,
        jnp.transpose(heads_sum, (1, 0, 2)),
        heads_bias_grad,
        merge_sum,
        model_sums[4],
        expand_sum,
        expand_bias_grad,
        shrink_sum,
        model_sums[5],
        model_sums[0:2],
        model_sums[2:4],
    )


def solution(mesh):
    placed = (
        P(("dp", "row"), None, "col"),
        P(("dp", "row"), None, "col"),
        P(("dp", "row")),
        P("row", None, "col"),
        P(None, "col"),
        P("col", "row"),
        P("col"),
        P("row", "col"),
        P("col"),
        P("col", "row"),
        P("col"),
        P(None, "col"),
        P(None, "col"),
    )
    return jax.shard_map(
        shards,
        mesh=mesh,
        in_specs=placed,
        out_specs=(
            P(("dp", "row"), None, "col"),
            P(("dp", "row"), None, "col"),
            P("row", None, "col"),
            P(None, "col"),
            P("col", "row"),
            P("col"),
            P("row", "col"),
            P("col"),
            P("col", "row"),
            P("col"),
            P(None, "col"),
            P(None, "col"),
        ),
        check_vma=False,
    )
```

```python
import functools

import jax
import jax.numpy as jnp
from jax import lax
from jax.experimental import pallas as pl
from jax.experimental.pallas import tpu as pltpu
from jax.sharding import PartitionSpec as P

HEAD_DIM = 64
MICRO = 2
BF16 = jnp.bfloat16
F32 = jnp.float32
VMEM_LIMIT = 58 << 20
STEP = 48


def peer(value, axis, p):
    n = lax.axis_size(axis)
    return lax.ppermute(value, axis, [(i, i ^ p) for i in range(n)])


def xor_order(value, dim, axis):
    n = lax.axis_size(axis)
    index = lax.axis_index(axis)
    size = value.shape[dim]
    bit = 1
    while bit < n:
        run = size * bit // n
        pieces = [lax.slice_in_dim(value, at, at + run, axis=dim) for at in range(0, size, run)]
        swapped = lax.concatenate([pieces[k ^ 1] for k in range(len(pieces))], dim)
        value = jnp.where((index & bit) != 0, swapped, value)
        bit *= 2
    return value


def cut(value, dim, n, k):
    run = value.shape[dim] // n
    return lax.slice_in_dim(value, k * run, (k + 1) * run, axis=dim)


def own_part(own, inner_dim):
    run = own.shape[inner_dim] // lax.axis_size("dp")
    return lax.dynamic_slice_in_dim(own, lax.axis_index("dp") * run, run, inner_dim)


def dp_parts(part):
    return [part] + [peer(part, "dp", p) for p in range(1, lax.axis_size("dp"))]


def sum_parts(parts, axis, start=None):
    n = lax.axis_size(axis)
    if start is not None:
        stacked = jnp.stack(parts)
        parts = [lax.dynamic_index_in_dim(stacked, start ^ p, 0, keepdims=False) for p in range(n)]
    total = parts[0].astype(F32)
    for p in range(1, n):
        total = total + peer(parts[p], axis, p).astype(F32)
    return total.astype(BF16)


def dp_sum(blocks):
    n = lax.axis_size("dp")
    blocks = blocks.reshape((n, blocks.shape[0] // n) + blocks.shape[1:])
    return add(lax.all_to_all(blocks, "dp", 0, 0))


def dp_all(part):
    n = lax.axis_size("dp")
    return lax.all_to_all(jnp.broadcast_to(part[None], (n,) + part.shape), "dp", 0, 0)


def scatter_row(value, model_dim):
    return lax.psum_scatter(value, "row", scatter_dimension=model_dim, tiled=True)


def sum_all(value):
    for axis in ("dp", "row"):
        terms = dp_parts(value) if axis == "dp" else [value] + [peer(value, "row", j) for j in range(1, lax.axis_size("row"))]
        while len(terms) > 1:
            terms = [terms[k] + terms[k + 1] for k in range(0, len(terms), 2)]
        value = terms[0]
    return value


def col_join(own, other):
    first = lax.axis_index("col") == 0
    return lax.concatenate([jnp.where(first, own, other), jnp.where(first, other, own)], own.ndim - 1)


def col_full(own, feature_dim):
    return lax.all_gather(own, "col", axis=feature_dim, tiled=True)


def col_own(full, feature_dim):
    n_col = lax.axis_size("col")
    if n_col == 2:
        return jnp.where(
            lax.axis_index("col") == 0, cut(full, feature_dim, 2, 0), cut(full, feature_dim, 2, 1)
        )
    width = full.shape[feature_dim] // n_col
    return lax.dynamic_slice_in_dim(full, lax.axis_index("col") * width, width, feature_dim)


def col_shares(part):
    if lax.axis_size("col") == 2:
        return part, peer(part, "col", 1)
    return lax.psum(part, "col"), jnp.zeros_like(part)


def nt(a, b):
    return lax.dot_general(a, b, (((1,), (1,)), ((), ())), preferred_element_type=F32)


def nn(a, b):
    return lax.dot_general(a, b, (((1,), (0,)), ((), ())), preferred_element_type=F32)


def cost(us, moved=1 << 20):
    return pl.CostEstimate(flops=int(us * 1.0e9), bytes_accessed=moved, transcendentals=0)


def scalar_call(body, at, grid, in_specs, out_specs, out_shape, name, us, scratch=(), limit=24, aliases=None):
    far = lambda a: pltpu.HBM(a.shape, a.dtype)
    out_shape = [far(a) for a in out_shape] if isinstance(out_shape, list) else far(out_shape)
    return pl.pallas_call(
        body,
        grid_spec=pltpu.PrefetchScalarGridSpec(
            num_scalar_prefetch=1,
            grid=grid,
            in_specs=in_specs,
            out_specs=out_specs,
            scratch_shapes=list(scratch),
        ),
        out_shape=out_shape,
        input_output_aliases=aliases or {},
        compiler_params=pltpu.CompilerParams(vmem_limit_bytes=limit << 20),
        cost_estimate=cost(us),
        name=name,
    )


def row_chunks(rows, body):
    turns = rows // STEP

    def step(i, carry):
        body(pl.ds(pl.multiple_of(i * STEP, 16), STEP))
        return carry

    lax.fori_loop(0, turns, step, 0)
    if rows % STEP:
        body(pl.ds(turns * STEP, rows % STEP))


def join_kernel(normal, at_ref, own_ref, other_ref, *refs):
    out_ref = refs[2] if normal else refs[0]
    rows, width = own_ref.shape
    to = pl.ds(pl.multiple_of(at_ref[2] * width, width), width)
    away = pl.ds(pl.multiple_of((1 - at_ref[2]) * width, width), width)
    out_ref[:, to] = own_ref[...]
    out_ref[:, away] = other_ref[...]
    if not normal:
        return
    gain_ref, shift_ref, _, normed_ref = refs

    def body(at):
        value = out_ref[at, :].astype(F32)
        centered = value - jnp.mean(value, axis=1, keepdims=True)
        inverse = lax.rsqrt(jnp.mean(centered * centered, axis=1, keepdims=True) + 1e-05)
        normed_ref[at, :] = (centered * inverse * gain_ref[...] + shift_ref[...]).astype(BF16)

    row_chunks(rows, body)


def join(at, own, other, vectors=None):
    count, rows, width = own.shape
    normal = vectors is not None
    shape = jax.ShapeDtypeStruct((count, rows, 2 * width), BF16)
    half = pl.BlockSpec((None, rows, width), lambda i, at: (i, 0, 0))
    full = pl.BlockSpec((None, rows, 2 * width), lambda i, at: (i, 0, 0))
    vector = pl.BlockSpec((1, 2 * width), lambda i, at: (0, 0))
    return scalar_call(
        functools.partial(join_kernel, normal),
        at,
        (count,),
        [half, half] + [vector] * (2 if normal else 0),
        [full, full] if normal else full,
        [shape, shape] if normal else shape,
        "join",
        2,
    )(at, own, other, *(vectors or ()))


def seed_kernel(at_ref, own_ref, other_ref, weight_ref, cot_ref, seed_ref, sums_ref, sums):
    rows, width = own_ref.shape
    scale = weight_ref[pl.program_id(0)]
    sums[...] = jnp.zeros_like(sums)
    for k, ref in enumerate((own_ref, other_ref)):
        place = at_ref[2] if k == 0 else 1 - at_ref[2]
        to = pl.ds(pl.multiple_of(place * width, width), width)

        def body(at):
            value = ref[at, :]
            low = (value.astype(F32) * scale).astype(BF16)
            cot_ref[at, to] = value
            seed_ref[at, to] = low
            low = low.astype(F32)
            sums[:, to] += jnp.sum(low.reshape(low.shape[0] // 8, 8, width), axis=0)

        row_chunks(rows, body)
    sums_ref[...] = jnp.sum(sums[...], axis=0, keepdims=True)


def seed_of(at, own, other, weight):
    count, rows, width = own.shape
    shape = jax.ShapeDtypeStruct
    half = pl.BlockSpec((None, rows, width), lambda i, at: (i, 0, 0))
    full = pl.BlockSpec((None, rows, 2 * width), lambda i, at: (i, 0, 0))
    return scalar_call(
        seed_kernel,
        at,
        (count,),
        [half, half, pl.BlockSpec(memory_space=pltpu.SMEM)],
        [full, full, pl.BlockSpec((None, 1, 2 * width), lambda i, at: (i, 0, 0))],
        [shape((count, rows, 2 * width), BF16)] * 2 + [shape((count, 1, 2 * width), F32)],
        "seed",
        2,
        scratch=[pltpu.VMEM((8, 2 * width), F32)],
    )(at, own, other, weight)


def stack_kernel(body_rows, own_ref, *refs):
    out_ref = refs[-1]
    total = own_ref[...].astype(F32)
    for k, ref in enumerate(refs[:-1]):
        out_ref[k * body_rows : (k + 1) * body_rows, :] = ref[:body_rows, :]
        total = total + ref[body_rows:, :].astype(F32)
    out_ref[(len(refs) - 1) * body_rows :, :] = total.astype(BF16)


def stack(own_tail, arrays):
    vmem = pl.BlockSpec(memory_space=pltpu.VMEM)
    more, lanes = own_tail.shape
    body = arrays[0].shape[0] - more
    return pl.pallas_call(
        functools.partial(stack_kernel, body),
        in_specs=[vmem] * (1 + len(arrays)),
        out_specs=vmem,
        out_shape=jax.ShapeDtypeStruct((len(arrays) * body + more, lanes), BF16),
        compiler_params=pltpu.CompilerParams(vmem_limit_bytes=16 << 20),
        cost_estimate=cost(1),
        name="stack",
    )(own_tail, *arrays)


def unpack_kernel(n_row, at_ref, in_ref, merge_ref, expand_ref):
    z = pl.program_id(0)
    rows, run = merge_ref.shape
    near = expand_ref.shape[0]
    merge_ref[...] = in_ref[:rows, :]
    for k in range(expand_ref.shape[1] // run):
        expand_ref[:, k * run : (k + 1) * run] = in_ref[rows + k * near : rows + (k + 1) * near, :]


def unpack(at, gathered, rows, near):
    n_row, total, run = gathered.shape
    wide = (total - rows) // near * run
    shape = jax.ShapeDtypeStruct
    return scalar_call(
        functools.partial(unpack_kernel, n_row),
        at,
        (n_row,),
        [pl.BlockSpec((None, total, run), lambda j, at: (at[1] ^ j, 0, 0))],
        [
            pl.BlockSpec((rows, run), lambda j, at: (0, at[1] ^ j)),
            pl.BlockSpec((None, near, wide), lambda j, at: (j, 0, 0)),
        ],
        [shape((rows, n_row * run), BF16), shape((n_row, near, wide), BF16)],
        "unpack",
        1,
    )(at, gathered)


def pick_kernel(at_ref, in_ref, out_ref):
    out_ref[...] = in_ref[...]


def others(at, gathered):
    n_row = gathered.shape[0]
    block = (None,) + gathered.shape[1:]
    return scalar_call(
        pick_kernel,
        at,
        (n_row - 1,),
        [pl.BlockSpec(block, lambda j, at: (at[1] ^ (j + 1), 0, 0))],
        pl.BlockSpec(block, lambda j, at: (j, 0, 0)),
        jax.ShapeDtypeStruct((n_row - 1,) + gathered.shape[1:], gathered.dtype),
        "others",
        1,
    )(at, gathered)


def place_kernel(n_row, at_ref, own_ref, rest_ref, *refs):
    out_ref = refs[-1]
    near = own_ref.shape[1]
    for j in range(n_row):
        to = pl.ds(pl.multiple_of((at_ref[1] ^ j) * near, near), near)
        out_ref[:, to] = own_ref[...] if j == 0 else rest_ref[j - 1]


def place(p, at, own, rest, before):
    total, near = own.shape
    others, run, _ = rest.shape
    n_row = others + 1
    return scalar_call(
        functools.partial(place_kernel, n_row),
        at,
        (1,),
        [
            pl.BlockSpec((run, near), lambda i, at: (at[0] ^ p, 0)),
            pl.BlockSpec(rest.shape, lambda i, at: (0, 0, 0)),
        ]
        + [pl.BlockSpec(memory_space=pl.ANY)] * len(before),
        pl.BlockSpec((run, n_row * near), lambda i, at: (at[0] ^ p, 0)),
        jax.ShapeDtypeStruct((total, n_row * near), own.dtype),
        "place",
        1,
        aliases={3: 0} if before else {},
    )(at, own, rest, *before)


def add_kernel(in_ref, out_ref):
    out_ref[...] = jnp.sum(in_ref[...].astype(F32), axis=0).astype(BF16)


def add(blocks):
    n, rows, lanes = blocks.shape
    step = rows // 4 if rows % 64 == 0 else rows
    return pl.pallas_call(
        add_kernel,
        grid=(rows // step,),
        in_specs=[pl.BlockSpec((n, step, lanes), lambda i: (0, i, 0))],
        out_specs=pl.BlockSpec((step, lanes), lambda i: (i, 0)),
        out_shape=jax.ShapeDtypeStruct((rows, lanes), BF16),
        compiler_params=pltpu.CompilerParams(vmem_limit_bytes=24 << 20),
        cost_estimate=cost(1),
        name="add",
    )(blocks)


def half_kernel(at_ref, in_ref, out_ref):
    out_ref[...] = in_ref[...]


def half(at, value, own):
    count, rows, model = value.shape
    place = (lambda at: at[2]) if own else (lambda at: 1 - at[2])
    return scalar_call(
        half_kernel,
        at,
        (count,),
        [pl.BlockSpec((None, rows, model // 2), lambda i, at: (i, 0, place(at)))],
        pl.BlockSpec((None, rows, model // 2), lambda i, at: (i, 0, 0)),
        jax.ShapeDtypeStruct((count, rows, model // 2), value.dtype),
        "half",
        1,
    )(at, value)


def close_kernel(at_ref, m_ref, a_ref, b_ref, bias_ref, out_ref):
    def body(at):
        share = a_ref[at, :].astype(F32) + b_ref[at, :].astype(F32)
        out_ref[at, :] = (m_ref[at, :] + (share + bias_ref[...])).astype(BF16)

    row_chunks(a_ref.shape[0], body)


def close(at, middle, part, other, bias):
    count, rows, width = other.shape
    mine = pl.BlockSpec((None, rows, width), lambda i, at: (i, 0, at[2]))
    plain = pl.BlockSpec((None, rows, width), lambda i, at: (i, 0, 0))
    return scalar_call(
        close_kernel,
        at,
        (count,),
        [mine, mine, plain, pl.BlockSpec((1, width), lambda i, at: (0, 0))],
        plain,
        jax.ShapeDtypeStruct(other.shape, BF16),
        "close",
        1,
    )(at, middle, part, other, bias)


def spread_kernel(n_dp, at_ref, *refs):
    out_ref = refs[-1]
    run = out_ref.shape[2] // n_dp
    for p in range(n_dp):
        to = pl.ds(pl.multiple_of((at_ref[0] ^ p) * run, run), run)
        for k in range(3):
            out_ref[k, :, to] = refs[p][:, k * run : (k + 1) * run].astype(F32)


def spread(at, parts):
    n_dp = len(parts)
    rows, three = parts[0].shape
    run = three // 3
    vmem = pl.BlockSpec((rows, three), lambda i, at: (0, 0))
    return scalar_call(
        functools.partial(spread_kernel, n_dp),
        at,
        (1,),
        [vmem] * n_dp,
        pl.BlockSpec((3, rows, n_dp * run), lambda i, at: (0, 0, 0)),
        jax.ShapeDtypeStruct((3, rows, n_dp * run), F32),
        "spread",
        1,
    )(at, *parts)


def head_mask(rows, width, h):
    lane = lax.broadcasted_iota(jnp.int32, (rows, width), 1)
    return (lane >= h * HEAD_DIM) & (lane < (h + 1) * HEAD_DIM)


def mix_kernel(length, n_row, at_ref, n_ref, own_ref, rest_ref, bias_ref, *refs):
    mixed_ref, o_ref, weight_ref = refs[-3:]
    rows = n_ref.shape[0]
    width = o_ref.shape[1]
    count = width // HEAD_DIM
    near = own_ref.shape[1]
    chunk = 256

    @pl.when(pl.program_id(0) == 0)
    def _():
        for j in range(n_row):
            to = pl.ds(pl.multiple_of((at_ref[1] ^ j) * near, near), near)
            for k in range(3):
                start = ((j - 1) * 3 + k) * near
                piece = own_ref[k] if j == 0 else rest_ref[start : start + near, :]
                weight_ref[to, k * width : (k + 1) * width] = piece

    for start in range(0, rows, chunk):
        size = min(chunk, rows - start)
        at = pl.ds(start, size)
        mixed = nn(n_ref[at, :], weight_ref[...]) + bias_ref[...]
        mixed_ref[at, :width] = (mixed[:, :width] * HEAD_DIM**-0.5).astype(BF16)
        mixed_ref[at, width:] = mixed[:, width:].astype(BF16)
    k = mixed_ref[:, width : 2 * width]
    v = mixed_ref[:, 2 * width :]
    for start in range(0, rows, chunk):
        size = min(chunk, rows - start)
        at = pl.ds(start, size)
        q = mixed_ref[at, :width]
        result = None
        for h in range(count):
            mask = head_mask(size, width, h)
            scores = nt(jnp.where(mask, q, jnp.zeros_like(q)), k)
            key = lax.broadcasted_iota(jnp.int32, scores.shape, 1)
            scores = jnp.where(key < length, scores, -1e30)
            top = jnp.max(scores, axis=1, keepdims=True)
            grown = jnp.exp(scores - top)
            total = jnp.sum(grown, axis=1, keepdims=True)
            out = nn(grown.astype(BF16), v) / total
            result = out if result is None else jnp.where(mask, out, result)
        o_ref[at, :] = result.astype(BF16)


def mix_back_kernel(length, at_ref, m_ref, up_ref, *refs):
    d_ref, sums_ref, probs, grads, q_all, up_all = refs[-6:]
    rows, width = up_ref.shape
    count = width // HEAD_DIM
    lanes = probs.shape[1] // count
    k = m_ref[:, width : 2 * width]
    v = m_ref[:, 2 * width :]
    chunk = 256
    for h in range(count):
        base = h * lanes
        if rows < lanes:
            probs[:, pl.ds(base + rows, lanes - rows)] = jnp.zeros((rows, lanes - rows), BF16)
            grads[:, pl.ds(base + rows, lanes - rows)] = jnp.zeros((rows, lanes - rows), BF16)
            q_all[pl.ds(base + rows, lanes - rows), :] = jnp.zeros((lanes - rows, width), BF16)
            up_all[pl.ds(base + rows, lanes - rows), :] = jnp.zeros((lanes - rows, width), BF16)
        for start in range(0, rows, chunk):
            size = min(chunk, rows - start)
            mask = head_mask(size, width, h)
            q = m_ref[pl.ds(start, size), :width]
            up = up_ref[pl.ds(start, size), :]
            q = jnp.where(mask, q, jnp.zeros_like(q))
            up = jnp.where(mask, up, jnp.zeros_like(up))
            q_all[pl.ds(base + start, size), :] = q
            up_all[pl.ds(base + start, size), :] = up
            scores = nt(k, q)
            key = lax.broadcasted_iota(jnp.int32, scores.shape, 0)
            scores = jnp.where(key < length, scores, -1e30)
            top = jnp.max(scores, axis=0, keepdims=True)
            grown = jnp.exp(scores - top)
            share = grown * (1.0 / jnp.sum(grown, axis=0, keepdims=True))
            prob_grad = nt(v, up)
            delta = jnp.sum(share * prob_grad, axis=0, keepdims=True)
            probs[:, pl.ds(base + start, size)] = share.astype(BF16)
            grads[:, pl.ds(base + start, size)] = (share * (prob_grad - delta)).astype(BF16)
    dv = nn(probs[...], up_all[...]).astype(BF16)
    dk = nn(grads[...], q_all[...]).astype(BF16)
    turned = k.astype(F32).T.astype(BF16)
    pieces = []
    for h in range(count):
        pieces.append(nn(turned[h * HEAD_DIM : (h + 1) * HEAD_DIM, :], grads[:, pl.ds(h * lanes, rows)]))
    dq = jnp.concatenate(pieces, axis=0).T if count > 1 else pieces[0].T
    dq = (dq.astype(BF16).astype(F32) * HEAD_DIM**-0.5).astype(BF16)
    for at, value in enumerate((dq, dk, dv)):
        d_ref[:, at * width : (at + 1) * width] = value
        sums_ref[:, at * width : (at + 1) * width] = jnp.sum(value.astype(F32), axis=0, keepdims=True)


def mix(length, g, at, normed, own, rest, bias, attended, weight, width):
    count, rows, model = normed.shape
    n_row = model // own.shape[1]
    wide = rest.shape[1]
    shape = jax.ShapeDtypeStruct
    more = [] if attended is None else [attended, weight]
    place = (lambda at: at[0] ^ g) if own.shape[2] > wide else (lambda at: 0)
    return scalar_call(
        functools.partial(mix_kernel, length, n_row),
        at,
        (count,),
        [
            pl.BlockSpec((None, rows, model), lambda i, at: (i, 0, 0)),
            pl.BlockSpec((3, own.shape[1], wide), lambda i, at: (0, 0, place(at))),
            pl.BlockSpec(rest.shape, lambda i, at: (0, 0)),
            pl.BlockSpec((None, 1, 3 * wide), lambda i, at: (place(at), 0, 0)),
        ]
        + [pl.BlockSpec(memory_space=pl.ANY)] * len(more),
        [
            pl.BlockSpec((None, rows, 3 * wide), lambda i, at: (i, 0, 0)),
            pl.BlockSpec((None, rows, wide), lambda i, at: (i, 0, place(at))),
            pl.BlockSpec((model, 3 * wide), lambda i, at: (0, g)),
        ],
        [
            shape((count, rows, 3 * wide), BF16),
            shape((count, rows, width), BF16),
            shape((model, 3 * width), BF16),
        ],
        "mix",
        2,
        aliases={5: 1, 6: 2} if more else {},
    )(at, normed, own, rest, bias, *more)


def mix_back(length, g, groups, at, mixed, up, grads):
    count, rows, three = mixed.shape
    wide = three // 3
    lanes = -(-rows // 128) * 128 * (wide // HEAD_DIM)
    shape = jax.ShapeDtypeStruct
    place = (lambda at: at[0] ^ g) if groups > 1 else (lambda at: 0)
    more = [] if grads is None else [grads]
    return scalar_call(
        functools.partial(mix_back_kernel, length),
        at,
        (count,),
        [
            pl.BlockSpec((None, rows, three), lambda i, at: (i, 0, 0)),
            pl.BlockSpec((None, rows, wide), lambda i, at: (i, 0, place(at))),
        ]
        + [pl.BlockSpec(memory_space=pl.ANY)] * len(more),
        [
            pl.BlockSpec((None, rows, three), lambda i, at: (i, 0, g)),
            pl.BlockSpec((None, 1, three), lambda i, at: (i, 0, 0)),
        ],
        [shape((count, rows, groups * three), BF16), shape((count, 1, three), F32)],
        "mix_back",
        2,
        scratch=[
            pltpu.VMEM((rows, lanes), BF16),
            pltpu.VMEM((rows, lanes), BF16),
            pltpu.VMEM((lanes, wide), BF16),
            pltpu.VMEM((lanes, wide), BF16),
        ],
        aliases={3: 0} if more else {},
    )(at, pltpu.with_memory_space_constraint(mixed, pltpu.HBM), pltpu.with_memory_space_constraint(up, pltpu.HBM), *more)


def up_kernel(n_row, at_ref, n_ref, own_ref, rest_ref, bias_ref, *refs):
    act_ref, slope_ref, weight_ref = refs[-3:]
    rows = n_ref.shape[0]
    near = own_ref.shape[0]

    @pl.when(pl.program_id(0) == 0)
    def _():
        for j in range(n_row):
            to = pl.ds(pl.multiple_of((at_ref[1] ^ j) * near, near), near)
            weight_ref[to, :] = own_ref[...] if j == 0 else rest_ref[j - 1]

    for start in range(0, rows, 256):
        at = pl.ds(start, min(256, rows - start))
        hidden = nn(n_ref[at, :], weight_ref[...]) + bias_ref[...]
        gate = 0.5 + 0.5 * jnp.tanh(0.851 * hidden)
        act = hidden * gate
        act_ref[at, :] = act.astype(BF16)
        slope_ref[at, :] = (gate + 1.702 * act * (1.0 - gate)).astype(BF16)


def up(p, at, normed, own, rest, bias, before):
    run = rest.shape[2]
    units = own.shape[1]
    count, rows, model = normed.shape
    shape = jax.ShapeDtypeStruct
    place = (lambda at: at[0] ^ p) if units > run else (lambda at: 0)
    block = pl.BlockSpec((None, rows, run), lambda i, at: (i, 0, place(at)))
    return scalar_call(
        functools.partial(up_kernel, model // own.shape[0]),
        at,
        (count,),
        [
            pl.BlockSpec((None, rows, model), lambda i, at: (i, 0, 0)),
            pl.BlockSpec((own.shape[0], run), lambda i, at: (0, place(at))),
            pl.BlockSpec(rest.shape, lambda i, at: (0, 0, 0)),
            pl.BlockSpec((1, run), lambda i, at: (0, place(at))),
        ]
        + [pl.BlockSpec(memory_space=pl.ANY)] * len(before),
        [block, block, pl.BlockSpec((model, run), lambda i, at: (0, place(at)))],
        [shape((count, rows, units), BF16)] * 2 + [shape((model, units), BF16)],
        "expand",
        1,
        limit=32,
        aliases={5: 0, 6: 1, 7: 2} if before else {},
    )(at, normed, own, rest, bias, *before)


def statistics(value):
    centered = value - jnp.mean(value, axis=-1, keepdims=True)
    inverse = lax.rsqrt(jnp.mean(centered * centered, axis=-1, keepdims=True) + 1e-05)
    return centered * inverse, inverse


def norm_back(upstream, value, gain):
    xhat, inverse = statistics(value)
    scaled = upstream * gain
    first = jnp.mean(scaled, axis=-1, keepdims=True)
    second = jnp.mean(scaled * xhat, axis=-1, keepdims=True)
    grad = inverse * (scaled - first - xhat * second)
    return grad, jnp.sum(upstream * xhat, axis=(0, 1)), jnp.sum(upstream, axis=(0, 1))


def shards(
    images,
    cotangent,
    micro_batch,
    heads_weight,
    heads_bias,
    merge_weight,
    merge_bias,
    expand_weight,
    expand_bias,
    shrink_weight,
    shrink_bias,
    norm_gains,
    norm_shifts,
):
    n_dp, n_row = lax.axis_size("dp"), lax.axis_size("row")
    count, length, width = images.shape
    model = width * lax.axis_size("col")
    rows = -(-length // 16) * 16
    pad = ((0, 0), (0, rows - length), (0, 0))
    units = expand_weight.shape[1]
    run = width // n_dp
    split = run % HEAD_DIM == 0
    groups = n_dp if split else 1
    wide = width // groups
    at = jnp.stack([lax.axis_index(axis) for axis in ("dp", "row", "col")]).astype(jnp.int32)

    heads_own = jnp.transpose(heads_weight, (1, 0, 2))
    heads_send = own_part(heads_own, 2).reshape(-1, run)
    all_slots = count * n_dp * n_row
    assert all_slots <= 256 and run >= MICRO
    member = (micro_batch[:, None] == jnp.arange(run, dtype=jnp.int32)[None, :]).astype(F32)
    tail_own = jnp.broadcast_to(jnp.sum(member, axis=0), (16, run)).astype(BF16)
    heads_send = jnp.concatenate([heads_send, tail_own])
    heads_send, images, cotangent, norm_gains = lax.optimization_barrier(
        (heads_send, images, cotangent, norm_gains)
    )
    heads_rows = [peer(heads_send, "row", j) for j in range(1, n_row)]

    params = jnp.concatenate([norm_gains, norm_shifts, merge_bias[None], shrink_bias[None]], axis=0)
    params_tail = jnp.pad(params, ((0, rows - length - params.shape[0]), (0, 0)))
    x_own = jnp.concatenate([images, jnp.broadcast_to(params_tail, (count,) + params_tail.shape)], axis=1)
    cot_own = jnp.pad(cotangent, pad)
    pair = lax.axis_size("col") == 2
    if pair:
        x_other = peer(x_own, "col", 1)
        params = col_join(params, x_other[0, length : length + 6])
    else:
        x = col_full(x_own, 2)
        params = x[0, length : length + 6]
    gain_one, gain_two, shift_one, shift_two, merge_bias_full, _ = (
        params[k].astype(F32) for k in range(6)
    )
    if pair:
        x, normed = join(at, x_own, x_other, (gain_one[None], shift_one[None]))
    else:
        xhat, _ = statistics(x.astype(F32))
        normed = (xhat * gain_one + shift_one).astype(BF16)
    bias3 = jnp.stack([heads_bias[0], jnp.zeros_like(heads_bias[0]), heads_bias[1]]).astype(F32)
    bias3 = bias3.reshape(3, groups, wide).transpose(1, 0, 2).reshape(groups, 1, 3 * wide)

    heads_rows, normed, x, cot_own, expand_send, shrink_send = (
        lax.optimization_barrier(
            (
                heads_rows,
                normed,
                x,
                cot_own,
                own_part(expand_weight, 1),
                own_part(shrink_weight, 0),
            )
        )
    )
    heads_parts = dp_parts(stack(tail_own, heads_rows))
    lanes = merge_weight.shape[1]
    joined = expand_send.shape[1] % lanes == 0
    if joined:
        pieces = [expand_send[:, k : k + lanes] for k in range(0, expand_send.shape[1], lanes)]
        gathered = lax.all_gather(jnp.concatenate([merge_weight, *pieces]), "row")
    else:
        merge_full = lax.all_gather(merge_weight, "row", axis=1, tiled=True)
        expand_rows = lax.all_gather(expand_send, "row")
    shrink_rows = lax.all_gather(shrink_send, "row")
    totals = [piece[-1:, :MICRO].astype(F32) for piece in heads_parts]
    while len(totals) > 1:
        totals = [totals[k] + totals[k + 1] for k in range(0, len(totals), 2)]
    batch_weight = all_slots / (MICRO * totals[0])
    slot_weight = jnp.sum(member[:, :MICRO] * batch_weight, axis=1)
    if not split:
        heads_parts = [xor_order(lax.concatenate(heads_parts, 1), 1, "dp")]

    cot_other = peer(cot_own, "col", 1) if pair else None

    mixed, attended, heads_full = [None] * groups, None, None
    for g in range(groups):
        mixed[g], attended, heads_full = mix(
            length, g, at, normed, heads_own, heads_parts[g], bias3, attended, heads_full, width
        )

    if joined:
        attended, gathered = lax.optimization_barrier((attended, gathered))
        merge_full, expand_rows = unpack(at, gathered, width, expand_weight.shape[0])
        expand_rest = dp_parts(expand_rows[1:])
    else:
        expand_rest = dp_parts(others(at, expand_rows))
    merge_part = jnp.einsum("itf,fd->itd", attended, merge_full, preferred_element_type=F32)
    merge_part, expand_rest[1:3] = lax.optimization_barrier((merge_part.astype(BF16), expand_rest[1:3]))
    share_a, share_b = col_shares(merge_part)
    middle = x.astype(F32) + ((share_a.astype(F32) + share_b.astype(F32)) + merge_bias_full)
    xhat, _ = statistics(middle)
    normed_two = (xhat * gain_two + shift_two).astype(BF16)

    if (units // n_dp) % 128:
        expand_rest = [xor_order(lax.concatenate(expand_rest, 2), 2, "dp")]
    made = ()
    for p, piece in enumerate(expand_rest):
        if p == min(1, len(expand_rest) - 1):
            made, shrink_rows = lax.optimization_barrier((made, shrink_rows))
            shrink_rest = others(at, shrink_rows)
            piece, shrink_rest = lax.optimization_barrier((piece, shrink_rest))
            shrink_rest = dp_parts(shrink_rest)
        made = up(p, at, normed_two, expand_weight, piece, expand_bias.astype(F32)[None], made)
    activated, slope, expand_full = made
    if pair:
        cot, seed_low, seed_sums = seed_of(at, cot_own, cot_other, slot_weight)
    else:
        cot = col_full(cot_own, 2)
        seed_low = (cot.astype(F32) * slot_weight[:, None, None]).astype(BF16)
        seed_sums = jnp.sum(seed_low.astype(F32), axis=1, keepdims=True)
    seed = cot.astype(F32) * slot_weight[:, None, None]

    shrink_grad = jnp.einsum("ith,itd->hd", activated, seed_low, preferred_element_type=F32)
    shrink_grad, seed_low, shrink_rest[0] = lax.optimization_barrier(
        (shrink_grad.astype(BF16), seed_low, shrink_rest[0])
    )
    shrink_sum = scatter_row(shrink_grad, 1)
    shrink_full = ()
    for p, piece in enumerate(shrink_rest):
        shrink_full = (place(p, at, shrink_weight, piece, shrink_full),)
    (shrink_full,) = shrink_full
    act_grad = jnp.einsum("itd,hd->ith", seed_low, shrink_full, preferred_element_type=F32)
    hidden_grad = (act_grad * slope.astype(F32)).astype(BF16)
    hidden_sums = jnp.sum(hidden_grad.astype(F32), axis=(0, 1))
    expand_grad = jnp.einsum("ith,itd->hd", hidden_grad, normed_two, preferred_element_type=F32)
    expand_grad, hidden_grad, hidden_sums = lax.optimization_barrier(
        (expand_grad.astype(BF16), hidden_grad, hidden_sums)
    )
    expand_sum = dp_sum(expand_grad)
    norm_part = jnp.einsum("ith,dh->itd", hidden_grad, expand_full, preferred_element_type=F32)
    norm_part = norm_part.astype(BF16)
    share_a, share_b = col_shares(norm_part)
    result, gain_sum_two, shift_sum_two = norm_back(
        share_a.astype(F32) + share_b.astype(F32), middle, gain_two
    )
    middle_grad = seed + result
    branch_grad = middle_grad.astype(BF16)

    attended_grad = jnp.einsum(
        "itd,fd->itf", branch_grad, merge_full, preferred_element_type=F32
    ).astype(BF16)
    merge_grad = jnp.einsum("itf,itd->fd", attended, branch_grad, preferred_element_type=F32)
    merge_grad, attended_grad = lax.optimization_barrier((merge_grad.astype(BF16), attended_grad))
    mixed_grad, mixed_sums, heads_grads = None, [None] * groups, [None] * groups
    merge_sum, heads_in = scatter_row(merge_grad, 1), [None] * groups
    part = units // n_dp
    order = list(range(1, groups)) + [0]
    for turn, g in enumerate(order):
        if turn == max(groups - 2, 0):
            attended_grad, expand_sum, shrink_sum = lax.optimization_barrier(
                (attended_grad, expand_sum, shrink_sum)
            )
            expand_sum = scatter_row(expand_sum, 1)
        if g == 0:
            attended_grad, merge_sum, heads_in[1:2] = lax.optimization_barrier(
                (attended_grad, merge_sum, heads_in[1:2])
            )
            both = jnp.concatenate(
                [shrink_sum.reshape(n_dp, part, -1), merge_sum.reshape(n_dp, run, -1)], axis=1
            )
            both = dp_sum(both.reshape(units + width, -1))
        mixed_grad, mixed_sums[g] = mix_back(length, g, groups, at, mixed[g], attended_grad, mixed_grad)
        piece = mixed_grad[:, :, g * 3 * wide : (g + 1) * 3 * wide]
        heads_grads[g] = jnp.einsum("itd,itf->df", normed, piece, preferred_element_type=F32).astype(BF16)
        if g:
            attended_grad, heads_grads[g] = lax.optimization_barrier((attended_grad, heads_grads[g]))
            heads_in[g] = peer(heads_grads[g], "dp", g)
    if not split:
        whole = xor_order(heads_grads[0].reshape(model, 3, width), 2, "dp")
        heads_grads = [cut(whole, 2, n_dp, p).reshape(model, 3 * run) for p in range(n_dp)]
        heads_in = [None] + [peer(heads_grads[p], "dp", p) for p in range(1, n_dp)]
    heads_sum = heads_grads[0].astype(F32)
    for piece in heads_in[1:]:
        heads_sum = heads_sum + piece.astype(F32)
    heads_sum = heads_sum.astype(BF16)
    heads_sum = sum_parts([cut(heads_sum, 0, n_row, j) for j in range(n_row)], "row", at[1])
    mixed_grad, activated, both, expand_sum = lax.optimization_barrier(
        (mixed_grad, activated, both, expand_sum)
    )
    first_part = jnp.einsum("itf,df->itd", mixed_grad, heads_full, preferred_element_type=F32)
    share_a, share_b = col_shares(first_part.astype(BF16))
    packed = dp_all(jnp.concatenate([both, expand_sum]))
    shrink_part = jnp.einsum("ith,hd->itd", activated, shrink_full, preferred_element_type=F32).astype(BF16)
    shrink_part, heads_sum = lax.optimization_barrier((shrink_part, heads_sum))
    result, gain_sum_one, shift_sum_one = norm_back(
        share_a.astype(F32) + share_b.astype(F32), x.astype(F32), gain_one
    )

    if pair:
        other = peer(half(at, shrink_part, False), "col", 1)
        output = close(at, middle, shrink_part, other, shrink_bias.astype(F32)[None])
    else:
        branch_two = col_own(lax.psum(shrink_part, "col").astype(F32), 2)
        output = (col_own(middle, 2) + (branch_two + shrink_bias.astype(F32))).astype(BF16)
    output = output[:, :length]
    input_grad = col_own(middle_grad + result, 2)[:, :length]
    heads_out = dp_parts(heads_sum)
    heads_out, packed, input_grad, output = lax.optimization_barrier((heads_out, packed, input_grad, output))

    model_sums = jnp.stack(
        [
            gain_sum_one,
            gain_sum_two,
            shift_sum_one,
            shift_sum_two,
            jnp.sum(branch_grad.astype(F32), axis=(0, 1)),
            jnp.sum(seed_sums, axis=(0, 1)),
        ]
    )
    model_sums = col_own(model_sums, 1)
    mixed_sums = jnp.sum(jnp.concatenate(mixed_sums, axis=1), axis=0)
    mixed_sums = mixed_sums.reshape(groups, 3, wide).transpose(1, 0, 2).reshape(3, width)
    heads_bias_grad = mixed_sums[0::2]
    if split:
        heads_bias_grad = xor_order(heads_bias_grad, 1, "dp")
    small = sum_all(jnp.concatenate([model_sums.ravel(), heads_bias_grad.ravel(), hidden_sums]))
    shrink_sum = packed[:, :part].reshape(units, -1).astype(F32)
    merge_sum = packed[:, part : part + run].reshape(width, -1).astype(F32)
    expand_sum = packed[:, part + run :].reshape(units, -1).T.astype(F32)
    if run % 128:
        heads_sum = [piece.reshape(-1, 3, run) for piece in heads_out]
        heads_sum = xor_order(jnp.concatenate(heads_sum, axis=2), 2, "dp").astype(F32)
    else:
        heads_sum = jnp.transpose(spread(at, heads_out), (1, 0, 2))

    model_sums = small[: 6 * width].reshape(6, width)
    return (
        output,
        input_grad,
        heads_sum,
        small[6 * width : 8 * width].reshape(2, width),
        merge_sum,
        model_sums[4],
        expand_sum,
        small[8 * width :],
        shrink_sum,
        model_sums[5],
        model_sums[0:2],
        model_sums[2:4],
    )


def solution(mesh):
    placed = (
        P(("dp", "row"), None, "col"),
        P(("dp", "row"), None, "col"),
        P(("dp", "row")),
        P("row", None, "col"),
        P(None, "col"),
        P("col", "row"),
        P("col"),
        P("row", "col"),
        P("col"),
        P("col", "row"),
        P("col"),
        P(None, "col"),
        P(None, "col"),
    )
    return jax.shard_map(
        shards,
        mesh=mesh,
        in_specs=placed,
        out_specs=(
            P(("dp", "row"), None, "col"),
            P(("dp", "row"), None, "col"),
            P("row", None, "col"),
            P(None, "col"),
            P("col", "row"),
            P("col"),
            P("row", "col"),
            P("col"),
            P("col", "row"),
            P("col"),
            P(None, "col"),
            P(None, "col"),
        ),
        check_vma=False,
    )
```

```python
import functools

import jax
import jax.numpy as jnp
from jax import lax
from jax.experimental import pallas as pl
from jax.experimental.pallas import tpu as pltpu
from jax.sharding import PartitionSpec as P

HEAD_DIM = 64
MICRO = 2
BF16 = jnp.bfloat16
F32 = jnp.float32
VMEM_LIMIT = 58 << 20
STEP = 304
KEYS = 304


def peer(value, axis, p):
    n = lax.axis_size(axis)
    return lax.ppermute(value, axis, [(i, i ^ p) for i in range(n)])


def xor_order(value, dim, axis):
    n = lax.axis_size(axis)
    index = lax.axis_index(axis)
    size = value.shape[dim]
    bit = 1
    while bit < n:
        run = size * bit // n
        pieces = [lax.slice_in_dim(value, at, at + run, axis=dim) for at in range(0, size, run)]
        swapped = lax.concatenate([pieces[k ^ 1] for k in range(len(pieces))], dim)
        value = jnp.where((index & bit) != 0, swapped, value)
        bit *= 2
    return value


def cut(value, dim, n, k):
    run = value.shape[dim] // n
    return lax.slice_in_dim(value, k * run, (k + 1) * run, axis=dim)


def own_part(own, inner_dim):
    run = own.shape[inner_dim] // lax.axis_size("dp")
    return lax.dynamic_slice_in_dim(own, lax.axis_index("dp") * run, run, inner_dim)


def dp_parts(part):
    return [part] + [peer(part, "dp", p) for p in range(1, lax.axis_size("dp"))]


def sum_parts(parts, axis, start=None):
    n = lax.axis_size(axis)
    if start is not None:
        stacked = jnp.stack(parts)
        parts = [lax.dynamic_index_in_dim(stacked, start ^ p, 0, keepdims=False) for p in range(n)]
    total = parts[0].astype(F32)
    for p in range(1, n):
        total = total + peer(parts[p], axis, p).astype(F32)
    return total.astype(BF16)


def dp_sum(blocks):
    n = lax.axis_size("dp")
    blocks = blocks.reshape((n, blocks.shape[0] // n) + blocks.shape[1:])
    return add(lax.all_to_all(blocks, "dp", 0, 0))


def dp_all(part):
    n = lax.axis_size("dp")
    return lax.all_to_all(jnp.broadcast_to(part[None], (n,) + part.shape), "dp", 0, 0)


def scatter_row(value, model_dim):
    return lax.psum_scatter(value, "row", scatter_dimension=model_dim, tiled=True)


def sum_all(value):
    for axis in ("dp", "row"):
        terms = dp_parts(value) if axis == "dp" else [value] + [peer(value, "row", j) for j in range(1, lax.axis_size("row"))]
        while len(terms) > 1:
            terms = [terms[k] + terms[k + 1] for k in range(0, len(terms), 2)]
        value = terms[0]
    return value


def col_join(own, other):
    first = lax.axis_index("col") == 0
    return lax.concatenate([jnp.where(first, own, other), jnp.where(first, other, own)], own.ndim - 1)


def col_full(own, feature_dim):
    return lax.all_gather(own, "col", axis=feature_dim, tiled=True)


def col_own(full, feature_dim):
    n_col = lax.axis_size("col")
    if n_col == 2:
        return jnp.where(
            lax.axis_index("col") == 0, cut(full, feature_dim, 2, 0), cut(full, feature_dim, 2, 1)
        )
    width = full.shape[feature_dim] // n_col
    return lax.dynamic_slice_in_dim(full, lax.axis_index("col") * width, width, feature_dim)


def col_shares(part):
    if lax.axis_size("col") == 2:
        return part, peer(part, "col", 1)
    return lax.psum(part, "col"), jnp.zeros_like(part)


def nt(a, b):
    return lax.dot_general(a, b, (((1,), (1,)), ((), ())), preferred_element_type=F32)


def nn(a, b):
    return lax.dot_general(a, b, (((1,), (0,)), ((), ())), preferred_element_type=F32)


def cost(us, moved=1 << 20):
    return pl.CostEstimate(flops=int(us * 1.0e7), bytes_accessed=1024, transcendentals=0)


def scalar_call(body, at, grid, in_specs, out_specs, out_shape, name, us, scratch=(), limit=24, aliases=None):
    far = lambda a: pltpu.HBM(a.shape, a.dtype)
    out_shape = [far(a) for a in out_shape] if isinstance(out_shape, list) else far(out_shape)
    return pl.pallas_call(
        body,
        grid_spec=pltpu.PrefetchScalarGridSpec(
            num_scalar_prefetch=1,
            grid=grid,
            in_specs=in_specs,
            out_specs=out_specs,
            scratch_shapes=list(scratch),
        ),
        out_shape=out_shape,
        input_output_aliases=aliases or {},
        compiler_params=pltpu.CompilerParams(vmem_limit_bytes=limit << 20),
        cost_estimate=cost(us),
        name=name,
    )


def row_chunks(rows, body):
    for start in range(0, rows, STEP):
        body(pl.ds(start, min(STEP, rows - start)))


def spread_of(value):
    centered = value - jnp.mean(value, axis=1, keepdims=True)
    inverse = lax.rsqrt(jnp.mean(centered * centered, axis=1, keepdims=True) + 1e-05)
    return centered * inverse, inverse


def norm_kernel(x_ref, a_ref, b_ref, params_ref, middle_ref, normed_ref):
    def body(at):
        value = a_ref[at, :].astype(F32) + b_ref[at, :].astype(F32)
        value = x_ref[at, :].astype(F32) + (value + params_ref[0:1, :])
        middle_ref[at, :] = value
        xhat, _ = spread_of(value)
        normed_ref[at, :] = (xhat * params_ref[1:2, :] + params_ref[2:3, :]).astype(BF16)

    row_chunks(x_ref.shape[0], body)


def norm_of_sum(x, share_a, share_b, params):
    count, rows, model = x.shape
    image = pl.BlockSpec((None, rows, model), lambda i: (i, 0, 0))
    return pl.pallas_call(
        norm_kernel,
        grid=(count,),
        in_specs=[image] * 3 + [pl.BlockSpec(params.shape, lambda i: (0, 0))],
        out_specs=[image] * 2,
        out_shape=[pltpu.HBM(x.shape, F32), pltpu.HBM(x.shape, BF16)],
        compiler_params=pltpu.CompilerParams(vmem_limit_bytes=32 << 20),
        cost_estimate=cost(2),
        name="norm_two",
    )(x, share_a, share_b, params)


def norm_back_kernel(second, at_ref, base_ref, v_ref, a_ref, b_ref, gain_ref, weight_ref, *refs):
    grad_ref, *low_ref, sums_ref, scratch = refs
    rows = v_ref.shape[0]
    totals = None

    def body(at):
        nonlocal totals
        xhat, inverse = spread_of(v_ref[at, :].astype(F32))
        upstream = a_ref[at, :].astype(F32) + b_ref[at, :].astype(F32)
        scaled = upstream * gain_ref[...]
        first = jnp.mean(scaled, axis=1, keepdims=True)
        other = jnp.mean(scaled * xhat, axis=1, keepdims=True)
        base = base_ref[at, :].astype(F32)
        if second:
            base = base * weight_ref[pl.program_id(0)]
        grad = base + inverse * (scaled - first - xhat * other)
        parts = [jnp.sum(upstream * xhat, axis=0, keepdims=True), jnp.sum(upstream, axis=0, keepdims=True)]
        if second:
            grad_ref[at, :] = grad
            low = grad.astype(BF16)
            low_ref[0][at, :] = low
            parts.append(jnp.sum(low.astype(F32), axis=0, keepdims=True))
        else:
            scratch[at, :] = grad
        totals = parts if totals is None else [x + y for x, y in zip(totals, parts)]

    row_chunks(rows, body)
    for k, total in enumerate(totals):
        sums_ref[k : k + 1, :] = total
    if not second:
        length, width = grad_ref.shape
        grad_ref[...] = scratch[:length, pl.ds(pl.multiple_of(at_ref[2] * width, width), width)]


def norm_back(at, base, v, share_a, share_b, gain, weight, own):
    count, rows, model = v.shape
    second = own is None
    shape = jax.ShapeDtypeStruct
    image = pl.BlockSpec((None, rows, model), lambda i, at: (i, 0, 0))
    sums = 3 if second else 2
    outs = [image, image] if second else [pl.BlockSpec((None,) + own, lambda i, at: (i, 0, 0))]
    shapes = [shape(v.shape, F32), shape(v.shape, BF16)] if second else [shape((count,) + own, F32)]
    return scalar_call(
        functools.partial(norm_back_kernel, second),
        at,
        (count,),
        [image] * 4
        + [pl.BlockSpec((1, model), lambda i, at: (0, 0)), pl.BlockSpec(memory_space=pltpu.SMEM)],
        outs + [pl.BlockSpec((None, sums, model), lambda i, at: (i, 0, 0))],
        shapes + [shape((count, sums, model), F32)],
        "norm_back",
        2,
        scratch=[pltpu.VMEM((8, 128) if second else (rows, model), F32)],
        limit=48,
    )(at, base, v, share_a, share_b, gain[None], weight)


def join_kernel(normal, at_ref, own_ref, other_ref, *refs):
    out_ref = refs[2] if normal else refs[0]
    rows, width = own_ref.shape
    to = pl.ds(pl.multiple_of(at_ref[2] * width, width), width)
    away = pl.ds(pl.multiple_of((1 - at_ref[2]) * width, width), width)
    out_ref[:, to] = own_ref[...]
    out_ref[:, away] = other_ref[...]
    if not normal:
        return
    gain_ref, shift_ref, _, normed_ref = refs

    def body(at):
        value = out_ref[at, :].astype(F32)
        centered = value - jnp.mean(value, axis=1, keepdims=True)
        inverse = lax.rsqrt(jnp.mean(centered * centered, axis=1, keepdims=True) + 1e-05)
        normed_ref[at, :] = (centered * inverse * gain_ref[...] + shift_ref[...]).astype(BF16)

    row_chunks(rows, body)


def join(at, own, other, vectors=None):
    count, rows, width = own.shape
    normal = vectors is not None
    shape = jax.ShapeDtypeStruct((count, rows, 2 * width), BF16)
    half = pl.BlockSpec((None, rows, width), lambda i, at: (i, 0, 0))
    full = pl.BlockSpec((None, rows, 2 * width), lambda i, at: (i, 0, 0))
    vector = pl.BlockSpec((1, 2 * width), lambda i, at: (0, 0))
    return scalar_call(
        functools.partial(join_kernel, normal),
        at,
        (count,),
        [half, half] + [vector] * (2 if normal else 0),
        [full, full] if normal else full,
        [shape, shape] if normal else shape,
        "join",
        2,
    )(at, own, other, *(vectors or ()))


def seed_kernel(at_ref, own_ref, other_ref, weight_ref, cot_ref, seed_ref, sums_ref, sums):
    rows, width = own_ref.shape
    scale = weight_ref[pl.program_id(0)]
    sums[...] = jnp.zeros_like(sums)
    for k, ref in enumerate((own_ref, other_ref)):
        place = at_ref[2] if k == 0 else 1 - at_ref[2]
        to = pl.ds(pl.multiple_of(place * width, width), width)

        def body(at):
            value = ref[at, :]
            low = (value.astype(F32) * scale).astype(BF16)
            cot_ref[at, to] = value
            seed_ref[at, to] = low
            low = low.astype(F32)
            sums[:, to] += jnp.sum(low.reshape(low.shape[0] // 8, 8, width), axis=0)

        row_chunks(rows, body)
    sums_ref[...] = jnp.sum(sums[...], axis=0, keepdims=True)


def seed_of(at, own, other, weight):
    count, rows, width = own.shape
    shape = jax.ShapeDtypeStruct
    half = pl.BlockSpec((None, rows, width), lambda i, at: (i, 0, 0))
    full = pl.BlockSpec((None, rows, 2 * width), lambda i, at: (i, 0, 0))
    return scalar_call(
        seed_kernel,
        at,
        (count,),
        [half, half, pl.BlockSpec(memory_space=pltpu.SMEM)],
        [full, full, pl.BlockSpec((None, 1, 2 * width), lambda i, at: (i, 0, 0))],
        [shape((count, rows, 2 * width), BF16)] * 2 + [shape((count, 1, 2 * width), F32)],
        "seed",
        2,
        scratch=[pltpu.VMEM((8, 2 * width), F32)],
    )(at, own, other, weight)


def stay(value):
    return pltpu.with_memory_space_constraint(value, pltpu.HBM)


def stack_kernel(body_rows, own_ref, *refs):
    out_ref = refs[-1]
    total = own_ref[...].astype(F32)
    for k, ref in enumerate(refs[:-1]):
        out_ref[k * body_rows : (k + 1) * body_rows, :] = ref[:body_rows, :]
        total = total + ref[body_rows:, :].astype(F32)
    out_ref[(len(refs) - 1) * body_rows :, :] = total.astype(BF16)


def stack(own_tail, arrays):
    vmem = pl.BlockSpec(memory_space=pltpu.VMEM)
    more, lanes = own_tail.shape
    body = arrays[0].shape[0] - more
    return pl.pallas_call(
        functools.partial(stack_kernel, body),
        in_specs=[vmem] * (1 + len(arrays)),
        out_specs=vmem,
        out_shape=jax.ShapeDtypeStruct((len(arrays) * body + more, lanes), BF16),
        compiler_params=pltpu.CompilerParams(vmem_limit_bytes=16 << 20),
        cost_estimate=cost(1),
        name="stack",
    )(own_tail, *arrays)


def unpack_kernel(n_row, at_ref, in_ref, merge_ref, expand_ref):
    z = pl.program_id(0)
    rows, run = merge_ref.shape
    near = expand_ref.shape[0]
    merge_ref[...] = in_ref[:rows, :]
    for k in range(expand_ref.shape[1] // run):
        expand_ref[:, k * run : (k + 1) * run] = in_ref[rows + k * near : rows + (k + 1) * near, :]


def unpack(at, gathered, rows, near):
    n_row, total, run = gathered.shape
    wide = (total - rows) // near * run
    shape = jax.ShapeDtypeStruct
    return scalar_call(
        functools.partial(unpack_kernel, n_row),
        at,
        (n_row,),
        [pl.BlockSpec((None, total, run), lambda j, at: (at[1] ^ j, 0, 0))],
        [
            pl.BlockSpec((rows, run), lambda j, at: (0, at[1] ^ j)),
            pl.BlockSpec((None, near, wide), lambda j, at: (jnp.maximum(j - 1, 0), 0, 0)),
        ],
        [shape((rows, n_row * run), BF16), shape((n_row - 1, near, wide), BF16)],
        "unpack",
        1,
    )(at, stay(gathered))


def pick_kernel(at_ref, in_ref, out_ref):
    for q in range(out_ref.shape[0]):
        out_ref[q] = in_ref[...]


def others(at, gathered):
    n_dp, n_row = lax.axis_size("dp"), gathered.shape[0]
    block = (None,) + gathered.shape[1:]
    return scalar_call(
        pick_kernel,
        at,
        (n_row - 1,),
        [pl.BlockSpec(block, lambda j, at: (at[1] ^ (j + 1), 0, 0))],
        pl.BlockSpec((n_dp,) + block, lambda j, at: (0, j, 0, 0)),
        jax.ShapeDtypeStruct((n_dp, n_row - 1) + gathered.shape[1:], gathered.dtype),
        "others",
        1,
    )(at, stay(gathered))


def place_kernel(at_ref, own_ref, rest_ref, out_ref, sems):
    n_dp, others, run, near = rest_ref.shape
    copies = [
        pltpu.make_async_copy(
            own_ref,
            out_ref.at[:, pl.ds(pl.multiple_of(at_ref[1] * near, near), near)],
            sems.at[0],
        )
    ]
    for q in range(n_dp):
        for j in range(others):
            to = pl.ds(pl.multiple_of((at_ref[1] ^ (j + 1)) * near, near), near)
            copies.append(
                pltpu.make_async_copy(
                    rest_ref.at[q, j], out_ref.at[q * run : (q + 1) * run, to], sems.at[len(copies)]
                )
            )
    for copy in copies:
        copy.start()
    for copy in copies:
        copy.wait()


def place(at, own, rest):
    n_dp, others, run, near = rest.shape
    return pl.pallas_call(
        place_kernel,
        in_specs=[pl.BlockSpec(memory_space=pltpu.SMEM)] + [pl.BlockSpec(memory_space=pl.ANY)] * 2,
        out_specs=pl.BlockSpec(memory_space=pltpu.VMEM),
        out_shape=jax.ShapeDtypeStruct((n_dp * run, (others + 1) * near), own.dtype),
        scratch_shapes=[pltpu.SemaphoreType.DMA((1 + n_dp * others,))],
        compiler_params=pltpu.CompilerParams(vmem_limit_bytes=8 << 20),
        cost_estimate=cost(1),
        name="place",
    )(at, stay(own), stay(rest))


def add_kernel(in_ref, out_ref):
    out_ref[...] = jnp.sum(in_ref[...].astype(F32), axis=0).astype(BF16)


def add(blocks):
    n, rows, lanes = blocks.shape
    step = rows // 4 if rows % 64 == 0 else rows
    return pl.pallas_call(
        add_kernel,
        grid=(rows // step,),
        in_specs=[pl.BlockSpec((n, step, lanes), lambda i: (0, i, 0))],
        out_specs=pl.BlockSpec((step, lanes), lambda i: (i, 0)),
        out_shape=jax.ShapeDtypeStruct((rows, lanes), BF16),
        compiler_params=pltpu.CompilerParams(vmem_limit_bytes=24 << 20),
        cost_estimate=cost(1),
        name="add",
    )(blocks)


def half_kernel(at_ref, in_ref, out_ref):
    out_ref[...] = in_ref[...]


def half(at, value, own):
    count, rows, model = value.shape
    place = (lambda at: at[2]) if own else (lambda at: 1 - at[2])
    return scalar_call(
        half_kernel,
        at,
        (count,),
        [pl.BlockSpec((None, rows, model // 2), lambda i, at: (i, 0, place(at)))],
        pl.BlockSpec((None, rows, model // 2), lambda i, at: (i, 0, 0)),
        jax.ShapeDtypeStruct((count, rows, model // 2), value.dtype),
        "half",
        1,
    )(at, value)


def close_kernel(at_ref, m_ref, a_ref, b_ref, bias_ref, out_ref):
    def body(at):
        share = a_ref[at, :].astype(F32) + b_ref[at, :].astype(F32)
        out_ref[at, :] = (m_ref[at, :] + (share + bias_ref[...])).astype(BF16)

    row_chunks(out_ref.shape[0], body)


def close(at, middle, part, other, bias, length):
    count, rows, width = other.shape
    mine = pl.BlockSpec((None, rows, width), lambda i, at: (i, 0, at[2]))
    plain = pl.BlockSpec((None, rows, width), lambda i, at: (i, 0, 0))
    return scalar_call(
        close_kernel,
        at,
        (count,),
        [mine, mine, plain, pl.BlockSpec((1, width), lambda i, at: (0, 0))],
        pl.BlockSpec((None, length, width), lambda i, at: (i, 0, 0)),
        jax.ShapeDtypeStruct((count, length, width), BF16),
        "close",
        1,
    )(at, middle, part, other, bias)


def spread_kernel(n_dp, at_ref, *refs):
    out_ref = refs[-1]
    run = out_ref.shape[2] // n_dp
    for p in range(n_dp):
        to = pl.ds(pl.multiple_of((at_ref[0] ^ p) * run, run), run)
        for k in range(3):
            out_ref[k, :, to] = refs[p][:, k * run : (k + 1) * run].astype(F32)


def spread(at, parts):
    n_dp = len(parts)
    rows, three = parts[0].shape
    run = three // 3
    vmem = pl.BlockSpec((rows, three), lambda i, at: (0, 0))
    return scalar_call(
        functools.partial(spread_kernel, n_dp),
        at,
        (1,),
        [vmem] * n_dp,
        pl.BlockSpec((3, rows, n_dp * run), lambda i, at: (0, 0, 0)),
        jax.ShapeDtypeStruct((3, rows, n_dp * run), F32),
        "spread",
        1,
    )(at, *parts)


def head_mask(rows, width, h):
    lane = lax.broadcasted_iota(jnp.int32, (rows, width), 1)
    return (lane >= h * HEAD_DIM) & (lane < (h + 1) * HEAD_DIM)


def mix_kernel(length, n_row, at_ref, n_ref, own_ref, rest_ref, bias_ref, *refs):
    mixed_ref, o_ref, weight_ref, exact_ref, stats_ref, lanes_ref = refs[-6:]
    rows = n_ref.shape[0]
    width = o_ref.shape[1]
    count = width // HEAD_DIM
    near = own_ref.shape[1]
    chunk = rows

    @pl.when(pl.program_id(0) == 0)
    def _():
        for j in range(n_row):
            to = pl.ds(pl.multiple_of((at_ref[1] ^ j) * near, near), near)
            for k in range(3):
                start = ((j - 1) * 3 + k) * near
                piece = own_ref[k] if j == 0 else rest_ref[start : start + near, :]
                weight_ref[to, k * width : (k + 1) * width] = piece

    for start in range(0, rows, chunk):
        size = min(chunk, rows - start)
        at = pl.ds(start, size)
        mixed = nn(n_ref[at, :], weight_ref[...]) + bias_ref[...]
        mixed_ref[at, :width] = (mixed[:, :width] * HEAD_DIM**-0.5).astype(BF16)
        mixed_ref[at, width:] = mixed[:, width:].astype(BF16)
    plain = length // 128 * 128
    k = mixed_ref[:, width : 2 * width]
    v = mixed_ref[:, 2 * width :]
    for start in range(0, rows, chunk):
        size = min(chunk, rows - start)
        at = pl.ds(start, size)
        q = mixed_ref[at, :width]
        result, stats = None, jnp.zeros((size, 128), F32)
        place = lax.broadcasted_iota(jnp.int32, (size, 128), 1)
        for h in range(count):
            mask = head_mask(size, width, h)
            query = jnp.where(mask, q, jnp.zeros_like(q))
            near, far = nt(query, k[:plain]), nt(query, k[plain:])
            key = lax.broadcasted_iota(jnp.int32, far.shape, 1) + plain
            far = jnp.where(key < length, far, -1e30)
            top = jnp.maximum(jnp.max(near, axis=1, keepdims=True), jnp.max(far, axis=1, keepdims=True))
            near, far = jnp.exp(near - top), jnp.exp(far - top)
            total = jnp.sum(near, axis=1, keepdims=True) + jnp.sum(far, axis=1, keepdims=True)
            out = (nn(near.astype(BF16), v[:plain]) + nn(far.astype(BF16), v[plain:])) / total
            result = out if result is None else jnp.where(mask, out, result)
            stats = jnp.where(place == h, top + jnp.log(total), stats)
        o_ref[at, :] = result.astype(BF16)
        exact_ref[at, :] = result
        lanes_ref[at, :] = stats
    row = lax.broadcasted_iota(jnp.int32, (8, 128), 0)
    lane = lax.broadcasted_iota(jnp.int32, (8, 128), 1)
    stats_ref[...] = turned(jnp.where(row == lane, 1.0, 0.0), lanes_ref[...])


def turned(select, value):
    return lax.dot_general(
        select, value, (((1,), (1,)), ((), ())), precision=lax.Precision.HIGHEST, preferred_element_type=F32
    )


def mix_back_kernel(length, at_ref, m_ref, up_ref, exact_ref, stats_ref, *refs):
    d_ref, sums_ref, probs, grads, q_all, up_all = refs[-6:]
    rows, width = up_ref.shape
    count = width // HEAD_DIM
    lanes = probs.shape[1] // count
    chunk = 256
    row = lax.broadcasted_iota(jnp.int32, (8, width), 0)
    lane = lax.broadcasted_iota(jnp.int32, (8, width), 1)
    select = jnp.where((lane >= row * HEAD_DIM) & (lane < (row + 1) * HEAD_DIM), 1.0, 0.0)
    delta = turned(select, up_ref[...].astype(F32) * exact_ref[...])
    for h in range(count):
        base = h * lanes
        if rows < lanes:
            probs[:, pl.ds(base + rows, lanes - rows)] = jnp.zeros((rows, lanes - rows), BF16)
            grads[:, pl.ds(base + rows, lanes - rows)] = jnp.zeros((rows, lanes - rows), BF16)
            q_all[pl.ds(base + rows, lanes - rows), :] = jnp.zeros((lanes - rows, width), BF16)
            up_all[pl.ds(base + rows, lanes - rows), :] = jnp.zeros((lanes - rows, width), BF16)
        for start in range(0, rows, chunk):
            size = min(chunk, rows - start)
            mask = head_mask(size, width, h)
            q = m_ref[pl.ds(start, size), :width]
            up = up_ref[pl.ds(start, size), :]
            q = jnp.where(mask, q, jnp.zeros_like(q))
            up = jnp.where(mask, up, jnp.zeros_like(up))
            q_all[pl.ds(base + start, size), :] = q
            up_all[pl.ds(base + start, size), :] = up
            total = stats_ref[h : h + 1, start : start + size]
            mean = delta[h : h + 1, start : start + size]
            for first in range(0, rows, KEYS):
                keys = pl.ds(first, min(KEYS, rows - first))
                share = jnp.exp(nt(m_ref[keys, width : 2 * width], q) - total)
                if first + KEYS > length:
                    key = lax.broadcasted_iota(jnp.int32, share.shape, 0) + first
                    share = jnp.where(key < length, share, 0.0)
                prob_grad = nt(m_ref[keys, 2 * width :], up)
                probs[keys, pl.ds(base + start, size)] = share.astype(BF16)
                grads[keys, pl.ds(base + start, size)] = (share * (prob_grad - mean)).astype(BF16)
    dv = nn(probs[...], up_all[...]).astype(BF16)
    dk = nn(grads[...], q_all[...]).astype(BF16)
    flipped = m_ref[:, width : 2 * width].astype(F32).T.astype(BF16)
    pieces = []
    for h in range(count):
        pieces.append(nn(flipped[h * HEAD_DIM : (h + 1) * HEAD_DIM, :], grads[:, pl.ds(h * lanes, rows)]))
    dq = jnp.concatenate(pieces, axis=0).T if count > 1 else pieces[0].T
    dq = (dq.astype(BF16).astype(F32) * HEAD_DIM**-0.5).astype(BF16)
    for at, value in enumerate((dq, dk, dv)):
        d_ref[:, at * width : (at + 1) * width] = value
        sums_ref[:, at * width : (at + 1) * width] = jnp.sum(value.astype(F32), axis=0, keepdims=True)


def mix(length, g, at, normed, own, rest, bias, attended, weight, width):
    count, rows, model = normed.shape
    n_row = model // own.shape[1]
    wide = rest.shape[1]
    shape = jax.ShapeDtypeStruct
    more = [] if attended is None else [attended, weight]
    place = (lambda at: at[0] ^ g) if own.shape[2] > wide else (lambda at: 0)
    return scalar_call(
        functools.partial(mix_kernel, length, n_row),
        at,
        (count,),
        [
            pl.BlockSpec((None, rows, model), lambda i, at: (i, 0, 0)),
            pl.BlockSpec((3, own.shape[1], wide), lambda i, at: (0, 0, place(at))),
            pl.BlockSpec(rest.shape, lambda i, at: (0, 0)),
            pl.BlockSpec((None, 1, 3 * wide), lambda i, at: (place(at), 0, 0)),
        ]
        + [pl.BlockSpec(memory_space=pl.ANY)] * len(more),
        [
            pl.BlockSpec((None, rows, 3 * wide), lambda i, at: (i, 0, 0)),
            pl.BlockSpec((None, rows, wide), lambda i, at: (i, 0, place(at))),
            pl.BlockSpec((model, 3 * wide), lambda i, at: (0, g)),
            pl.BlockSpec((None, rows, wide), lambda i, at: (i, 0, 0)),
            pl.BlockSpec((None, 8, rows), lambda i, at: (i, 0, 0)),
        ],
        [
            shape((count, rows, 3 * wide), BF16),
            shape((count, rows, width), BF16),
            shape((model, 3 * width), BF16),
            shape((count, rows, wide), F32),
            shape((count, 8, rows), F32),
        ],
        "mix",
        2,
        scratch=[pltpu.VMEM((rows, 128), F32)],
        aliases={5: 1, 6: 2} if more else {},
    )(at, normed, own, rest, bias, *more)


def mix_back(length, g, groups, at, mixed, up, exact, stats, grads):
    count, rows, three = mixed.shape
    wide = three // 3
    lanes = -(-rows // 128) * 128 * (wide // HEAD_DIM)
    shape = jax.ShapeDtypeStruct
    place = (lambda at: at[0] ^ g) if groups > 1 else (lambda at: 0)
    more = [] if grads is None else [grads]
    return scalar_call(
        functools.partial(mix_back_kernel, length),
        at,
        (count,),
        [
            pl.BlockSpec((None, rows, three), lambda i, at: (i, 0, 0)),
            pl.BlockSpec((None, rows, wide), lambda i, at: (i, 0, place(at))),
            pl.BlockSpec((None, rows, wide), lambda i, at: (i, 0, 0)),
            pl.BlockSpec((None, 8, rows), lambda i, at: (i, 0, 0)),
        ]
        + [pl.BlockSpec(memory_space=pl.ANY)] * len(more),
        [
            pl.BlockSpec((None, rows, three), lambda i, at: (i, 0, g)),
            pl.BlockSpec((None, 1, three), lambda i, at: (i, 0, 0)),
        ],
        [shape((count, rows, groups * three), BF16), shape((count, 1, three), F32)],
        "mix_back",
        2,
        scratch=[
            pltpu.VMEM((rows, lanes), BF16),
            pltpu.VMEM((rows, lanes), BF16),
            pltpu.VMEM((lanes, wide), BF16),
            pltpu.VMEM((lanes, wide), BF16),
        ],
        aliases={5: 0} if more else {},
    )(at, stay(mixed), stay(up), stay(exact), stats, *more)


def up_kernel(n_row, at_ref, n_ref, own_ref, rest_ref, bias_ref, *refs):
    act_ref, slope_ref, weight_ref = refs[-3:]
    rows = n_ref.shape[0]
    near = own_ref.shape[0]

    @pl.when(pl.program_id(0) == 0)
    def _():
        for j in range(n_row):
            to = pl.ds(pl.multiple_of((at_ref[1] ^ j) * near, near), near)
            weight_ref[to, :] = own_ref[...] if j == 0 else rest_ref[j - 1]

    for start in range(0, rows, 256):
        at = pl.ds(start, min(256, rows - start))
        hidden = nn(n_ref[at, :], weight_ref[...]) + bias_ref[...]
        gate = 0.5 + 0.5 * jnp.tanh(0.851 * hidden)
        act = hidden * gate
        act_ref[at, :] = act.astype(BF16)
        slope_ref[at, :] = (gate + 1.702 * act * (1.0 - gate)).astype(BF16)


def up(p, at, normed, own, rest, bias, before):
    run = rest.shape[2]
    units = own.shape[1]
    count, rows, model = normed.shape
    shape = jax.ShapeDtypeStruct
    place = (lambda at: at[0] ^ p) if units > run else (lambda at: 0)
    block = pl.BlockSpec((None, rows, run), lambda i, at: (i, 0, place(at)))
    return scalar_call(
        functools.partial(up_kernel, model // own.shape[0]),
        at,
        (count,),
        [
            pl.BlockSpec((None, rows, model), lambda i, at: (i, 0, 0)),
            pl.BlockSpec((own.shape[0], run), lambda i, at: (0, place(at))),
            pl.BlockSpec(rest.shape, lambda i, at: (0, 0, 0)),
            pl.BlockSpec((1, run), lambda i, at: (0, place(at))),
        ]
        + [pl.BlockSpec(memory_space=pl.ANY)] * len(before),
        [block, block, pl.BlockSpec((model, run), lambda i, at: (0, place(at)))],
        [shape((count, rows, units), BF16)] * 2 + [shape((model, units), BF16)],
        "expand",
        1,
        limit=32,
        aliases={5: 0, 6: 1, 7: 2} if before else {},
    )(at, normed, own, rest, bias, *before)


def statistics(value):
    centered = value - jnp.mean(value, axis=-1, keepdims=True)
    inverse = lax.rsqrt(jnp.mean(centered * centered, axis=-1, keepdims=True) + 1e-05)
    return centered * inverse, inverse


def shards(
    images,
    cotangent,
    micro_batch,
    heads_weight,
    heads_bias,
    merge_weight,
    merge_bias,
    expand_weight,
    expand_bias,
    shrink_weight,
    shrink_bias,
    norm_gains,
    norm_shifts,
):
    n_dp, n_row = lax.axis_size("dp"), lax.axis_size("row")
    count, length, width = images.shape
    model = width * lax.axis_size("col")
    rows = -(-length // 16) * 16
    pad = ((0, 0), (0, rows - length), (0, 0))
    units = expand_weight.shape[1]
    run = width // n_dp
    split = run % HEAD_DIM == 0
    groups = n_dp if split else 1
    wide = width // groups
    at = jnp.stack([lax.axis_index(axis) for axis in ("dp", "row", "col")]).astype(jnp.int32)

    heads_own = jnp.transpose(heads_weight, (1, 0, 2))
    heads_send = own_part(heads_own, 2).reshape(-1, run)
    all_slots = count * n_dp * n_row
    assert all_slots <= 256 and run >= MICRO
    member = (micro_batch[:, None] == jnp.arange(run, dtype=jnp.int32)[None, :]).astype(F32)
    tail_own = jnp.broadcast_to(jnp.sum(member, axis=0), (16, run)).astype(BF16)
    heads_send = jnp.concatenate([heads_send, tail_own])
    heads_send, images, cotangent, norm_gains = lax.optimization_barrier(
        (heads_send, images, cotangent, norm_gains)
    )
    heads_rows = [peer(heads_send, "row", j) for j in range(1, n_row)]

    params = jnp.concatenate([norm_gains, norm_shifts, merge_bias[None], shrink_bias[None]], axis=0)
    params_tail = jnp.pad(params, ((0, rows - length - params.shape[0]), (0, 0)))
    x_own = jnp.concatenate([images, jnp.broadcast_to(params_tail, (count,) + params_tail.shape)], axis=1)
    cot_own = jnp.pad(cotangent, pad)
    pair = lax.axis_size("col") == 2
    if pair:
        x_other = peer(x_own, "col", 1)
        params = col_join(params, x_other[0, length : length + 6])
    else:
        x = col_full(x_own, 2)
        params = x[0, length : length + 6]
    gain_one, gain_two, shift_one, shift_two, merge_bias_full, _ = (
        params[k].astype(F32) for k in range(6)
    )
    if pair:
        x, normed = join(at, x_own, x_other, (gain_one[None], shift_one[None]))
    else:
        xhat, _ = statistics(x.astype(F32))
        normed = (xhat * gain_one + shift_one).astype(BF16)
    bias3 = jnp.stack([heads_bias[0], jnp.zeros_like(heads_bias[0]), heads_bias[1]]).astype(F32)
    bias3 = bias3.reshape(3, groups, wide).transpose(1, 0, 2).reshape(groups, 1, 3 * wide)

    heads_rows, normed, x, cot_own, expand_send, shrink_send = (
        lax.optimization_barrier(
            (
                heads_rows,
                normed,
                x,
                cot_own,
                own_part(expand_weight, 1),
                own_part(shrink_weight, 0),
            )
        )
    )
    heads_parts = dp_parts(stack(tail_own, heads_rows))
    lanes = merge_weight.shape[1]
    joined = expand_send.shape[1] % lanes == 0
    if joined:
        pieces = [expand_send[:, k : k + lanes] for k in range(0, expand_send.shape[1], lanes)]
        gathered = lax.all_gather(jnp.concatenate([merge_weight, *pieces]), "row")
    else:
        merge_full = lax.all_gather(merge_weight, "row", axis=1, tiled=True)
        expand_rows = lax.all_gather(expand_send, "row")
    shrink_rows = lax.all_gather(shrink_send, "row")
    totals = [piece[-1:, :MICRO].astype(F32) for piece in heads_parts]
    while len(totals) > 1:
        totals = [totals[k] + totals[k + 1] for k in range(0, len(totals), 2)]
    batch_weight = all_slots / (MICRO * totals[0])
    slot_weight = jnp.sum(member[:, :MICRO] * batch_weight, axis=1)
    if not split:
        heads_parts = [xor_order(lax.concatenate(heads_parts, 1), 1, "dp")]

    cot_other = peer(cot_own, "col", 1) if pair else None

    mixed, exact, stats = [None] * groups, [None] * groups, [None] * groups
    attended = heads_full = None
    for g in range(groups):
        mixed[g], attended, heads_full, exact[g], stats[g] = mix(
            length, g, at, normed, heads_own, heads_parts[g], bias3, attended, heads_full, width
        )

    if joined:
        attended, gathered = lax.optimization_barrier((attended, gathered))
        merge_full, expand_rows = unpack(at, gathered, width, expand_weight.shape[0])
        expand_rest = dp_parts(expand_rows)
    else:
        expand_rest = dp_parts(others(at, expand_rows)[0])
    shrink_rows = others(at, shrink_rows)
    attended, expand_rest[1:3], shrink_rows = lax.optimization_barrier(
        (attended, expand_rest[1:3], shrink_rows)
    )
    shrink_all = lax.all_to_all(shrink_rows, "dp", 0, 0)
    merge_part = jnp.einsum("itf,fd->itd", attended, merge_full, preferred_element_type=F32)
    share_a, share_b = col_shares(merge_part.astype(BF16))
    middle, normed_two = norm_of_sum(
        x, share_a, share_b, jnp.stack([merge_bias_full, gain_two, shift_two])
    )

    if (units // n_dp) % 128:
        expand_rest = [xor_order(lax.concatenate(expand_rest, 2), 2, "dp")]
    made = ()
    for p, piece in enumerate(expand_rest):
        made = up(p, at, normed_two, expand_weight, piece, expand_bias.astype(F32)[None], made)
    activated, slope, expand_full = made

    if pair:
        cot, seed_low, seed_sums = seed_of(at, cot_own, cot_other, slot_weight)
    else:
        cot = col_full(cot_own, 2)
        seed_low = (cot.astype(F32) * slot_weight[:, None, None]).astype(BF16)
        seed_sums = jnp.sum(seed_low.astype(F32), axis=1, keepdims=True)

    shrink_grad = jnp.einsum("ith,itd->hd", activated, seed_low, preferred_element_type=F32)
    shrink_grad = shrink_grad.astype(BF16)
    shrink_sum = scatter_row(shrink_grad, 1)
    shrink_grad, seed_low, shrink_all = lax.optimization_barrier((shrink_grad, seed_low, shrink_all))
    shrink_full = place(at, shrink_weight, shrink_all)
    act_grad = jnp.einsum("itd,hd->ith", seed_low, shrink_full, preferred_element_type=F32)
    hidden_grad = (act_grad * slope.astype(F32)).astype(BF16)
    hidden_sums = jnp.sum(hidden_grad.astype(F32), axis=(0, 1))
    expand_grad = jnp.einsum("ith,itd->hd", hidden_grad, normed_two, preferred_element_type=F32)
    expand_grad, hidden_grad, hidden_sums = lax.optimization_barrier(
        (expand_grad.astype(BF16), hidden_grad, hidden_sums)
    )
    expand_sum = dp_sum(expand_grad)
    norm_part = jnp.einsum("ith,dh->itd", hidden_grad, expand_full, preferred_element_type=F32)
    norm_part = norm_part.astype(BF16)
    share_a, share_b = col_shares(norm_part)
    middle_grad, branch_grad, sums_two = norm_back(
        at, cot, middle, share_a, share_b, gain_two, slot_weight, None
    )

    attended_grad = jnp.einsum(
        "itd,fd->itf", branch_grad, merge_full, preferred_element_type=F32
    ).astype(BF16)
    merge_grad = jnp.einsum("itf,itd->fd", attended, branch_grad, preferred_element_type=F32)
    merge_grad, attended_grad = lax.optimization_barrier((merge_grad.astype(BF16), attended_grad))
    mixed_grad, mixed_sums, heads_grads = None, [None] * groups, [None] * groups
    merge_sum, heads_in = scatter_row(merge_grad, 1), [None] * groups
    part = units // n_dp
    order = list(range(1, groups)) + [0]
    for turn, g in enumerate(order):
        if turn == max(groups - 2, 0):
            attended_grad, expand_sum, shrink_sum = lax.optimization_barrier(
                (attended_grad, expand_sum, shrink_sum)
            )
            expand_sum = scatter_row(expand_sum, 1)
        if g == 0:
            attended_grad, merge_sum, heads_in[1:2] = lax.optimization_barrier(
                (attended_grad, merge_sum, heads_in[1:2])
            )
            both = jnp.concatenate(
                [shrink_sum.reshape(n_dp, part, -1), merge_sum.reshape(n_dp, run, -1)], axis=1
            )
            both = dp_sum(both.reshape(units + width, -1))
        mixed_grad, mixed_sums[g] = mix_back(
            length, g, groups, at, mixed[g], attended_grad, exact[g], stats[g], mixed_grad
        )
        piece = mixed_grad[:, :, g * 3 * wide : (g + 1) * 3 * wide]
        heads_grads[g] = jnp.einsum("itd,itf->df", normed, piece, preferred_element_type=F32).astype(BF16)
        if g:
            attended_grad, heads_grads[g] = lax.optimization_barrier((attended_grad, heads_grads[g]))
            heads_in[g] = peer(heads_grads[g], "dp", g)
    if not split:
        whole = xor_order(heads_grads[0].reshape(model, 3, width), 2, "dp")
        heads_grads = [cut(whole, 2, n_dp, p).reshape(model, 3 * run) for p in range(n_dp)]
        heads_in = [None] + [peer(heads_grads[p], "dp", p) for p in range(1, n_dp)]
    heads_sum = heads_grads[0].astype(F32)
    for piece in heads_in[1:]:
        heads_sum = heads_sum + piece.astype(F32)
    heads_sum = heads_sum.astype(BF16)
    heads_sum = sum_parts([cut(heads_sum, 0, n_row, j) for j in range(n_row)], "row", at[1])
    mixed_grad, activated, both, expand_sum = lax.optimization_barrier(
        (mixed_grad, activated, both, expand_sum)
    )
    first_part = jnp.einsum("itf,df->itd", mixed_grad, heads_full, preferred_element_type=F32)
    share_a, share_b = col_shares(first_part.astype(BF16))
    packed = dp_all(jnp.concatenate([both, expand_sum]))
    shrink_part = jnp.einsum("ith,hd->itd", activated, shrink_full, preferred_element_type=F32).astype(BF16)
    shrink_part, heads_sum = lax.optimization_barrier((shrink_part, heads_sum))
    own = (length, width) if pair else (rows, model)
    place_of = at if pair else at * jnp.array([1, 1, 0], jnp.int32)
    input_grad, sums_one = norm_back(
        place_of, middle_grad, x, share_a, share_b, gain_one, slot_weight, own
    )

    if pair:
        other = peer(half(at, shrink_part, False), "col", 1)
        output = close(at, middle, shrink_part, other, shrink_bias.astype(F32)[None], length)
    else:
        branch_two = col_own(lax.psum(shrink_part, "col").astype(F32), 2)
        output = (col_own(middle, 2) + (branch_two + shrink_bias.astype(F32))).astype(BF16)[:, :length]
        input_grad = col_own(input_grad, 2)[:, :length]
    packed, sums_one = lax.optimization_barrier((packed, sums_one))
    heads_out = dp_parts(heads_sum)
    heads_out, packed, sums_one = lax.optimization_barrier((heads_out, packed, sums_one))

    sums_one, sums_two = jnp.sum(sums_one, axis=0), jnp.sum(sums_two, axis=0)
    model_sums = jnp.stack(
        [sums_one[0], sums_two[0], sums_one[1], sums_two[1], sums_two[2], jnp.sum(seed_sums, axis=(0, 1))]
    )
    model_sums = col_own(model_sums, 1)
    mixed_sums = jnp.sum(jnp.concatenate(mixed_sums, axis=1), axis=0)
    mixed_sums = mixed_sums.reshape(groups, 3, wide).transpose(1, 0, 2).reshape(3, width)
    heads_bias_grad = mixed_sums[0::2]
    if split:
        heads_bias_grad = xor_order(heads_bias_grad, 1, "dp")
    small = sum_all(jnp.concatenate([model_sums.ravel(), heads_bias_grad.ravel(), hidden_sums]))
    shrink_sum = packed[:, :part].reshape(units, -1).astype(F32)
    merge_sum = packed[:, part : part + run].reshape(width, -1).astype(F32)
    expand_sum = packed[:, part + run :].reshape(units, -1).T.astype(F32)
    if run % 128:
        heads_sum = [piece.reshape(-1, 3, run) for piece in heads_out]
        heads_sum = xor_order(jnp.concatenate(heads_sum, axis=2), 2, "dp").astype(F32)
    else:
        heads_sum = jnp.transpose(spread(at, heads_out), (1, 0, 2))

    model_sums = small[: 6 * width].reshape(6, width)
    return (
        output,
        input_grad,
        heads_sum,
        small[6 * width : 8 * width].reshape(2, width),
        merge_sum,
        model_sums[4],
        expand_sum,
        small[8 * width :],
        shrink_sum,
        model_sums[5],
        model_sums[0:2],
        model_sums[2:4],
    )


def solution(mesh):
    placed = (
        P(("dp", "row"), None, "col"),
        P(("dp", "row"), None, "col"),
        P(("dp", "row")),
        P("row", None, "col"),
        P(None, "col"),
        P("col", "row"),
        P("col"),
        P("row", "col"),
        P("col"),
        P("col", "row"),
        P("col"),
        P(None, "col"),
        P(None, "col"),
    )
    return jax.shard_map(
        shards,
        mesh=mesh,
        in_specs=placed,
        out_specs=(
            P(("dp", "row"), None, "col"),
            P(("dp", "row"), None, "col"),
            P("row", None, "col"),
            P(None, "col"),
            P("col", "row"),
            P("col"),
            P("row", "col"),
            P("col"),
            P("col", "row"),
            P("col"),
            P(None, "col"),
            P(None, "col"),
        ),
        check_vma=False,
    )
```

```python
import functools

import jax
import jax.numpy as jnp
from jax import lax
from jax.experimental import pallas as pl
from jax.experimental.pallas import tpu as pltpu
from jax.sharding import PartitionSpec as P

HEAD_DIM = 64
MICRO = 2
BF16 = jnp.bfloat16
F32 = jnp.float32
VMEM_LIMIT = 58 << 20
STEP = 304
KEYS = 304


def peer(value, axis, p):
    n = lax.axis_size(axis)
    return lax.ppermute(value, axis, [(i, i ^ p) for i in range(n)])


def xor_order(value, dim, axis):
    n = lax.axis_size(axis)
    index = lax.axis_index(axis)
    size = value.shape[dim]
    bit = 1
    while bit < n:
        run = size * bit // n
        pieces = [lax.slice_in_dim(value, at, at + run, axis=dim) for at in range(0, size, run)]
        swapped = lax.concatenate([pieces[k ^ 1] for k in range(len(pieces))], dim)
        value = jnp.where((index & bit) != 0, swapped, value)
        bit *= 2
    return value


def cut(value, dim, n, k):
    run = value.shape[dim] // n
    return lax.slice_in_dim(value, k * run, (k + 1) * run, axis=dim)


def own_part(own, inner_dim):
    run = own.shape[inner_dim] // lax.axis_size("dp")
    return lax.dynamic_slice_in_dim(own, lax.axis_index("dp") * run, run, inner_dim)


def dp_parts(part):
    return [part] + [peer(part, "dp", p) for p in range(1, lax.axis_size("dp"))]


def sum_parts(parts, axis, start=None):
    n = lax.axis_size(axis)
    if start is not None:
        stacked = jnp.stack(parts)
        parts = [lax.dynamic_index_in_dim(stacked, start ^ p, 0, keepdims=False) for p in range(n)]
    total = parts[0].astype(F32)
    for p in range(1, n):
        total = total + peer(parts[p], axis, p).astype(F32)
    return total.astype(BF16)


def dp_sum(blocks):
    n = lax.axis_size("dp")
    blocks = blocks.reshape((n, blocks.shape[0] // n) + blocks.shape[1:])
    return add(lax.all_to_all(blocks, "dp", 0, 0))


def dp_all(part):
    n = lax.axis_size("dp")
    return lax.all_to_all(jnp.broadcast_to(part[None], (n,) + part.shape), "dp", 0, 0)


def scatter_row(value, model_dim):
    return lax.psum_scatter(value, "row", scatter_dimension=model_dim, tiled=True)


def sum_all(value):
    for axis in ("dp", "row"):
        terms = dp_parts(value) if axis == "dp" else [value] + [peer(value, "row", j) for j in range(1, lax.axis_size("row"))]
        while len(terms) > 1:
            terms = [terms[k] + terms[k + 1] for k in range(0, len(terms), 2)]
        value = terms[0]
    return value


def col_join(own, other):
    first = lax.axis_index("col") == 0
    return lax.concatenate([jnp.where(first, own, other), jnp.where(first, other, own)], own.ndim - 1)


def col_full(own, feature_dim):
    return lax.all_gather(own, "col", axis=feature_dim, tiled=True)


def col_own(full, feature_dim):
    n_col = lax.axis_size("col")
    if n_col == 2:
        return jnp.where(
            lax.axis_index("col") == 0, cut(full, feature_dim, 2, 0), cut(full, feature_dim, 2, 1)
        )
    width = full.shape[feature_dim] // n_col
    return lax.dynamic_slice_in_dim(full, lax.axis_index("col") * width, width, feature_dim)


def col_shares(part):
    if lax.axis_size("col") == 2:
        return part, peer(part, "col", 1)
    return lax.psum(part, "col"), jnp.zeros_like(part)


def nt(a, b):
    return lax.dot_general(a, b, (((1,), (1,)), ((), ())), preferred_element_type=F32)


def nn(a, b):
    return lax.dot_general(a, b, (((1,), (0,)), ((), ())), preferred_element_type=F32)


def cost(us, moved=1 << 20):
    return pl.CostEstimate(flops=int(us * 1.0e9), bytes_accessed=1024, transcendentals=0)


def scalar_call(body, at, grid, in_specs, out_specs, out_shape, name, us, scratch=(), limit=24, aliases=None):
    far = lambda a: pltpu.HBM(a.shape, a.dtype)
    out_shape = [far(a) for a in out_shape] if isinstance(out_shape, list) else far(out_shape)
    return pl.pallas_call(
        body,
        grid_spec=pltpu.PrefetchScalarGridSpec(
            num_scalar_prefetch=1,
            grid=grid,
            in_specs=in_specs,
            out_specs=out_specs,
            scratch_shapes=list(scratch),
        ),
        out_shape=out_shape,
        input_output_aliases=aliases or {},
        compiler_params=pltpu.CompilerParams(vmem_limit_bytes=limit << 20),
        cost_estimate=cost(us),
        name=name,
    )


def row_chunks(rows, body):
    for start in range(0, rows, STEP):
        body(pl.ds(start, min(STEP, rows - start)))


def spread_of(value):
    centered = value - jnp.mean(value, axis=1, keepdims=True)
    inverse = lax.rsqrt(jnp.mean(centered * centered, axis=1, keepdims=True) + 1e-05)
    return centered * inverse, inverse


def norm_kernel(x_ref, a_ref, b_ref, params_ref, middle_ref, normed_ref):
    def body(at):
        value = a_ref[at, :].astype(F32) + b_ref[at, :].astype(F32)
        value = x_ref[at, :].astype(F32) + (value + params_ref[0:1, :])
        middle_ref[at, :] = value.astype(BF16)
        xhat, _ = spread_of(value)
        normed_ref[at, :] = (xhat * params_ref[1:2, :] + params_ref[2:3, :]).astype(BF16)

    row_chunks(x_ref.shape[0], body)


def norm_of_sum(x, share_a, share_b, params):
    count, rows, model = x.shape
    image = pl.BlockSpec((None, rows, model), lambda i: (i, 0, 0))
    return pl.pallas_call(
        norm_kernel,
        grid=(count,),
        in_specs=[image] * 3 + [pl.BlockSpec(params.shape, lambda i: (0, 0))],
        out_specs=[image] * 2,
        out_shape=[pltpu.HBM(x.shape, BF16)] * 2,
        compiler_params=pltpu.CompilerParams(vmem_limit_bytes=32 << 20),
        cost_estimate=cost(0.01),
        name="norm_two",
    )(x, share_a, share_b, params)


def norm_back_kernel(second, at_ref, base_ref, v_ref, a_ref, b_ref, gain_ref, weight_ref, *refs):
    grad_ref, sums_ref, scratch = refs
    rows = v_ref.shape[0]
    totals = None

    def body(at):
        nonlocal totals
        xhat, inverse = spread_of(v_ref[at, :].astype(F32))
        upstream = a_ref[at, :].astype(F32) + b_ref[at, :].astype(F32)
        scaled = upstream * gain_ref[...]
        first = jnp.mean(scaled, axis=1, keepdims=True)
        other = jnp.mean(scaled * xhat, axis=1, keepdims=True)
        base = base_ref[at, :].astype(F32)
        if second:
            base = base * weight_ref[pl.program_id(0)]
        grad = base + inverse * (scaled - first - xhat * other)
        parts = [jnp.sum(upstream * xhat, axis=0, keepdims=True), jnp.sum(upstream, axis=0, keepdims=True)]
        if second:
            low = grad.astype(BF16)
            grad_ref[at, :] = low
            parts.append(jnp.sum(low.astype(F32), axis=0, keepdims=True))
        else:
            scratch[at, :] = grad
        totals = parts if totals is None else [x + y for x, y in zip(totals, parts)]

    row_chunks(rows, body)
    for k, total in enumerate(totals):
        sums_ref[k : k + 1, :] = total
    if not second:
        length, width = grad_ref.shape
        grad_ref[...] = scratch[:length, pl.ds(pl.multiple_of(at_ref[2] * width, width), width)]


def norm_back(at, base, v, share_a, share_b, gain, weight, own):
    count, rows, model = v.shape
    second = own is None
    shape = jax.ShapeDtypeStruct
    image = pl.BlockSpec((None, rows, model), lambda i, at: (i, 0, 0))
    sums = 3 if second else 2
    outs = [image] if second else [pl.BlockSpec((None,) + own, lambda i, at: (i, 0, 0))]
    shapes = [shape(v.shape, BF16)] if second else [shape((count,) + own, F32)]
    return scalar_call(
        functools.partial(norm_back_kernel, second),
        at,
        (count,),
        [image] * 4
        + [pl.BlockSpec((1, model), lambda i, at: (0, 0)), pl.BlockSpec(memory_space=pltpu.SMEM)],
        outs + [pl.BlockSpec((None, sums, model), lambda i, at: (i, 0, 0))],
        shapes + [shape((count, sums, model), F32)],
        "norm_back",
        0.01,
        scratch=[pltpu.VMEM((8, 128) if second else (rows, model), F32)],
        limit=48,
    )(at, base, v, share_a, share_b, gain[None], weight)


def join_kernel(normal, at_ref, own_ref, other_ref, *refs):
    out_ref = refs[2] if normal else refs[0]
    rows, width = own_ref.shape
    to = pl.ds(pl.multiple_of(at_ref[2] * width, width), width)
    away = pl.ds(pl.multiple_of((1 - at_ref[2]) * width, width), width)
    out_ref[:, to] = own_ref[...]
    out_ref[:, away] = other_ref[...]
    if not normal:
        return
    gain_ref, shift_ref, _, normed_ref = refs

    def body(at):
        value = out_ref[at, :].astype(F32)
        centered = value - jnp.mean(value, axis=1, keepdims=True)
        inverse = lax.rsqrt(jnp.mean(centered * centered, axis=1, keepdims=True) + 1e-05)
        normed_ref[at, :] = (centered * inverse * gain_ref[...] + shift_ref[...]).astype(BF16)

    row_chunks(rows, body)


def join(at, own, other, vectors=None):
    count, rows, width = own.shape
    normal = vectors is not None
    shape = jax.ShapeDtypeStruct((count, rows, 2 * width), BF16)
    half = pl.BlockSpec((None, rows, width), lambda i, at: (i, 0, 0))
    full = pl.BlockSpec((None, rows, 2 * width), lambda i, at: (i, 0, 0))
    vector = pl.BlockSpec((1, 2 * width), lambda i, at: (0, 0))
    return scalar_call(
        functools.partial(join_kernel, normal),
        at,
        (count,),
        [half, half] + [vector] * (2 if normal else 0),
        [full, full] if normal else full,
        [shape, shape] if normal else shape,
        "join",
        0.01,
    )(at, own, other, *(vectors or ()))


def seed_kernel(at_ref, own_ref, other_ref, weight_ref, cot_ref, seed_ref, sums_ref, sums):
    rows, width = own_ref.shape
    scale = weight_ref[pl.program_id(0)]
    sums[...] = jnp.zeros_like(sums)
    for k, ref in enumerate((own_ref, other_ref)):
        place = at_ref[2] if k == 0 else 1 - at_ref[2]
        to = pl.ds(pl.multiple_of(place * width, width), width)

        def body(at):
            value = ref[at, :]
            low = (value.astype(F32) * scale).astype(BF16)
            cot_ref[at, to] = value
            seed_ref[at, to] = low
            low = low.astype(F32)
            sums[:, to] += jnp.sum(low.reshape(low.shape[0] // 8, 8, width), axis=0)

        row_chunks(rows, body)
    sums_ref[...] = jnp.sum(sums[...], axis=0, keepdims=True)


def seed_of(at, own, other, weight):
    count, rows, width = own.shape
    shape = jax.ShapeDtypeStruct
    half = pl.BlockSpec((None, rows, width), lambda i, at: (i, 0, 0))
    full = pl.BlockSpec((None, rows, 2 * width), lambda i, at: (i, 0, 0))
    return scalar_call(
        seed_kernel,
        at,
        (count,),
        [half, half, pl.BlockSpec(memory_space=pltpu.SMEM)],
        [full, full, pl.BlockSpec((None, 1, 2 * width), lambda i, at: (i, 0, 0))],
        [shape((count, rows, 2 * width), BF16)] * 2 + [shape((count, 1, 2 * width), F32)],
        "seed",
        0.01,
        scratch=[pltpu.VMEM((8, 2 * width), F32)],
    )(at, own, other, weight)


def stay(value):
    return pltpu.with_memory_space_constraint(value, pltpu.HBM)


def stack_kernel(body_rows, own_ref, *refs):
    out_ref = refs[-1]
    total = own_ref[...].astype(F32)
    for k, ref in enumerate(refs[:-1]):
        out_ref[k * body_rows : (k + 1) * body_rows, :] = ref[:body_rows, :]
        total = total + ref[body_rows:, :].astype(F32)
    out_ref[(len(refs) - 1) * body_rows :, :] = total.astype(BF16)


def stack(own_tail, arrays):
    vmem = pl.BlockSpec(memory_space=pltpu.VMEM)
    more, lanes = own_tail.shape
    body = arrays[0].shape[0] - more
    return pl.pallas_call(
        functools.partial(stack_kernel, body),
        in_specs=[vmem] * (1 + len(arrays)),
        out_specs=vmem,
        out_shape=jax.ShapeDtypeStruct((len(arrays) * body + more, lanes), BF16),
        compiler_params=pltpu.CompilerParams(vmem_limit_bytes=16 << 20),
        cost_estimate=cost(0.01),
        name="stack",
    )(own_tail, *arrays)


def unpack_kernel(rows, at_ref, in_ref, out_ref):
    run = in_ref.shape[1]
    near = out_ref.shape[0]
    for k in range(out_ref.shape[1] // run):
        out_ref[:, k * run : (k + 1) * run] = in_ref[rows + k * near : rows + (k + 1) * near, :]


def unpack(at, gathered, rows, near):
    n_row, total, run = gathered.shape
    wide = (total - rows) // near * run
    return scalar_call(
        functools.partial(unpack_kernel, rows),
        at,
        (n_row - 1,),
        [pl.BlockSpec((None, total, run), lambda j, at: (at[1] ^ (j + 1), 0, 0))],
        pl.BlockSpec((None, near, wide), lambda j, at: (j, 0, 0)),
        jax.ShapeDtypeStruct((n_row - 1, near, wide), BF16),
        "unpack",
        0.01,
    )(at, stay(gathered))


def merge_kernel(at_ref, a_ref, g_ref, out_ref, weight_ref):
    n_row, _, near = g_ref.shape

    @pl.when(pl.program_id(0) == 0)
    def _():
        for z in range(n_row):
            weight_ref[:, z * near : (z + 1) * near] = g_ref[z]

    out_ref[...] = nn(a_ref[...], weight_ref[...]).astype(BF16)


def merge(at, attended, gathered):
    count, rows, width = attended.shape
    n_row, _, near = gathered.shape
    shape = jax.ShapeDtypeStruct
    return scalar_call(
        merge_kernel,
        at,
        (count,),
        [
            pl.BlockSpec((None, rows, width), lambda i, at: (i, 0, 0)),
            pl.BlockSpec((n_row, width, near), lambda i, at: (0, 0, 0), pipeline_mode=pl.Buffered(1)),
        ],
        [
            pl.BlockSpec((None, rows, n_row * near), lambda i, at: (i, 0, 0)),
            pl.BlockSpec((width, n_row * near), lambda i, at: (0, 0)),
        ],
        [shape((count, rows, n_row * near), BF16), shape((width, n_row * near), BF16)],
        "merge",
        0.01,
    )(at, attended, stay(gathered))


def product_kernel(a_ref, b_ref, out_ref):
    total = None
    for i in range(a_ref.shape[0]):
        part = lax.dot_general(a_ref[i], b_ref[i], (((0,), (0,)), ((), ())), preferred_element_type=F32)
        total = part if total is None else total + part
    out_ref[...] = total.astype(BF16)


def product(a, b, run, lanes=None, block=0, us=0.01):
    count, rows, units = a.shape
    lanes = b.shape[2] if lanes is None else lanes
    run = run if run % 128 == 0 else units
    return pl.pallas_call(
        product_kernel,
        grid=(units // run,),
        in_specs=[
            pl.BlockSpec((count, rows, run), lambda q: (0, 0, q)),
            pl.BlockSpec((count, rows, lanes), lambda q: (0, 0, block), pipeline_mode=pl.Buffered(1)),
        ],
        out_specs=pl.BlockSpec((run, lanes), lambda q: (q, 0)),
        out_shape=pltpu.HBM((units, lanes), BF16),
        compiler_params=pltpu.CompilerParams(vmem_limit_bytes=40 << 20),
        cost_estimate=cost(us),
        name="product",
    )(stay(a), stay(b))


def pick_kernel(at_ref, in_ref, out_ref):
    out_ref[...] = in_ref[...]


def others(at, gathered):
    n_row = gathered.shape[0]
    block = (None,) + gathered.shape[1:]
    return scalar_call(
        pick_kernel,
        at,
        (n_row - 1,),
        [pl.BlockSpec(block, lambda j, at: (at[1] ^ (j + 1), 0, 0))],
        pl.BlockSpec(block, lambda j, at: (j, 0, 0)),
        jax.ShapeDtypeStruct((n_row - 1,) + gathered.shape[1:], gathered.dtype),
        "others",
        0.01,
    )(at, stay(gathered))


def down_back_kernel(n_dp, at_ref, seed_ref, slope_ref, own_ref, *refs):
    rest, (grad_ref, sums_ref, weight_ref) = refs[:n_dp], refs[n_dp:]
    others, _, near = rest[0].shape
    for p in range(n_dp):

        @pl.when(pl.program_id(0) == p)
        def _(p=p):
            for j in range(others + 1):
                to = pl.ds(pl.multiple_of((at_ref[1] ^ j) * near, near), near)
                weight_ref[:, to] = rest[p][j - 1] if j else own_ref[...]

    sums = None
    for i in range(seed_ref.shape[0]):
        grad = (nt(seed_ref[i], weight_ref[...]) * slope_ref[i].astype(F32)).astype(BF16)
        grad_ref[i] = grad
        part = jnp.sum(grad.astype(F32), axis=0, keepdims=True)
        sums = part if sums is None else sums + part
    sums_ref[...] = sums


def down_back(at, seed, slope, own, rest):
    if rest[0].shape[1] % 128:
        rest = [xor_order(lax.concatenate(rest, 1), 1, "dp")]
    n_dp = len(rest)
    others, run, near = rest[0].shape
    count, rows, model = seed.shape
    units = own.shape[0]
    shape = jax.ShapeDtypeStruct
    place = (lambda at, p: at[0] ^ p) if n_dp > 1 else (lambda at, p: 0)
    block = pl.BlockSpec((count, rows, run), lambda p, at: (0, 0, place(at, p)))
    return scalar_call(
        functools.partial(down_back_kernel, n_dp),
        at,
        (n_dp,),
        [
            pl.BlockSpec(seed.shape, lambda p, at: (0, 0, 0), pipeline_mode=pl.Buffered(1)),
            block,
            pl.BlockSpec((run, near), lambda p, at: (place(at, p), 0)),
        ]
        + [pl.BlockSpec(a.shape, lambda p, at: (0, 0, 0), pipeline_mode=pl.Buffered(1)) for a in rest],
        [
            block,
            pl.BlockSpec((1, run), lambda p, at: (0, place(at, p))),
            pl.BlockSpec((run, model), lambda p, at: (place(at, p), 0)),
        ],
        [shape((count, rows, units), BF16), shape((1, units), F32), shape((units, model), BF16)],
        "down_back",
        0.01,
        limit=40,
    )(at, stay(seed), stay(slope), own, *[stay(a) for a in rest])


def add_kernel(in_ref, out_ref):
    out_ref[...] = jnp.sum(in_ref[...].astype(F32), axis=0).astype(BF16)


def add(blocks):
    n, rows, lanes = blocks.shape
    step = rows // 4 if rows % 64 == 0 else rows
    return pl.pallas_call(
        add_kernel,
        grid=(rows // step,),
        in_specs=[pl.BlockSpec((n, step, lanes), lambda i: (0, i, 0))],
        out_specs=pl.BlockSpec((step, lanes), lambda i: (i, 0)),
        out_shape=jax.ShapeDtypeStruct((rows, lanes), BF16),
        compiler_params=pltpu.CompilerParams(vmem_limit_bytes=24 << 20),
        cost_estimate=cost(0.01),
        name="add",
    )(blocks)


def half_kernel(at_ref, in_ref, out_ref):
    out_ref[...] = in_ref[...]


def half(at, value, own):
    count, rows, model = value.shape
    place = (lambda at: at[2]) if own else (lambda at: 1 - at[2])
    return scalar_call(
        half_kernel,
        at,
        (count,),
        [pl.BlockSpec((None, rows, model // 2), lambda i, at: (i, 0, place(at)))],
        pl.BlockSpec((None, rows, model // 2), lambda i, at: (i, 0, 0)),
        jax.ShapeDtypeStruct((count, rows, model // 2), value.dtype),
        "half",
        0.01,
    )(at, value)


def close_kernel(at_ref, m_ref, a_ref, b_ref, bias_ref, out_ref):
    def body(at):
        share = a_ref[at, :].astype(F32) + b_ref[at, :].astype(F32)
        out_ref[at, :] = (m_ref[at, :].astype(F32) + (share + bias_ref[...])).astype(BF16)

    row_chunks(out_ref.shape[0], body)


def close(at, middle, part, other, bias, length):
    count, rows, width = other.shape
    mine = pl.BlockSpec((None, rows, width), lambda i, at: (i, 0, at[2]))
    plain = pl.BlockSpec((None, rows, width), lambda i, at: (i, 0, 0))
    return scalar_call(
        close_kernel,
        at,
        (count,),
        [mine, mine, plain, pl.BlockSpec((1, width), lambda i, at: (0, 0))],
        pl.BlockSpec((None, length, width), lambda i, at: (i, 0, 0)),
        jax.ShapeDtypeStruct((count, length, width), BF16),
        "close",
        0.01,
    )(at, middle, part, other, bias)


def spread_kernel(n_dp, at_ref, *refs):
    out_ref = refs[-1]
    run = out_ref.shape[2] // n_dp
    for p in range(n_dp):
        to = pl.ds(pl.multiple_of((at_ref[0] ^ p) * run, run), run)
        for k in range(3):
            out_ref[k, :, to] = refs[p][:, k * run : (k + 1) * run].astype(F32)


def spread(at, parts):
    n_dp = len(parts)
    rows, three = parts[0].shape
    run = three // 3
    vmem = pl.BlockSpec((rows, three), lambda i, at: (0, 0))
    return scalar_call(
        functools.partial(spread_kernel, n_dp),
        at,
        (1,),
        [vmem] * n_dp,
        pl.BlockSpec((3, rows, n_dp * run), lambda i, at: (0, 0, 0)),
        jax.ShapeDtypeStruct((3, rows, n_dp * run), F32),
        "spread",
        0.01,
    )(at, *parts)


def head_mask(rows, width, h):
    lane = lax.broadcasted_iota(jnp.int32, (rows, width), 1)
    return (lane >= h * HEAD_DIM) & (lane < (h + 1) * HEAD_DIM)


def mix_kernel(length, n_row, at_ref, n_ref, own_ref, rest_ref, bias_ref, *refs):
    mixed_ref, o_ref, weight_ref, exact_ref, stats_ref, lanes_ref = refs[-6:]
    rows = n_ref.shape[0]
    width = o_ref.shape[1]
    count = width // HEAD_DIM
    near = own_ref.shape[1]
    chunk = rows

    @pl.when(pl.program_id(0) == 0)
    def _():
        for j in range(n_row):
            to = pl.ds(pl.multiple_of((at_ref[1] ^ j) * near, near), near)
            for k in range(3):
                start = ((j - 1) * 3 + k) * near
                piece = own_ref[k] if j == 0 else rest_ref[start : start + near, :]
                weight_ref[to, k * width : (k + 1) * width] = piece

    for start in range(0, rows, chunk):
        size = min(chunk, rows - start)
        at = pl.ds(start, size)
        mixed = nn(n_ref[at, :], weight_ref[...]) + bias_ref[...]
        mixed_ref[at, :width] = (mixed[:, :width] * HEAD_DIM**-0.5).astype(BF16)
        mixed_ref[at, width:] = mixed[:, width:].astype(BF16)
    plain = length // 128 * 128
    k = mixed_ref[:, width : 2 * width]
    v = mixed_ref[:, 2 * width :]
    for start in range(0, rows, chunk):
        size = min(chunk, rows - start)
        at = pl.ds(start, size)
        q = mixed_ref[at, :width]
        result, stats = None, jnp.zeros((size, 128), F32)
        place = lax.broadcasted_iota(jnp.int32, (size, 128), 1)
        for h in range(count):
            mask = head_mask(size, width, h)
            query = jnp.where(mask, q, jnp.zeros_like(q))
            near, far = nt(query, k[:plain]), nt(query, k[plain:])
            key = lax.broadcasted_iota(jnp.int32, far.shape, 1) + plain
            far = jnp.where(key < length, far, -1e30)
            top = jnp.maximum(jnp.max(near, axis=1, keepdims=True), jnp.max(far, axis=1, keepdims=True))
            near, far = jnp.exp(near - top), jnp.exp(far - top)
            total = jnp.sum(near, axis=1, keepdims=True) + jnp.sum(far, axis=1, keepdims=True)
            out = (nn(near.astype(BF16), v[:plain]) + nn(far.astype(BF16), v[plain:])) / total
            result = out if result is None else jnp.where(mask, out, result)
            stats = jnp.where(place == h, top + jnp.log(total), stats)
        o_ref[at, :] = result.astype(BF16)
        exact_ref[at, :] = result
        lanes_ref[at, :] = stats
    row = lax.broadcasted_iota(jnp.int32, (8, 128), 0)
    lane = lax.broadcasted_iota(jnp.int32, (8, 128), 1)
    stats_ref[...] = turned(jnp.where(row == lane, 1.0, 0.0), lanes_ref[...])


def turned(select, value):
    return lax.dot_general(
        select, value, (((1,), (1,)), ((), ())), precision=lax.Precision.HIGHEST, preferred_element_type=F32
    )


def mix_back_kernel(length, at_ref, m_ref, up_ref, exact_ref, stats_ref, *refs):
    d_ref, sums_ref, probs, grads, q_all, up_all = refs[-6:]
    rows, width = up_ref.shape
    count = width // HEAD_DIM
    lanes = probs.shape[1] // count
    chunk = 256
    row = lax.broadcasted_iota(jnp.int32, (8, width), 0)
    lane = lax.broadcasted_iota(jnp.int32, (8, width), 1)
    select = jnp.where((lane >= row * HEAD_DIM) & (lane < (row + 1) * HEAD_DIM), 1.0, 0.0)
    delta = turned(select, up_ref[...].astype(F32) * exact_ref[...])
    for h in range(count):
        base = h * lanes
        if rows < lanes:
            probs[:, pl.ds(base + rows, lanes - rows)] = jnp.zeros((rows, lanes - rows), BF16)
            grads[:, pl.ds(base + rows, lanes - rows)] = jnp.zeros((rows, lanes - rows), BF16)
            q_all[pl.ds(base + rows, lanes - rows), :] = jnp.zeros((lanes - rows, width), BF16)
            up_all[pl.ds(base + rows, lanes - rows), :] = jnp.zeros((lanes - rows, width), BF16)
        for start in range(0, rows, chunk):
            size = min(chunk, rows - start)
            mask = head_mask(size, width, h)
            q = m_ref[pl.ds(start, size), :width]
            up = up_ref[pl.ds(start, size), :]
            q = jnp.where(mask, q, jnp.zeros_like(q))
            up = jnp.where(mask, up, jnp.zeros_like(up))
            q_all[pl.ds(base + start, size), :] = q
            up_all[pl.ds(base + start, size), :] = up
            total = stats_ref[h : h + 1, start : start + size]
            mean = delta[h : h + 1, start : start + size]
            for first in range(0, rows, KEYS):
                keys = pl.ds(first, min(KEYS, rows - first))
                share = jnp.exp(nt(m_ref[keys, width : 2 * width], q) - total)
                if first + KEYS > length:
                    key = lax.broadcasted_iota(jnp.int32, share.shape, 0) + first
                    share = jnp.where(key < length, share, 0.0)
                prob_grad = nt(m_ref[keys, 2 * width :], up)
                probs[keys, pl.ds(base + start, size)] = share.astype(BF16)
                grads[keys, pl.ds(base + start, size)] = (share * (prob_grad - mean)).astype(BF16)
    dv = nn(probs[...], up_all[...]).astype(BF16)
    dk = nn(grads[...], q_all[...]).astype(BF16)
    flipped = m_ref[:, width : 2 * width].astype(F32).T.astype(BF16)
    pieces = []
    for h in range(count):
        pieces.append(nn(flipped[h * HEAD_DIM : (h + 1) * HEAD_DIM, :], grads[:, pl.ds(h * lanes, rows)]))
    dq = jnp.concatenate(pieces, axis=0).T if count > 1 else pieces[0].T
    dq = (dq.astype(BF16).astype(F32) * HEAD_DIM**-0.5).astype(BF16)
    for at, value in enumerate((dq, dk, dv)):
        d_ref[:, at * width : (at + 1) * width] = value
        sums_ref[:, at * width : (at + 1) * width] = jnp.sum(value.astype(F32), axis=0, keepdims=True)


def mix(length, g, at, normed, own, rest, bias, attended, weight, width):
    count, rows, model = normed.shape
    n_row = model // own.shape[1]
    wide = rest.shape[1]
    shape = jax.ShapeDtypeStruct
    more = [] if attended is None else [attended, weight]
    place = (lambda at: at[0] ^ g) if own.shape[2] > wide else (lambda at: 0)
    return scalar_call(
        functools.partial(mix_kernel, length, n_row),
        at,
        (count,),
        [
            pl.BlockSpec((None, rows, model), lambda i, at: (i, 0, 0)),
            pl.BlockSpec((3, own.shape[1], wide), lambda i, at: (0, 0, place(at))),
            pl.BlockSpec(rest.shape, lambda i, at: (0, 0)),
            pl.BlockSpec((None, 1, 3 * wide), lambda i, at: (place(at), 0, 0)),
        ]
        + [pl.BlockSpec(memory_space=pl.ANY)] * len(more),
        [
            pl.BlockSpec((None, rows, 3 * wide), lambda i, at: (i, 0, 0)),
            pl.BlockSpec((None, rows, wide), lambda i, at: (i, 0, place(at))),
            pl.BlockSpec((model, 3 * wide), lambda i, at: (0, g)),
            pl.BlockSpec((None, rows, wide), lambda i, at: (i, 0, 0)),
            pl.BlockSpec((None, 8, rows), lambda i, at: (i, 0, 0)),
        ],
        [
            shape((count, rows, 3 * wide), BF16),
            shape((count, rows, width), BF16),
            shape((model, 3 * width), BF16),
            shape((count, rows, wide), F32),
            shape((count, 8, rows), F32),
        ],
        "mix",
        0.01,
        scratch=[pltpu.VMEM((rows, 128), F32)],
        aliases={5: 1, 6: 2} if more else {},
    )(at, normed, own, rest, bias, *more)


def mix_back(length, g, groups, at, mixed, up, exact, stats, grads):
    count, rows, three = mixed.shape
    wide = three // 3
    lanes = -(-rows // 128) * 128 * (wide // HEAD_DIM)
    shape = jax.ShapeDtypeStruct
    place = (lambda at: at[0] ^ g) if groups > 1 else (lambda at: 0)
    more = [] if grads is None else [grads]
    return scalar_call(
        functools.partial(mix_back_kernel, length),
        at,
        (count,),
        [
            pl.BlockSpec((None, rows, three), lambda i, at: (i, 0, 0)),
            pl.BlockSpec((None, rows, wide), lambda i, at: (i, 0, place(at))),
            pl.BlockSpec((None, rows, wide), lambda i, at: (i, 0, 0)),
            pl.BlockSpec((None, 8, rows), lambda i, at: (i, 0, 0)),
        ]
        + [pl.BlockSpec(memory_space=pl.ANY)] * len(more),
        [
            pl.BlockSpec((None, rows, three), lambda i, at: (i, 0, g)),
            pl.BlockSpec((None, 1, three), lambda i, at: (i, 0, 0)),
        ],
        [shape((count, rows, groups * three), BF16), shape((count, 1, three), F32)],
        "mix_back",
        0.01,
        scratch=[
            pltpu.VMEM((rows, lanes), BF16),
            pltpu.VMEM((rows, lanes), BF16),
            pltpu.VMEM((lanes, wide), BF16),
            pltpu.VMEM((lanes, wide), BF16),
        ],
        aliases={5: 0} if more else {},
    )(at, stay(mixed), stay(up), stay(exact), stats, *more)


def up_kernel(n_row, at_ref, n_ref, own_ref, rest_ref, bias_ref, *refs):
    act_ref, slope_ref, weight_ref = refs[-3:]
    rows = n_ref.shape[0]
    near = own_ref.shape[0]

    @pl.when(pl.program_id(0) == 0)
    def _():
        for j in range(n_row):
            to = pl.ds(pl.multiple_of((at_ref[1] ^ j) * near, near), near)
            weight_ref[to, :] = own_ref[...] if j == 0 else rest_ref[j - 1]

    for start in range(0, rows, 256):
        at = pl.ds(start, min(256, rows - start))
        hidden = nn(n_ref[at, :], weight_ref[...]) + bias_ref[...]
        gate = 0.5 + 0.5 * jnp.tanh(0.851 * hidden)
        act = hidden * gate
        act_ref[at, :] = act.astype(BF16)
        slope_ref[at, :] = (gate + 1.702 * act * (1.0 - gate)).astype(BF16)


def up(p, at, normed, own, rest, bias, before, us):
    run = rest.shape[2]
    units = own.shape[1]
    count, rows, model = normed.shape
    shape = jax.ShapeDtypeStruct
    place = (lambda at: at[0] ^ p) if units > run else (lambda at: 0)
    block = pl.BlockSpec((None, rows, run), lambda i, at: (i, 0, place(at)))
    return scalar_call(
        functools.partial(up_kernel, model // own.shape[0]),
        at,
        (count,),
        [
            pl.BlockSpec((None, rows, model), lambda i, at: (i, 0, 0)),
            pl.BlockSpec((own.shape[0], run), lambda i, at: (0, place(at))),
            pl.BlockSpec(rest.shape, lambda i, at: (0, 0, 0)),
            pl.BlockSpec((1, run), lambda i, at: (0, place(at))),
        ]
        + [pl.BlockSpec(memory_space=pl.ANY)] * len(before),
        [block, block, pl.BlockSpec((model, run), lambda i, at: (0, place(at)))],
        [shape((count, rows, units), BF16)] * 2 + [shape((model, units), BF16)],
        "expand",
        us,
        limit=32,
        aliases={5: 0, 6: 1, 7: 2} if before else {},
    )(at, normed, own, rest, bias, *before)


def statistics(value):
    centered = value - jnp.mean(value, axis=-1, keepdims=True)
    inverse = lax.rsqrt(jnp.mean(centered * centered, axis=-1, keepdims=True) + 1e-05)
    return centered * inverse, inverse


def shards(
    images,
    cotangent,
    micro_batch,
    heads_weight,
    heads_bias,
    merge_weight,
    merge_bias,
    expand_weight,
    expand_bias,
    shrink_weight,
    shrink_bias,
    norm_gains,
    norm_shifts,
):
    n_dp, n_row = lax.axis_size("dp"), lax.axis_size("row")
    count, length, width = images.shape
    model = width * lax.axis_size("col")
    rows = -(-length // 16) * 16
    pad = ((0, 0), (0, rows - length), (0, 0))
    units = expand_weight.shape[1]
    run = width // n_dp
    split = run % HEAD_DIM == 0
    groups = n_dp if split else 1
    wide = width // groups
    at = jnp.stack([lax.axis_index(axis) for axis in ("dp", "row", "col")]).astype(jnp.int32)

    heads_own = jnp.transpose(heads_weight, (1, 0, 2))
    heads_send = own_part(heads_own, 2).reshape(-1, run)
    all_slots = count * n_dp * n_row
    assert all_slots <= 256 and run >= MICRO
    member = (micro_batch[:, None] == jnp.arange(run, dtype=jnp.int32)[None, :]).astype(F32)
    tail_own = jnp.broadcast_to(jnp.sum(member, axis=0), (16, run)).astype(BF16)
    heads_send = jnp.concatenate([heads_send, tail_own])
    heads_send, images, cotangent, norm_gains = lax.optimization_barrier(
        (heads_send, images, cotangent, norm_gains)
    )
    heads_rows = [peer(heads_send, "row", j) for j in range(1, n_row)]

    params = jnp.concatenate([norm_gains, norm_shifts, merge_bias[None], shrink_bias[None]], axis=0)
    params_tail = jnp.pad(params, ((0, rows - length - params.shape[0]), (0, 0)))
    x_own = jnp.concatenate([images, jnp.broadcast_to(params_tail, (count,) + params_tail.shape)], axis=1)
    cot_own = jnp.pad(cotangent, pad)
    pair = lax.axis_size("col") == 2
    if pair:
        x_other = peer(x_own, "col", 1)
        params = col_join(params, x_other[0, length : length + 6])
    else:
        x = col_full(x_own, 2)
        params = x[0, length : length + 6]
    gain_one, gain_two, shift_one, shift_two, merge_bias_full, _ = (
        params[k].astype(F32) for k in range(6)
    )
    if pair:
        x, normed = join(at, x_own, x_other, (gain_one[None], shift_one[None]))
    else:
        xhat, _ = statistics(x.astype(F32))
        normed = (xhat * gain_one + shift_one).astype(BF16)
    bias3 = jnp.stack([heads_bias[0], jnp.zeros_like(heads_bias[0]), heads_bias[1]]).astype(F32)
    bias3 = bias3.reshape(3, groups, wide).transpose(1, 0, 2).reshape(groups, 1, 3 * wide)

    heads_rows, normed, x, cot_own, expand_send, shrink_send = (
        lax.optimization_barrier(
            (
                heads_rows,
                normed,
                x,
                cot_own,
                own_part(expand_weight, 1),
                own_part(shrink_weight, 0),
            )
        )
    )
    heads_parts = dp_parts(stack(tail_own, heads_rows))
    lanes = merge_weight.shape[1]
    joined = expand_send.shape[1] % lanes == 0
    if joined:
        pieces = [expand_send[:, k : k + lanes] for k in range(0, expand_send.shape[1], lanes)]
        gathered = lax.all_gather(jnp.concatenate([merge_weight, *pieces]), "row")
    else:
        merge_full = lax.all_gather(merge_weight, "row", axis=1, tiled=True)
        expand_rows = lax.all_gather(expand_send, "row")
    shrink_rows = lax.all_gather(shrink_send, "row")
    totals = [piece[-1:, :MICRO].astype(F32) for piece in heads_parts]
    while len(totals) > 1:
        totals = [totals[k] + totals[k + 1] for k in range(0, len(totals), 2)]
    batch_weight = all_slots / (MICRO * totals[0])
    slot_weight = jnp.sum(member[:, :MICRO] * batch_weight, axis=1)
    if not split:
        heads_parts = [xor_order(lax.concatenate(heads_parts, 1), 1, "dp")]

    cot_other = peer(cot_own, "col", 1) if pair else None

    mixed, exact, stats = [None] * groups, [None] * groups, [None] * groups
    attended = heads_full = None
    for g in range(groups):
        mixed[g], attended, heads_full, exact[g], stats[g] = mix(
            length, g, at, normed, heads_own, heads_parts[g], bias3, attended, heads_full, width
        )

    if joined:
        attended, gathered = lax.optimization_barrier((attended, gathered))
        expand_rest = dp_parts(unpack(at, gathered, width, expand_weight.shape[0]))
        attended, expand_rest[0] = lax.optimization_barrier((attended, expand_rest[0]))
        merge_part, merge_full = merge(at, attended, gathered)
    else:
        expand_rest = dp_parts(others(at, expand_rows))
        merge_part = jnp.einsum("itf,fd->itd", attended, merge_full, preferred_element_type=F32)
    share_a, share_b = col_shares(merge_part.astype(BF16))
    middle, normed_two = norm_of_sum(
        x, share_a, share_b, jnp.stack([merge_bias_full, gain_two, shift_two])
    )

    if (units // n_dp) % 128:
        expand_rest = [xor_order(lax.concatenate(expand_rest, 2), 2, "dp")]
    made = ()
    for p in range(len(expand_rest)):
        if p == min(1, len(expand_rest) - 1):
            made, shrink_rows = lax.optimization_barrier((made, shrink_rows))
            shrink_rows = others(at, shrink_rows)
            shrink_all = dp_parts(shrink_rows)
            expand_rest[1:], _ = lax.optimization_barrier((expand_rest[1:], shrink_rows))
        made = up(p, at, normed_two, expand_weight, expand_rest[p], expand_bias.astype(F32)[None], made, 1 if p == 1 else 0.01)
    activated, slope, expand_full = made

    if pair:
        cot, seed_low, seed_sums = seed_of(at, cot_own, cot_other, slot_weight)
    else:
        cot = col_full(cot_own, 2)
        seed_low = (cot.astype(F32) * slot_weight[:, None, None]).astype(BF16)
        seed_sums = jnp.sum(seed_low.astype(F32), axis=1, keepdims=True)

    shrink_grad = product(activated, seed_low, units // n_dp, us=0.01)
    shrink_grad, seed_low, shrink_all = lax.optimization_barrier((shrink_grad, seed_low, shrink_all))
    hidden_grad, hidden_sums, shrink_full = down_back(at, seed_low, slope, shrink_weight, shrink_all)
    hidden_grad, shrink_grad = lax.optimization_barrier((hidden_grad, shrink_grad))
    shrink_sum = scatter_row(shrink_grad, 1)
    expand_grad = product(hidden_grad, normed_two, units // n_dp)
    expand_grad, hidden_grad = lax.optimization_barrier((expand_grad, hidden_grad))
    expand_sum = dp_sum(expand_grad)
    norm_part = jnp.einsum("ith,dh->itd", hidden_grad, expand_full, preferred_element_type=F32)
    norm_part = norm_part.astype(BF16)
    share_a, share_b = col_shares(norm_part)
    branch_grad, sums_two = norm_back(
        at, cot, middle, share_a, share_b, gain_two, slot_weight, None
    )

    attended_grad = jnp.einsum(
        "itd,fd->itf", branch_grad, merge_full, preferred_element_type=F32
    ).astype(BF16)
    merge_grad = jnp.einsum("itf,itd->fd", attended, branch_grad, preferred_element_type=F32)
    merge_grad, attended_grad = lax.optimization_barrier((merge_grad.astype(BF16), attended_grad))
    mixed_grad, mixed_sums, heads_grads = None, [None] * groups, [None] * groups
    merge_sum, heads_in = scatter_row(merge_grad, 1), [None] * groups
    part = units // n_dp
    order = list(range(1, groups)) + [0]
    for turn, g in enumerate(order):
        if turn == max(groups - 2, 0):
            attended_grad, expand_sum, shrink_sum = lax.optimization_barrier(
                (attended_grad, expand_sum, shrink_sum)
            )
            expand_sum = scatter_row(expand_sum, 1)
        if g == 0:
            attended_grad, heads_in[1:2] = lax.optimization_barrier((attended_grad, heads_in[1:2]))
        mixed_grad, mixed_sums[g] = mix_back(
            length, g, groups, at, mixed[g], attended_grad, exact[g], stats[g], mixed_grad
        )
        piece = mixed_grad[:, :, g * 3 * wide : (g + 1) * 3 * wide]
        heads_grads[g] = jnp.einsum("itd,itf->df", normed, piece, preferred_element_type=F32).astype(BF16)
        if g:
            attended_grad, heads_grads[g] = lax.optimization_barrier((attended_grad, heads_grads[g]))
            heads_in[g] = peer(heads_grads[g], "dp", g)
    heads_grads[0], heads_in[1:], shrink_sum, merge_sum = lax.optimization_barrier(
        (heads_grads[0], heads_in[1:], shrink_sum, merge_sum)
    )
    both = jnp.concatenate(
        [shrink_sum.reshape(n_dp, part, -1), merge_sum.reshape(n_dp, run, -1)], axis=1
    )
    both = dp_sum(both.reshape(units + width, -1))
    if not split:
        whole = xor_order(heads_grads[0].reshape(model, 3, width), 2, "dp")
        heads_grads = [cut(whole, 2, n_dp, p).reshape(model, 3 * run) for p in range(n_dp)]
        heads_in = [None] + [peer(heads_grads[p], "dp", p) for p in range(1, n_dp)]
    heads_sum = heads_grads[0].astype(F32)
    for piece in heads_in[1:]:
        heads_sum = heads_sum + piece.astype(F32)
    heads_sum = heads_sum.astype(BF16)
    heads_sum = sum_parts([cut(heads_sum, 0, n_row, j) for j in range(n_row)], "row", at[1])
    first_part = jnp.einsum("itf,df->itd", mixed_grad, heads_full, preferred_element_type=F32)
    first_part = first_part.astype(BF16)
    first_part, activated = lax.optimization_barrier((first_part, activated))
    share_a, share_b = col_shares(first_part)
    packed = dp_all(jnp.concatenate([both, expand_sum]))
    shrink_part = jnp.einsum("ith,hd->itd", activated, shrink_full, preferred_element_type=F32).astype(BF16)
    shrink_part, heads_sum = lax.optimization_barrier((shrink_part, heads_sum))
    own = (length, width) if pair else (rows, model)
    place_of = at if pair else at * jnp.array([1, 1, 0], jnp.int32)
    input_grad, sums_one = norm_back(
        place_of, branch_grad, x, share_a, share_b, gain_one, slot_weight, own
    )

    if pair:
        other = peer(half(at, shrink_part, False), "col", 1)
        output = close(at, middle, shrink_part, other, shrink_bias.astype(F32)[None], length)
    else:
        branch_two = col_own(lax.psum(shrink_part, "col").astype(F32), 2)
        output = (col_own(middle, 2).astype(F32) + (branch_two + shrink_bias.astype(F32))).astype(BF16)[:, :length]
        input_grad = col_own(input_grad, 2)[:, :length]
    packed, sums_one = lax.optimization_barrier((packed, sums_one))
    heads_out = dp_parts(heads_sum)
    heads_out, packed, sums_one = lax.optimization_barrier((heads_out, packed, sums_one))

    sums_one, sums_two = jnp.sum(sums_one, axis=0), jnp.sum(sums_two, axis=0)
    model_sums = jnp.stack(
        [sums_one[0], sums_two[0], sums_one[1], sums_two[1], sums_two[2], jnp.sum(seed_sums, axis=(0, 1))]
    )
    model_sums = col_own(model_sums, 1)
    mixed_sums = jnp.sum(jnp.concatenate(mixed_sums, axis=1), axis=0)
    mixed_sums = mixed_sums.reshape(groups, 3, wide).transpose(1, 0, 2).reshape(3, width)
    heads_bias_grad = mixed_sums[0::2]
    if split:
        heads_bias_grad = xor_order(heads_bias_grad, 1, "dp")
    small = sum_all(jnp.concatenate([model_sums.ravel(), heads_bias_grad.ravel(), hidden_sums[0]]))
    shrink_sum = packed[:, :part].reshape(units, -1).astype(F32)
    merge_sum = packed[:, part : part + run].reshape(width, -1).astype(F32)
    expand_sum = packed[:, part + run :].reshape(units, -1).T.astype(F32)
    if run % 128:
        heads_sum = [piece.reshape(-1, 3, run) for piece in heads_out]
        heads_sum = xor_order(jnp.concatenate(heads_sum, axis=2), 2, "dp").astype(F32)
    else:
        heads_sum = jnp.transpose(spread(at, heads_out), (1, 0, 2))

    model_sums = small[: 6 * width].reshape(6, width)
    return (
        output,
        input_grad,
        heads_sum,
        small[6 * width : 8 * width].reshape(2, width),
        merge_sum,
        model_sums[4],
        expand_sum,
        small[8 * width :],
        shrink_sum,
        model_sums[5],
        model_sums[0:2],
        model_sums[2:4],
    )


def solution(mesh):
    placed = (
        P(("dp", "row"), None, "col"),
        P(("dp", "row"), None, "col"),
        P(("dp", "row")),
        P("row", None, "col"),
        P(None, "col"),
        P("col", "row"),
        P("col"),
        P("row", "col"),
        P("col"),
        P("col", "row"),
        P("col"),
        P(None, "col"),
        P(None, "col"),
    )
    return jax.shard_map(
        shards,
        mesh=mesh,
        in_specs=placed,
        out_specs=(
            P(("dp", "row"), None, "col"),
            P(("dp", "row"), None, "col"),
            P("row", None, "col"),
            P(None, "col"),
            P("col", "row"),
            P("col"),
            P("row", "col"),
            P("col"),
            P("col", "row"),
            P("col"),
            P(None, "col"),
            P(None, "col"),
        ),
        check_vma=False,
    )
```

```python
import functools

import jax
import jax.numpy as jnp
from jax import lax
from jax.experimental import pallas as pl
from jax.experimental.pallas import tpu as pltpu
from jax.sharding import PartitionSpec as P

HEAD_DIM = 64
MICRO = 2
BF16 = jnp.bfloat16
F32 = jnp.float32
VMEM_LIMIT = 58 << 20
STEP = 304
KEYS = 304


def peer(value, axis, p):
    n = lax.axis_size(axis)
    return lax.ppermute(value, axis, [(i, i ^ p) for i in range(n)])


def xor_order(value, dim, axis):
    n = lax.axis_size(axis)
    index = lax.axis_index(axis)
    size = value.shape[dim]
    bit = 1
    while bit < n:
        run = size * bit // n
        pieces = [lax.slice_in_dim(value, at, at + run, axis=dim) for at in range(0, size, run)]
        swapped = lax.concatenate([pieces[k ^ 1] for k in range(len(pieces))], dim)
        value = jnp.where((index & bit) != 0, swapped, value)
        bit *= 2
    return value


def cut(value, dim, n, k):
    run = value.shape[dim] // n
    return lax.slice_in_dim(value, k * run, (k + 1) * run, axis=dim)


def own_part(own, inner_dim):
    run = own.shape[inner_dim] // lax.axis_size("dp")
    return lax.dynamic_slice_in_dim(own, lax.axis_index("dp") * run, run, inner_dim)


def dp_parts(part):
    return [part] + [peer(part, "dp", p) for p in range(1, lax.axis_size("dp"))]


def sum_parts(parts, axis, start=None):
    n = lax.axis_size(axis)
    if start is not None:
        stacked = jnp.stack(parts)
        parts = [lax.dynamic_index_in_dim(stacked, start ^ p, 0, keepdims=False) for p in range(n)]
    total = parts[0].astype(F32)
    for p in range(1, n):
        total = total + peer(parts[p], axis, p).astype(F32)
    return total.astype(BF16)


def dp_sum(blocks):
    n = lax.axis_size("dp")
    blocks = blocks.reshape((n, blocks.shape[0] // n) + blocks.shape[1:])
    return add(lax.all_to_all(blocks, "dp", 0, 0))


def dp_all(part):
    n = lax.axis_size("dp")
    return lax.all_to_all(jnp.broadcast_to(part[None], (n,) + part.shape), "dp", 0, 0)


def scatter_row(value, model_dim):
    return lax.psum_scatter(value, "row", scatter_dimension=model_dim, tiled=True)


def sum_all(value):
    for axis in ("dp", "row"):
        terms = dp_parts(value) if axis == "dp" else [value] + [peer(value, "row", j) for j in range(1, lax.axis_size("row"))]
        while len(terms) > 1:
            terms = [terms[k] + terms[k + 1] for k in range(0, len(terms), 2)]
        value = terms[0]
    return value


def col_join(own, other):
    first = lax.axis_index("col") == 0
    return lax.concatenate([jnp.where(first, own, other), jnp.where(first, other, own)], own.ndim - 1)


def col_full(own, feature_dim):
    return lax.all_gather(own, "col", axis=feature_dim, tiled=True)


def col_own(full, feature_dim):
    n_col = lax.axis_size("col")
    if n_col == 2:
        return jnp.where(
            lax.axis_index("col") == 0, cut(full, feature_dim, 2, 0), cut(full, feature_dim, 2, 1)
        )
    width = full.shape[feature_dim] // n_col
    return lax.dynamic_slice_in_dim(full, lax.axis_index("col") * width, width, feature_dim)


def col_shares(part):
    if lax.axis_size("col") == 2:
        return part, peer(part, "col", 1)
    return lax.psum(part, "col"), jnp.zeros_like(part)


def nt(a, b):
    return lax.dot_general(a, b, (((1,), (1,)), ((), ())), preferred_element_type=F32)


def nn(a, b):
    return lax.dot_general(a, b, (((1,), (0,)), ((), ())), preferred_element_type=F32)


def cost(us, moved=1 << 20):
    return pl.CostEstimate(flops=int(us * 1.0e9), bytes_accessed=1024, transcendentals=0)


def scalar_call(body, at, grid, in_specs, out_specs, out_shape, name, us, scratch=(), limit=24, aliases=None):
    far = lambda a: pltpu.HBM(a.shape, a.dtype)
    out_shape = [far(a) for a in out_shape] if isinstance(out_shape, list) else far(out_shape)
    return pl.pallas_call(
        body,
        grid_spec=pltpu.PrefetchScalarGridSpec(
            num_scalar_prefetch=1,
            grid=grid,
            in_specs=in_specs,
            out_specs=out_specs,
            scratch_shapes=list(scratch),
        ),
        out_shape=out_shape,
        input_output_aliases=aliases or {},
        compiler_params=pltpu.CompilerParams(vmem_limit_bytes=limit << 20),
        cost_estimate=cost(us),
        name=name,
    )


def row_chunks(rows, body):
    for start in range(0, rows, STEP):
        body(pl.ds(start, min(STEP, rows - start)))


def spread_of(value):
    centered = value - jnp.mean(value, axis=1, keepdims=True)
    inverse = lax.rsqrt(jnp.mean(centered * centered, axis=1, keepdims=True) + 1e-05)
    return centered * inverse, inverse


def norm_kernel(x_ref, a_ref, b_ref, params_ref, middle_ref, normed_ref):
    def body(at):
        value = a_ref[at, :].astype(F32) + b_ref[at, :].astype(F32)
        value = x_ref[at, :].astype(F32) + (value + params_ref[0:1, :])
        middle_ref[at, :] = value.astype(BF16)
        xhat, _ = spread_of(value)
        normed_ref[at, :] = (xhat * params_ref[1:2, :] + params_ref[2:3, :]).astype(BF16)

    row_chunks(x_ref.shape[0], body)


def norm_of_sum(x, share_a, share_b, params):
    count, rows, model = x.shape
    image = pl.BlockSpec((None, rows, model), lambda i: (i, 0, 0))
    return pl.pallas_call(
        norm_kernel,
        grid=(count,),
        in_specs=[image] * 3 + [pl.BlockSpec(params.shape, lambda i: (0, 0))],
        out_specs=[image] * 2,
        out_shape=[pltpu.HBM(x.shape, BF16)] * 2,
        compiler_params=pltpu.CompilerParams(vmem_limit_bytes=32 << 20),
        cost_estimate=cost(0.01),
        name="norm_two",
    )(stay(x), stay(share_a), stay(share_b), params)


def norm_back_kernel(second, at_ref, base_ref, v_ref, a_ref, b_ref, gain_ref, weight_ref, *refs):
    grad_ref, sums_ref, scratch = refs
    rows = v_ref.shape[0]
    totals = None

    def body(at):
        nonlocal totals
        xhat, inverse = spread_of(v_ref[at, :].astype(F32))
        upstream = a_ref[at, :].astype(F32) + b_ref[at, :].astype(F32)
        scaled = upstream * gain_ref[...]
        first = jnp.mean(scaled, axis=1, keepdims=True)
        other = jnp.mean(scaled * xhat, axis=1, keepdims=True)
        base = base_ref[at, :].astype(F32)
        if second:
            base = base * weight_ref[pl.program_id(0)]
        grad = base + inverse * (scaled - first - xhat * other)
        parts = [jnp.sum(upstream * xhat, axis=0, keepdims=True), jnp.sum(upstream, axis=0, keepdims=True)]
        if second:
            low = grad.astype(BF16)
            grad_ref[at, :] = low
            parts.append(jnp.sum(low.astype(F32), axis=0, keepdims=True))
        else:
            scratch[at, :] = grad
        totals = parts if totals is None else [x + y for x, y in zip(totals, parts)]

    row_chunks(rows, body)
    for k, total in enumerate(totals):
        sums_ref[k : k + 1, :] = total
    if not second:
        length, width = grad_ref.shape
        grad_ref[...] = scratch[:length, pl.ds(pl.multiple_of(at_ref[2] * width, width), width)]


def norm_back(at, base, v, share_a, share_b, gain, weight, own):
    count, rows, model = v.shape
    second = own is None
    shape = jax.ShapeDtypeStruct
    image = pl.BlockSpec((None, rows, model), lambda i, at: (i, 0, 0))
    sums = 3 if second else 2
    outs = [image] if second else [pl.BlockSpec((None,) + own, lambda i, at: (i, 0, 0))]
    shapes = [shape(v.shape, BF16)] if second else [shape((count,) + own, F32)]
    return scalar_call(
        functools.partial(norm_back_kernel, second),
        at,
        (count,),
        [image] * 4
        + [pl.BlockSpec((1, model), lambda i, at: (0, 0)), pl.BlockSpec(memory_space=pltpu.SMEM)],
        outs + [pl.BlockSpec((None, sums, model), lambda i, at: (i, 0, 0))],
        shapes + [shape((count, sums, model), F32)],
        "norm_back",
        0.01,
        scratch=[pltpu.VMEM((8, 128) if second else (rows, model), F32)],
        limit=48,
    )(at, stay(base), stay(v), stay(share_a), stay(share_b), gain[None], weight)


def join_kernel(normal, at_ref, own_ref, other_ref, *refs):
    out_ref = refs[2] if normal else refs[0]
    rows, width = own_ref.shape
    to = pl.ds(pl.multiple_of(at_ref[2] * width, width), width)
    away = pl.ds(pl.multiple_of((1 - at_ref[2]) * width, width), width)
    out_ref[:, to] = own_ref[...]
    out_ref[:, away] = other_ref[...]
    if not normal:
        return
    gain_ref, shift_ref, _, normed_ref = refs

    def body(at):
        value = out_ref[at, :].astype(F32)
        centered = value - jnp.mean(value, axis=1, keepdims=True)
        inverse = lax.rsqrt(jnp.mean(centered * centered, axis=1, keepdims=True) + 1e-05)
        normed_ref[at, :] = (centered * inverse * gain_ref[...] + shift_ref[...]).astype(BF16)

    row_chunks(rows, body)


def join(at, own, other, vectors=None):
    count, rows, width = own.shape
    normal = vectors is not None
    shape = jax.ShapeDtypeStruct((count, rows, 2 * width), BF16)
    half = pl.BlockSpec((None, rows, width), lambda i, at: (i, 0, 0))
    full = pl.BlockSpec((None, rows, 2 * width), lambda i, at: (i, 0, 0))
    vector = pl.BlockSpec((1, 2 * width), lambda i, at: (0, 0))
    return scalar_call(
        functools.partial(join_kernel, normal),
        at,
        (count,),
        [half, half] + [vector] * (2 if normal else 0),
        [full, full] if normal else full,
        [shape, shape] if normal else shape,
        "join",
        0.01,
    )(at, own, other, *(vectors or ()))


def seed_kernel(at_ref, own_ref, other_ref, weight_ref, cot_ref, seed_ref, sums_ref, sums):
    rows, width = own_ref.shape
    scale = weight_ref[pl.program_id(0)]
    sums[...] = jnp.zeros_like(sums)
    for k, ref in enumerate((own_ref, other_ref)):
        place = at_ref[2] if k == 0 else 1 - at_ref[2]
        to = pl.ds(pl.multiple_of(place * width, width), width)

        def body(at):
            value = ref[at, :]
            low = (value.astype(F32) * scale).astype(BF16)
            cot_ref[at, to] = value
            seed_ref[at, to] = low
            low = low.astype(F32)
            sums[:, to] += jnp.sum(low.reshape(low.shape[0] // 8, 8, width), axis=0)

        row_chunks(rows, body)
    sums_ref[...] = jnp.sum(sums[...], axis=0, keepdims=True)


def seed_of(at, own, other, weight):
    count, rows, width = own.shape
    shape = jax.ShapeDtypeStruct
    half = pl.BlockSpec((None, rows, width), lambda i, at: (i, 0, 0))
    full = pl.BlockSpec((None, rows, 2 * width), lambda i, at: (i, 0, 0))
    return scalar_call(
        seed_kernel,
        at,
        (count,),
        [half, half, pl.BlockSpec(memory_space=pltpu.SMEM)],
        [full, full, pl.BlockSpec((None, 1, 2 * width), lambda i, at: (i, 0, 0))],
        [shape((count, rows, 2 * width), BF16)] * 2 + [shape((count, 1, 2 * width), F32)],
        "seed",
        0.01,
        scratch=[pltpu.VMEM((8, 2 * width), F32)],
    )(at, own, other, weight)


def stay(value):
    return pltpu.with_memory_space_constraint(value, pltpu.HBM)


def stack_kernel(body_rows, own_ref, *refs):
    out_ref = refs[-1]
    total = own_ref[...].astype(F32)
    for k, ref in enumerate(refs[:-1]):
        out_ref[k * body_rows : (k + 1) * body_rows, :] = ref[:body_rows, :]
        total = total + ref[body_rows:, :].astype(F32)
    out_ref[(len(refs) - 1) * body_rows :, :] = total.astype(BF16)


def stack(own_tail, arrays):
    vmem = pl.BlockSpec(memory_space=pltpu.VMEM)
    more, lanes = own_tail.shape
    body = arrays[0].shape[0] - more
    return pl.pallas_call(
        functools.partial(stack_kernel, body),
        in_specs=[vmem] * (1 + len(arrays)),
        out_specs=vmem,
        out_shape=jax.ShapeDtypeStruct((len(arrays) * body + more, lanes), BF16),
        compiler_params=pltpu.CompilerParams(vmem_limit_bytes=16 << 20),
        cost_estimate=cost(0.01),
        name="stack",
    )(own_tail, *arrays)


def unpack_kernel(rows, at_ref, in_ref, out_ref):
    run = in_ref.shape[1]
    near = out_ref.shape[0]
    for k in range(out_ref.shape[1] // run):
        out_ref[:, k * run : (k + 1) * run] = in_ref[rows + k * near : rows + (k + 1) * near, :]


def unpack(at, gathered, rows, near):
    n_row, total, run = gathered.shape
    wide = (total - rows) // near * run
    return scalar_call(
        functools.partial(unpack_kernel, rows),
        at,
        (n_row - 1,),
        [pl.BlockSpec((None, total, run), lambda j, at: (at[1] ^ (j + 1), 0, 0))],
        pl.BlockSpec((None, near, wide), lambda j, at: (j, 0, 0)),
        jax.ShapeDtypeStruct((n_row - 1, near, wide), BF16),
        "unpack",
        0.01,
    )(at, stay(gathered))


def merge_kernel(at_ref, a_ref, g_ref, out_ref, weight_ref):
    n_row, _, near = g_ref.shape

    @pl.when(pl.program_id(0) == 0)
    def _():
        for z in range(n_row):
            weight_ref[:, z * near : (z + 1) * near] = g_ref[z]

    out_ref[...] = nn(a_ref[...], weight_ref[...]).astype(BF16)


def merge(at, attended, gathered):
    count, rows, width = attended.shape
    n_row, _, near = gathered.shape
    shape = jax.ShapeDtypeStruct
    return scalar_call(
        merge_kernel,
        at,
        (count,),
        [
            pl.BlockSpec((None, rows, width), lambda i, at: (i, 0, 0)),
            pl.BlockSpec((n_row, width, near), lambda i, at: (0, 0, 0), pipeline_mode=pl.Buffered(1)),
        ],
        [
            pl.BlockSpec((None, rows, n_row * near), lambda i, at: (i, 0, 0)),
            pl.BlockSpec((width, n_row * near), lambda i, at: (0, 0)),
        ],
        [shape((count, rows, n_row * near), BF16), shape((width, n_row * near), BF16)],
        "merge",
        0.01,
    )(at, attended, stay(gathered))


def product_kernel(a_ref, b_ref, out_ref):
    total = None
    for i in range(a_ref.shape[0]):
        part = lax.dot_general(a_ref[i], b_ref[i], (((0,), (0,)), ((), ())), preferred_element_type=F32)
        total = part if total is None else total + part
    out_ref[...] = total.astype(BF16)


def product(a, b, run, lanes=None, block=0, us=0.01):
    count, rows, units = a.shape
    lanes = b.shape[2] if lanes is None else lanes
    run = run if run % 128 == 0 else units
    return pl.pallas_call(
        product_kernel,
        grid=(units // run,),
        in_specs=[
            pl.BlockSpec((count, rows, run), lambda q: (0, 0, q)),
            pl.BlockSpec((count, rows, lanes), lambda q: (0, 0, block), pipeline_mode=pl.Buffered(1)),
        ],
        out_specs=pl.BlockSpec((run, lanes), lambda q: (q, 0)),
        out_shape=pltpu.HBM((units, lanes), BF16),
        compiler_params=pltpu.CompilerParams(vmem_limit_bytes=40 << 20),
        cost_estimate=cost(us),
        name="product",
    )(stay(a), stay(b))


def pick_kernel(at_ref, in_ref, out_ref):
    out_ref[...] = in_ref[...]


def others(at, gathered):
    n_row = gathered.shape[0]
    block = (None,) + gathered.shape[1:]
    return scalar_call(
        pick_kernel,
        at,
        (n_row - 1,),
        [pl.BlockSpec(block, lambda j, at: (at[1] ^ (j + 1), 0, 0))],
        pl.BlockSpec(block, lambda j, at: (j, 0, 0)),
        jax.ShapeDtypeStruct((n_row - 1,) + gathered.shape[1:], gathered.dtype),
        "others",
        0.01,
    )(at, stay(gathered))


def down_back_kernel(n_dp, at_ref, seed_ref, slope_ref, own_ref, *refs):
    rest, (grad_ref, sums_ref, weight_ref) = refs[:n_dp], refs[n_dp:]
    others, _, near = rest[0].shape
    for p in range(n_dp):

        @pl.when(pl.program_id(0) == p)
        def _(p=p):
            for j in range(others + 1):
                to = pl.ds(pl.multiple_of((at_ref[1] ^ j) * near, near), near)
                weight_ref[:, to] = rest[p][j - 1] if j else own_ref[...]

    sums = None
    for i in range(seed_ref.shape[0]):
        grad = (nt(seed_ref[i], weight_ref[...]) * slope_ref[i].astype(F32)).astype(BF16)
        grad_ref[i] = grad
        part = jnp.sum(grad.astype(F32), axis=0, keepdims=True)
        sums = part if sums is None else sums + part
    sums_ref[...] = sums


def down_back(at, seed, slope, own, rest):
    if rest[0].shape[1] % 128:
        rest = [xor_order(lax.concatenate(rest, 1), 1, "dp")]
    n_dp = len(rest)
    others, run, near = rest[0].shape
    count, rows, model = seed.shape
    units = own.shape[0]
    shape = jax.ShapeDtypeStruct
    place = (lambda at, p: at[0] ^ p) if n_dp > 1 else (lambda at, p: 0)
    block = pl.BlockSpec((count, rows, run), lambda p, at: (0, 0, place(at, p)))
    return scalar_call(
        functools.partial(down_back_kernel, n_dp),
        at,
        (n_dp,),
        [
            pl.BlockSpec(seed.shape, lambda p, at: (0, 0, 0), pipeline_mode=pl.Buffered(1)),
            block,
            pl.BlockSpec((run, near), lambda p, at: (place(at, p), 0)),
        ]
        + [pl.BlockSpec(a.shape, lambda p, at: (0, 0, 0), pipeline_mode=pl.Buffered(1)) for a in rest],
        [
            block,
            pl.BlockSpec((1, run), lambda p, at: (0, place(at, p))),
            pl.BlockSpec((run, model), lambda p, at: (place(at, p), 0)),
        ],
        [shape((count, rows, units), BF16), shape((1, units), F32), shape((units, model), BF16)],
        "down_back",
        0.01,
        limit=40,
    )(at, stay(seed), stay(slope), own, *[stay(a) for a in rest])


def add_kernel(in_ref, out_ref):
    out_ref[...] = jnp.sum(in_ref[...].astype(F32), axis=0).astype(BF16)


def add(blocks):
    n, rows, lanes = blocks.shape
    step = rows // 4 if rows % 64 == 0 else rows
    return pl.pallas_call(
        add_kernel,
        grid=(rows // step,),
        in_specs=[pl.BlockSpec((n, step, lanes), lambda i: (0, i, 0))],
        out_specs=pl.BlockSpec((step, lanes), lambda i: (i, 0)),
        out_shape=jax.ShapeDtypeStruct((rows, lanes), BF16),
        compiler_params=pltpu.CompilerParams(vmem_limit_bytes=24 << 20),
        cost_estimate=cost(0.01),
        name="add",
    )(blocks)


def half_kernel(at_ref, in_ref, out_ref):
    out_ref[...] = in_ref[...]


def half(at, value, own):
    count, rows, model = value.shape
    place = (lambda at: at[2]) if own else (lambda at: 1 - at[2])
    return scalar_call(
        half_kernel,
        at,
        (count,),
        [pl.BlockSpec((None, rows, model // 2), lambda i, at: (i, 0, place(at)))],
        pl.BlockSpec((None, rows, model // 2), lambda i, at: (i, 0, 0)),
        jax.ShapeDtypeStruct((count, rows, model // 2), value.dtype),
        "half",
        0.01,
    )(at, value)


def close_kernel(at_ref, m_ref, a_ref, b_ref, bias_ref, out_ref):
    def body(at):
        share = a_ref[at, :].astype(F32) + b_ref[at, :].astype(F32)
        out_ref[at, :] = (m_ref[at, :].astype(F32) + (share + bias_ref[...])).astype(BF16)

    row_chunks(out_ref.shape[0], body)


def close(at, middle, part, other, bias, length):
    count, rows, width = other.shape
    mine = pl.BlockSpec((None, rows, width), lambda i, at: (i, 0, at[2]))
    plain = pl.BlockSpec((None, rows, width), lambda i, at: (i, 0, 0))
    return scalar_call(
        close_kernel,
        at,
        (count,),
        [mine, mine, plain, pl.BlockSpec((1, width), lambda i, at: (0, 0))],
        pl.BlockSpec((None, length, width), lambda i, at: (i, 0, 0)),
        jax.ShapeDtypeStruct((count, length, width), BF16),
        "close",
        0.01,
    )(at, stay(middle), stay(part), other, bias)


def spread_kernel(n_dp, at_ref, *refs):
    out_ref = refs[-1]
    run = out_ref.shape[2] // n_dp
    for p in range(n_dp):
        to = pl.ds(pl.multiple_of((at_ref[0] ^ p) * run, run), run)
        for k in range(3):
            out_ref[k, :, to] = refs[p][:, k * run : (k + 1) * run].astype(F32)


def spread(at, parts):
    n_dp = len(parts)
    rows, three = parts[0].shape
    run = three // 3
    vmem = pl.BlockSpec((rows, three), lambda i, at: (0, 0))
    return scalar_call(
        functools.partial(spread_kernel, n_dp),
        at,
        (1,),
        [vmem] * n_dp,
        pl.BlockSpec((3, rows, n_dp * run), lambda i, at: (0, 0, 0)),
        jax.ShapeDtypeStruct((3, rows, n_dp * run), F32),
        "spread",
        0.01,
    )(at, *parts)


def head_mask(rows, width, h):
    lane = lax.broadcasted_iota(jnp.int32, (rows, width), 1)
    return (lane >= h * HEAD_DIM) & (lane < (h + 1) * HEAD_DIM)


def mix_kernel(length, n_row, at_ref, n_ref, own_ref, rest_ref, bias_ref, *refs):
    mixed_ref, o_ref, weight_ref, exact_ref, stats_ref, lanes_ref = refs[-6:]
    rows = n_ref.shape[0]
    width = o_ref.shape[1]
    count = width // HEAD_DIM
    near = own_ref.shape[1]
    chunk = rows

    @pl.when(pl.program_id(0) == 0)
    def _():
        for j in range(n_row):
            to = pl.ds(pl.multiple_of((at_ref[1] ^ j) * near, near), near)
            for k in range(3):
                start = ((j - 1) * 3 + k) * near
                piece = own_ref[k] if j == 0 else rest_ref[start : start + near, :]
                weight_ref[to, k * width : (k + 1) * width] = piece

    for start in range(0, rows, chunk):
        size = min(chunk, rows - start)
        at = pl.ds(start, size)
        mixed = nn(n_ref[at, :], weight_ref[...]) + bias_ref[...]
        mixed_ref[at, :width] = (mixed[:, :width] * HEAD_DIM**-0.5).astype(BF16)
        mixed_ref[at, width:] = mixed[:, width:].astype(BF16)
    plain = length // 128 * 128
    k = mixed_ref[:, width : 2 * width]
    v = mixed_ref[:, 2 * width :]
    for start in range(0, rows, chunk):
        size = min(chunk, rows - start)
        at = pl.ds(start, size)
        q = mixed_ref[at, :width]
        result, stats = None, jnp.zeros((size, 128), F32)
        place = lax.broadcasted_iota(jnp.int32, (size, 128), 1)
        for h in range(count):
            mask = head_mask(size, width, h)
            query = jnp.where(mask, q, jnp.zeros_like(q))
            near, far = nt(query, k[:plain]), nt(query, k[plain:])
            key = lax.broadcasted_iota(jnp.int32, far.shape, 1) + plain
            far = jnp.where(key < length, far, -1e30)
            top = jnp.maximum(jnp.max(near, axis=1, keepdims=True), jnp.max(far, axis=1, keepdims=True))
            near, far = jnp.exp(near - top), jnp.exp(far - top)
            total = jnp.sum(near, axis=1, keepdims=True) + jnp.sum(far, axis=1, keepdims=True)
            out = (nn(near.astype(BF16), v[:plain]) + nn(far.astype(BF16), v[plain:])) / total
            result = out if result is None else jnp.where(mask, out, result)
            stats = jnp.where(place == h, top + jnp.log(total), stats)
        o_ref[at, :] = result.astype(BF16)
        exact_ref[at, :] = result
        lanes_ref[at, :] = stats
    row = lax.broadcasted_iota(jnp.int32, (8, 128), 0)
    lane = lax.broadcasted_iota(jnp.int32, (8, 128), 1)
    stats_ref[...] = turned(jnp.where(row == lane, 1.0, 0.0), lanes_ref[...])


def turned(select, value):
    return lax.dot_general(
        select, value, (((1,), (1,)), ((), ())), precision=lax.Precision.HIGHEST, preferred_element_type=F32
    )


def mix_back_kernel(length, at_ref, m_ref, up_ref, exact_ref, stats_ref, *refs):
    d_ref, sums_ref, probs, grads, q_all, up_all = refs[-6:]
    rows, width = up_ref.shape
    count = width // HEAD_DIM
    lanes = probs.shape[1] // count
    chunk = 256
    row = lax.broadcasted_iota(jnp.int32, (8, width), 0)
    lane = lax.broadcasted_iota(jnp.int32, (8, width), 1)
    select = jnp.where((lane >= row * HEAD_DIM) & (lane < (row + 1) * HEAD_DIM), 1.0, 0.0)
    delta = turned(select, up_ref[...].astype(F32) * exact_ref[...])
    for h in range(count):
        base = h * lanes
        if rows < lanes:
            probs[:, pl.ds(base + rows, lanes - rows)] = jnp.zeros((rows, lanes - rows), BF16)
            grads[:, pl.ds(base + rows, lanes - rows)] = jnp.zeros((rows, lanes - rows), BF16)
            q_all[pl.ds(base + rows, lanes - rows), :] = jnp.zeros((lanes - rows, width), BF16)
            up_all[pl.ds(base + rows, lanes - rows), :] = jnp.zeros((lanes - rows, width), BF16)
        for start in range(0, rows, chunk):
            size = min(chunk, rows - start)
            mask = head_mask(size, width, h)
            q = m_ref[pl.ds(start, size), :width]
            up = up_ref[pl.ds(start, size), :]
            q = jnp.where(mask, q, jnp.zeros_like(q))
            up = jnp.where(mask, up, jnp.zeros_like(up))
            q_all[pl.ds(base + start, size), :] = q
            up_all[pl.ds(base + start, size), :] = up
            total = stats_ref[h : h + 1, start : start + size]
            mean = delta[h : h + 1, start : start + size]
            for first in range(0, rows, KEYS):
                keys = pl.ds(first, min(KEYS, rows - first))
                share = jnp.exp(nt(m_ref[keys, width : 2 * width], q) - total)
                if first + KEYS > length:
                    key = lax.broadcasted_iota(jnp.int32, share.shape, 0) + first
                    share = jnp.where(key < length, share, 0.0)
                prob_grad = nt(m_ref[keys, 2 * width :], up)
                probs[keys, pl.ds(base + start, size)] = share.astype(BF16)
                grads[keys, pl.ds(base + start, size)] = (share * (prob_grad - mean)).astype(BF16)
    dv = nn(probs[...], up_all[...]).astype(BF16)
    dk = nn(grads[...], q_all[...]).astype(BF16)
    flipped = m_ref[:, width : 2 * width].astype(F32).T.astype(BF16)
    pieces = []
    for h in range(count):
        pieces.append(nn(flipped[h * HEAD_DIM : (h + 1) * HEAD_DIM, :], grads[:, pl.ds(h * lanes, rows)]))
    dq = jnp.concatenate(pieces, axis=0).T if count > 1 else pieces[0].T
    dq = (dq.astype(BF16).astype(F32) * HEAD_DIM**-0.5).astype(BF16)
    for at, value in enumerate((dq, dk, dv)):
        d_ref[:, at * width : (at + 1) * width] = value
        sums_ref[:, at * width : (at + 1) * width] = jnp.sum(value.astype(F32), axis=0, keepdims=True)


def mix(length, g, at, normed, own, rest, bias, attended, weight, width):
    count, rows, model = normed.shape
    n_row = model // own.shape[1]
    wide = rest.shape[1]
    shape = jax.ShapeDtypeStruct
    more = [] if attended is None else [attended, weight]
    place = (lambda at: at[0] ^ g) if own.shape[2] > wide else (lambda at: 0)
    return scalar_call(
        functools.partial(mix_kernel, length, n_row),
        at,
        (count,),
        [
            pl.BlockSpec((None, rows, model), lambda i, at: (i, 0, 0)),
            pl.BlockSpec((3, own.shape[1], wide), lambda i, at: (0, 0, place(at))),
            pl.BlockSpec(rest.shape, lambda i, at: (0, 0)),
            pl.BlockSpec((None, 1, 3 * wide), lambda i, at: (place(at), 0, 0)),
        ]
        + [pl.BlockSpec(memory_space=pl.ANY)] * len(more),
        [
            pl.BlockSpec((None, rows, 3 * wide), lambda i, at: (i, 0, 0)),
            pl.BlockSpec((None, rows, wide), lambda i, at: (i, 0, place(at))),
            pl.BlockSpec((model, 3 * wide), lambda i, at: (0, g)),
            pl.BlockSpec((None, rows, wide), lambda i, at: (i, 0, 0)),
            pl.BlockSpec((None, 8, rows), lambda i, at: (i, 0, 0)),
        ],
        [
            shape((count, rows, 3 * wide), BF16),
            shape((count, rows, width), BF16),
            shape((model, 3 * width), BF16),
            shape((count, rows, wide), F32),
            shape((count, 8, rows), F32),
        ],
        "mix",
        0.01,
        scratch=[pltpu.VMEM((rows, 128), F32)],
        aliases={5: 1, 6: 2} if more else {},
    )(at, normed, own, rest, bias, *more)


def mix_back(length, g, groups, at, mixed, up, exact, stats, grads):
    count, rows, three = mixed.shape
    wide = three // 3
    lanes = -(-rows // 128) * 128 * (wide // HEAD_DIM)
    shape = jax.ShapeDtypeStruct
    place = (lambda at: at[0] ^ g) if groups > 1 else (lambda at: 0)
    more = [] if grads is None else [grads]
    return scalar_call(
        functools.partial(mix_back_kernel, length),
        at,
        (count,),
        [
            pl.BlockSpec((None, rows, three), lambda i, at: (i, 0, 0)),
            pl.BlockSpec((None, rows, wide), lambda i, at: (i, 0, place(at))),
            pl.BlockSpec((None, rows, wide), lambda i, at: (i, 0, 0)),
            pl.BlockSpec((None, 8, rows), lambda i, at: (i, 0, 0)),
        ]
        + [pl.BlockSpec(memory_space=pl.ANY)] * len(more),
        [
            pl.BlockSpec((None, rows, three), lambda i, at: (i, 0, g)),
            pl.BlockSpec((None, 1, three), lambda i, at: (i, 0, 0)),
        ],
        [shape((count, rows, groups * three), BF16), shape((count, 1, three), F32)],
        "mix_back",
        0.01,
        scratch=[
            pltpu.VMEM((rows, lanes), BF16),
            pltpu.VMEM((rows, lanes), BF16),
            pltpu.VMEM((lanes, wide), BF16),
            pltpu.VMEM((lanes, wide), BF16),
        ],
        aliases={5: 0} if more else {},
    )(at, stay(mixed), stay(up), stay(exact), stats, *more)


def up_kernel(n_row, at_ref, n_ref, own_ref, rest_ref, bias_ref, *refs):
    act_ref, slope_ref, weight_ref = refs[-3:]
    rows = n_ref.shape[0]
    near = own_ref.shape[0]

    @pl.when(pl.program_id(0) == 0)
    def _():
        for j in range(n_row):
            to = pl.ds(pl.multiple_of((at_ref[1] ^ j) * near, near), near)
            weight_ref[to, :] = own_ref[...] if j == 0 else rest_ref[j - 1]

    for start in range(0, rows, 256):
        at = pl.ds(start, min(256, rows - start))
        hidden = nn(n_ref[at, :], weight_ref[...]) + bias_ref[...]
        gate = 0.5 + 0.5 * jnp.tanh(0.851 * hidden)
        act = hidden * gate
        act_ref[at, :] = act.astype(BF16)
        slope_ref[at, :] = (gate + 1.702 * act * (1.0 - gate)).astype(BF16)


def up(p, at, normed, own, rest, bias, before, us):
    run = rest.shape[2]
    units = own.shape[1]
    count, rows, model = normed.shape
    shape = jax.ShapeDtypeStruct
    place = (lambda at: at[0] ^ p) if units > run else (lambda at: 0)
    block = pl.BlockSpec((None, rows, run), lambda i, at: (i, 0, place(at)))
    return scalar_call(
        functools.partial(up_kernel, model // own.shape[0]),
        at,
        (count,),
        [
            pl.BlockSpec((None, rows, model), lambda i, at: (i, 0, 0)),
            pl.BlockSpec((own.shape[0], run), lambda i, at: (0, place(at))),
            pl.BlockSpec(rest.shape, lambda i, at: (0, 0, 0)),
            pl.BlockSpec((1, run), lambda i, at: (0, place(at))),
        ]
        + [pl.BlockSpec(memory_space=pl.ANY)] * len(before),
        [block, block, pl.BlockSpec((model, run), lambda i, at: (0, place(at)))],
        [shape((count, rows, units), BF16)] * 2 + [shape((model, units), BF16)],
        "expand",
        us,
        limit=32,
        aliases={5: 0, 6: 1, 7: 2} if before else {},
    )(at, normed, own, rest, bias, *before)


def statistics(value):
    centered = value - jnp.mean(value, axis=-1, keepdims=True)
    inverse = lax.rsqrt(jnp.mean(centered * centered, axis=-1, keepdims=True) + 1e-05)
    return centered * inverse, inverse


def shards(
    images,
    cotangent,
    micro_batch,
    heads_weight,
    heads_bias,
    merge_weight,
    merge_bias,
    expand_weight,
    expand_bias,
    shrink_weight,
    shrink_bias,
    norm_gains,
    norm_shifts,
):
    n_dp, n_row = lax.axis_size("dp"), lax.axis_size("row")
    count, length, width = images.shape
    model = width * lax.axis_size("col")
    rows = -(-length // 16) * 16
    pad = ((0, 0), (0, rows - length), (0, 0))
    units = expand_weight.shape[1]
    run = width // n_dp
    split = run % HEAD_DIM == 0
    groups = n_dp if split else 1
    wide = width // groups
    at = jnp.stack([lax.axis_index(axis) for axis in ("dp", "row", "col")]).astype(jnp.int32)

    heads_own = jnp.transpose(heads_weight, (1, 0, 2))
    heads_send = own_part(heads_own, 2).reshape(-1, run)
    all_slots = count * n_dp * n_row
    assert all_slots <= 256 and run >= MICRO
    member = (micro_batch[:, None] == jnp.arange(run, dtype=jnp.int32)[None, :]).astype(F32)
    tail_own = jnp.broadcast_to(jnp.sum(member, axis=0), (16, run)).astype(BF16)
    heads_send = jnp.concatenate([heads_send, tail_own])
    heads_send, images, cotangent, norm_gains = lax.optimization_barrier(
        (heads_send, images, cotangent, norm_gains)
    )
    heads_rows = [peer(heads_send, "row", j) for j in range(1, n_row)]

    params = jnp.concatenate([norm_gains, norm_shifts, merge_bias[None], shrink_bias[None]], axis=0)
    params_tail = jnp.pad(params, ((0, rows - length - params.shape[0]), (0, 0)))
    x_own = jnp.concatenate([images, jnp.broadcast_to(params_tail, (count,) + params_tail.shape)], axis=1)
    cot_own = jnp.pad(cotangent, pad)
    pair = lax.axis_size("col") == 2
    if pair:
        x_other = peer(x_own, "col", 1)
        params = col_join(params, x_other[0, length : length + 6])
    else:
        x = col_full(x_own, 2)
        params = x[0, length : length + 6]
    gain_one, gain_two, shift_one, shift_two, merge_bias_full, _ = (
        params[k].astype(F32) for k in range(6)
    )
    if pair:
        x, normed = join(at, x_own, x_other, (gain_one[None], shift_one[None]))
    else:
        xhat, _ = statistics(x.astype(F32))
        normed = (xhat * gain_one + shift_one).astype(BF16)
    bias3 = jnp.stack([heads_bias[0], jnp.zeros_like(heads_bias[0]), heads_bias[1]]).astype(F32)
    bias3 = bias3.reshape(3, groups, wide).transpose(1, 0, 2).reshape(groups, 1, 3 * wide)

    heads_rows, normed, x, cot_own, expand_send, shrink_send = (
        lax.optimization_barrier(
            (
                heads_rows,
                normed,
                x,
                cot_own,
                own_part(expand_weight, 1),
                own_part(shrink_weight, 0),
            )
        )
    )
    heads_parts = dp_parts(stack(tail_own, heads_rows))
    lanes = merge_weight.shape[1]
    joined = expand_send.shape[1] % lanes == 0
    if joined:
        pieces = [expand_send[:, k : k + lanes] for k in range(0, expand_send.shape[1], lanes)]
        gathered = lax.all_gather(jnp.concatenate([merge_weight, *pieces]), "row")
    else:
        merge_full = lax.all_gather(merge_weight, "row", axis=1, tiled=True)
        expand_rows = lax.all_gather(expand_send, "row")
    shrink_rows = lax.all_gather(shrink_send, "row")
    totals = [piece[-1:, :MICRO].astype(F32) for piece in heads_parts]
    while len(totals) > 1:
        totals = [totals[k] + totals[k + 1] for k in range(0, len(totals), 2)]
    batch_weight = all_slots / (MICRO * totals[0])
    slot_weight = jnp.sum(member[:, :MICRO] * batch_weight, axis=1)
    if not split:
        heads_parts = [xor_order(lax.concatenate(heads_parts, 1), 1, "dp")]

    cot_other = peer(cot_own, "col", 1) if pair else None

    mixed, exact, stats = [None] * groups, [None] * groups, [None] * groups
    attended = heads_full = None
    for g in range(groups):
        mixed[g], attended, heads_full, exact[g], stats[g] = mix(
            length, g, at, normed, heads_own, heads_parts[g], bias3, attended, heads_full, width
        )

    if joined:
        attended, gathered = lax.optimization_barrier((attended, gathered))
        expand_rest = dp_parts(unpack(at, gathered, width, expand_weight.shape[0]))
        attended, expand_rest[0] = lax.optimization_barrier((attended, expand_rest[0]))
        merge_part, merge_full = merge(at, attended, gathered)
    else:
        expand_rest = dp_parts(others(at, expand_rows))
        merge_part = jnp.einsum("itf,fd->itd", attended, merge_full, preferred_element_type=F32)
    share_a, share_b = col_shares(merge_part.astype(BF16))
    middle, normed_two = norm_of_sum(
        x, share_a, share_b, jnp.stack([merge_bias_full, gain_two, shift_two])
    )

    if (units // n_dp) % 128:
        expand_rest = [xor_order(lax.concatenate(expand_rest, 2), 2, "dp")]
    made = ()
    for p in range(len(expand_rest)):
        if p == min(1, len(expand_rest) - 1):
            made, shrink_rows = lax.optimization_barrier((made, shrink_rows))
            shrink_rows = others(at, shrink_rows)
            shrink_all = dp_parts(shrink_rows)
            expand_rest[1:], _ = lax.optimization_barrier((expand_rest[1:], shrink_rows))
        made = up(p, at, normed_two, expand_weight, expand_rest[p], expand_bias.astype(F32)[None], made, 1 if p == 1 else 0.01)
    activated, slope, expand_full = made

    if pair:
        cot, seed_low, seed_sums = seed_of(at, cot_own, cot_other, slot_weight)
    else:
        cot = col_full(cot_own, 2)
        seed_low = (cot.astype(F32) * slot_weight[:, None, None]).astype(BF16)
        seed_sums = jnp.sum(seed_low.astype(F32), axis=1, keepdims=True)

    shrink_grad = product(activated, seed_low, units // n_dp, us=0.01)
    shrink_grad, seed_low, shrink_all = lax.optimization_barrier((shrink_grad, seed_low, shrink_all))
    hidden_grad, hidden_sums, shrink_full = down_back(at, seed_low, slope, shrink_weight, shrink_all)
    hidden_grad, shrink_grad = lax.optimization_barrier((hidden_grad, shrink_grad))
    shrink_sum = scatter_row(shrink_grad, 1)
    expand_grad = product(hidden_grad, normed_two, units // n_dp)
    expand_grad, hidden_grad = lax.optimization_barrier((expand_grad, hidden_grad))
    expand_sum = dp_sum(expand_grad)
    norm_part = jnp.einsum("ith,dh->itd", hidden_grad, expand_full, preferred_element_type=F32)
    norm_part = norm_part.astype(BF16)
    share_a, share_b = col_shares(norm_part)
    branch_grad, sums_two = norm_back(
        at, cot, middle, share_a, share_b, gain_two, slot_weight, None
    )

    attended_grad = jnp.einsum(
        "itd,fd->itf", branch_grad, merge_full, preferred_element_type=F32
    ).astype(BF16)
    merge_grad = jnp.einsum("itf,itd->fd", attended, branch_grad, preferred_element_type=F32)
    merge_grad, attended_grad = lax.optimization_barrier((merge_grad.astype(BF16), attended_grad))
    mixed_grad, mixed_sums, heads_grads = None, [None] * groups, [None] * groups
    merge_sum, heads_in = scatter_row(merge_grad, 1), [None] * groups
    part = units // n_dp
    order = list(range(1, groups)) + [0]
    for turn, g in enumerate(order):
        if turn == max(groups - 2, 0):
            attended_grad, expand_sum, shrink_sum = lax.optimization_barrier(
                (attended_grad, expand_sum, shrink_sum)
            )
            expand_sum = scatter_row(expand_sum, 1)
        if g == 0:
            attended_grad, heads_in[1:2] = lax.optimization_barrier((attended_grad, heads_in[1:2]))
        mixed_grad, mixed_sums[g] = mix_back(
            length, g, groups, at, mixed[g], attended_grad, exact[g], stats[g], mixed_grad
        )
        piece = mixed_grad[:, :, g * 3 * wide : (g + 1) * 3 * wide]
        heads_grads[g] = jnp.einsum("itd,itf->df", normed, piece, preferred_element_type=F32).astype(BF16)
        if g:
            attended_grad, heads_grads[g] = lax.optimization_barrier((attended_grad, heads_grads[g]))
            heads_in[g] = peer(heads_grads[g], "dp", g)
    heads_grads[0], heads_in[1:], shrink_sum, merge_sum = lax.optimization_barrier(
        (heads_grads[0], heads_in[1:], shrink_sum, merge_sum)
    )
    both = jnp.concatenate(
        [shrink_sum.reshape(n_dp, part, -1), merge_sum.reshape(n_dp, run, -1)], axis=1
    )
    both = dp_sum(both.reshape(units + width, -1))
    if not split:
        whole = xor_order(heads_grads[0].reshape(model, 3, width), 2, "dp")
        heads_grads = [cut(whole, 2, n_dp, p).reshape(model, 3 * run) for p in range(n_dp)]
        heads_in = [None] + [peer(heads_grads[p], "dp", p) for p in range(1, n_dp)]
    heads_sum = heads_grads[0].astype(F32)
    for piece in heads_in[1:]:
        heads_sum = heads_sum + piece.astype(F32)
    heads_sum = heads_sum.astype(BF16)
    heads_sum = sum_parts([cut(heads_sum, 0, n_row, j) for j in range(n_row)], "row", at[1])
    first_part = jnp.einsum("itf,df->itd", mixed_grad, heads_full, preferred_element_type=F32)
    first_part = first_part.astype(BF16)
    first_part, activated = lax.optimization_barrier((first_part, activated))
    share_a, share_b = col_shares(first_part)
    packed = dp_all(jnp.concatenate([both, expand_sum]))
    shrink_part = jnp.einsum("ith,hd->itd", activated, shrink_full, preferred_element_type=F32).astype(BF16)
    shrink_part, heads_sum = lax.optimization_barrier((shrink_part, heads_sum))
    own = (length, width) if pair else (rows, model)
    place_of = at if pair else at * jnp.array([1, 1, 0], jnp.int32)
    input_grad, sums_one = norm_back(
        place_of, branch_grad, x, share_a, share_b, gain_one, slot_weight, own
    )

    if pair:
        other = peer(half(at, shrink_part, False), "col", 1)
        output = close(at, middle, shrink_part, other, shrink_bias.astype(F32)[None], length)
    else:
        branch_two = col_own(lax.psum(shrink_part, "col").astype(F32), 2)
        output = (col_own(middle, 2).astype(F32) + (branch_two + shrink_bias.astype(F32))).astype(BF16)[:, :length]
        input_grad = col_own(input_grad, 2)[:, :length]
    packed, sums_one = lax.optimization_barrier((packed, sums_one))
    heads_out = dp_parts(heads_sum)
    heads_out, packed, sums_one = lax.optimization_barrier((heads_out, packed, sums_one))

    sums_one, sums_two = jnp.sum(sums_one, axis=0), jnp.sum(sums_two, axis=0)
    model_sums = jnp.stack(
        [sums_one[0], sums_two[0], sums_one[1], sums_two[1], sums_two[2], jnp.sum(seed_sums, axis=(0, 1))]
    )
    model_sums = col_own(model_sums, 1)
    mixed_sums = jnp.sum(jnp.concatenate(mixed_sums, axis=1), axis=0)
    mixed_sums = mixed_sums.reshape(groups, 3, wide).transpose(1, 0, 2).reshape(3, width)
    heads_bias_grad = mixed_sums[0::2]
    if split:
        heads_bias_grad = xor_order(heads_bias_grad, 1, "dp")
    small = sum_all(jnp.concatenate([model_sums.ravel(), heads_bias_grad.ravel(), hidden_sums[0]]))
    shrink_sum = packed[:, :part].reshape(units, -1).astype(F32)
    merge_sum = packed[:, part : part + run].reshape(width, -1).astype(F32)
    expand_sum = packed[:, part + run :].reshape(units, -1).T.astype(F32)
    if run % 128:
        heads_sum = [piece.reshape(-1, 3, run) for piece in heads_out]
        heads_sum = xor_order(jnp.concatenate(heads_sum, axis=2), 2, "dp").astype(F32)
    else:
        heads_sum = jnp.transpose(spread(at, heads_out), (1, 0, 2))

    model_sums = small[: 6 * width].reshape(6, width)
    return (
        output,
        input_grad,
        heads_sum,
        small[6 * width : 8 * width].reshape(2, width),
        merge_sum,
        model_sums[4],
        expand_sum,
        small[8 * width :],
        shrink_sum,
        model_sums[5],
        model_sums[0:2],
        model_sums[2:4],
    )


def solution(mesh):
    placed = (
        P(("dp", "row"), None, "col"),
        P(("dp", "row"), None, "col"),
        P(("dp", "row")),
        P("row", None, "col"),
        P(None, "col"),
        P("col", "row"),
        P("col"),
        P("row", "col"),
        P("col"),
        P("col", "row"),
        P("col"),
        P(None, "col"),
        P(None, "col"),
    )
    return jax.shard_map(
        shards,
        mesh=mesh,
        in_specs=placed,
        out_specs=(
            P(("dp", "row"), None, "col"),
            P(("dp", "row"), None, "col"),
            P("row", None, "col"),
            P(None, "col"),
            P("col", "row"),
            P("col"),
            P("row", "col"),
            P("col"),
            P("col", "row"),
            P("col"),
            P(None, "col"),
            P(None, "col"),
        ),
        check_vma=False,
    )
```
